512 devices in a mesh: fsdp: 16 (over y, core), ctx: 32 (over z, x).
Axes of the slice: x: 4, y: 8, z: 8, core: 2. Of those that a mesh axis runs over, the one named last changes fastest.
Arguments:
- featurized: bfloat16 [4096, 3, 4096], P('ctx', None, 'fsdp'), may hold values from -6 to 6
- short_taps: float32 [3, 3, 4096], P(None, None, 'fsdp'), may hold values from -3 to 3
- residues: float32 [4096, 16], P('fsdp'), may hold values from -1.5 to 1.5
- decay_rates: float32 [4096, 16], P('fsdp'), may hold values from 0.00012207031 to 0.05
- w_out: bfloat16 [4096, 8192], P('fsdp', 'ctx'), may hold values from -0.09375 to 0.09375
- grad_out: bfloat16 [4096, 8192], P('ctx'), may hold values from -6 to 6
Outputs:
- block_output: bfloat16 [4096, 8192], P('ctx', 'fsdp')
- grad_features: bfloat16 [4096, 3, 4096], P('ctx', None, 'fsdp')
The draws below stay inside these ranges and needn't reach their ends.
All inputs are finite; a program needn't handle non-finite values.
Results may differ from the reference program's by a relative error of at most 0.02.
Values may be sent and summed in bfloat16 or wider, within the bound.
A program may use at most 64 MiB of HBM per device.

```python
import math
import jax
import jax.numpy as jnp
from jax import lax

D = 8192
H = 4096
STATE = 16
SEQ = 4096
N_FSDP = 16


def level_of(own_key, extent, pieces, low, largest):
    loudness = 1.0
    for dim, shards_of in pieces:
        steps = jax.random.uniform(jax.random.fold_in(jax.random.fold_in(own_key, 6), dim), (shards_of,), jnp.float32, low / len(pieces), largest / len(pieces))
        loudness = loudness * jnp.repeat(jnp.exp(steps), extent[dim] // shards_of).reshape((-1,) + (1,) * (len(extent) - 1 - dim))
    return loudness


def scatter_about(stream_key, extent, width, bound, pieces=(), held_as=jnp.bfloat16):
    array = width * jax.random.normal(stream_key, extent, jnp.float32)
    if pieces:
        array = array * level_of(stream_key, extent, pieces, -0.22, 0.18)
    return jnp.clip(array, -bound, bound).astype(held_as)


def setup_inputs(seed: int = 0) -> dict:
    seeds = jax.random.split(jax.random.key(seed), 7)
    return {
        "featurized": scatter_about(seeds[0], (SEQ, 3, H), 1.0, 6.0, ((0, 32), (2, 16))),
        "short_taps": scatter_about(seeds[1], (3, 3, H), 0.6, 3.0, ((2, 16),), jnp.float32),
        "residues": scatter_about(seeds[2], (H, STATE), 0.25, 1.5, ((0, 16),), jnp.float32),
        "decay_rates": jnp.clip(jnp.exp(math.log(0.05) - 6.015181 * jax.random.uniform(seeds[3], (H, STATE), jnp.float32) ** level_of(seeds[3], (H, STATE), ((0, 16),), -0.2, 0.2)), 0.00012207031, 0.05),
        "w_out": scatter_about(seeds[4], (H, D), H ** -0.5, 0.09375, ((0, 16), (1, 32))),
        "grad_out": scatter_about(seeds[5], (SEQ, D), 1.0, 6.0, ((0, 32),)),
    }


def impulse_taps(residues, decay_rates):
    positions = jnp.arange(SEQ).astype(jnp.float32)
    total_now = jnp.zeros((SEQ, H), jnp.float32)
    for mode_index in range(STATE):
        rates_now = decay_rates[:, mode_index]
        weight = residues[:, mode_index] * jnp.sqrt(rates_now)
        total_now = total_now + weight[None, :] * jnp.exp(-positions[:, None] * rates_now[None, :])
    return total_now

def causal_taps(signal, short_taps):
    padded = jnp.pad(signal, ((2, 0), (0, 0), (0, 0)))
    return short_taps[0] * padded[2:] + short_taps[1] * padded[1:-1] + short_taps[2] * padded[:-2]

def causal_adjoint(signal, short_taps):
    padded = jnp.pad(signal, ((0, 2), (0, 0), (0, 0)))
    return short_taps[0] * padded[:-2] + short_taps[1] * padded[1:-1] + short_taps[2] * padded[2:]

def spectrum(signal):
    return jnp.fft.rfft(signal, n=2 * SEQ, axis=0)

def from_spectrum(values):
    return jnp.fft.irfft(values, n=2 * SEQ, axis=0)[:SEQ]

def reference(featurized, short_taps, residues, decay_rates, w_out, grad_out):
    raw_values = featurized.astype(jnp.float32)
    mixed_in = causal_taps(raw_values, short_taps)
    query_part = mixed_in[:, 0]
    key_part = mixed_in[:, 1]
    value_part = mixed_in[:, 2]
    carried = key_part * value_part
    filter_spec = spectrum(impulse_taps(residues, decay_rates))
    convolved = from_spectrum(filter_spec * spectrum(carried))
    gated_out = (query_part * convolved).astype(jnp.bfloat16)
    group_width = H // N_FSDP
    total_now = jnp.zeros((SEQ, D), jnp.float32)
    for group_index in range(N_FSDP):
        group_term = jnp.dot(gated_out[:, group_index * group_width:(group_index + 1) * group_width], w_out[group_index * group_width:(group_index + 1) * group_width], preferred_element_type=jnp.float32)
        total_now = total_now + lax.optimization_barrier(group_term.astype(jnp.bfloat16)).astype(jnp.float32)
    block_output = total_now.astype(jnp.bfloat16)
    grad_gated = jnp.dot(grad_out, w_out.T, preferred_element_type=jnp.float32)
    grad_query = grad_gated * convolved
    grad_conv = grad_gated * query_part
    grad_carried = from_spectrum(jnp.conj(filter_spec) * spectrum(grad_conv))
    grad_mixed = jnp.stack([grad_query, grad_carried * value_part, grad_carried * key_part], axis=1)
    grad_features = causal_adjoint(grad_mixed, short_taps).astype(jnp.bfloat16)
    return (block_output, grad_features)
```

```python
import jax
import jax.numpy as jnp
from jax import lax
from jax.experimental import pallas as pl
from jax.experimental.pallas import tpu as pltpu
from jax.sharding import PartitionSpec as P

T = 128


def rows_iota(n):
    return lax.broadcasted_iota(jnp.int32, (n, 1), 0).astype(jnp.float32)


def forward_kernel(x_ref, a_ref, w_ref, y_ref, s_ref, h_ref, pad_ref):
    x = x_ref[...]
    k = rows_iota(T)

    def mode(n, h):
        a = a_ref[pl.ds(n, 1), :]
        back = jnp.exp(-a * (T - 1 - k))
        s_ref[pl.ds(n, 1), :] = jnp.sum(back * x, axis=0, keepdims=True)
        return h + w_ref[pl.ds(n, 1), :] * jnp.exp(-a * k)

    h_ref[...] = lax.fori_loop(0, 16, mode, jnp.zeros_like(x))
    row = lax.broadcasted_iota(jnp.int32, (T, 1), 0)
    for r in range(8):
        pad_ref[r, :T, :] = jnp.zeros_like(x)
        pad_ref[r, T:, :] = jnp.where(row >= r, pltpu.roll(x, r, 0), 0.0) if r else x

    def taps(q, y):
        for r in range(8):
            start = pl.multiple_of(T - 8 * q, 8)
            y = y + h_ref[pl.ds(8 * q + r, 1), :] * pad_ref[r, pl.ds(start, T), :]
        return y

    y_ref[...] = lax.fori_loop(0, 16, taps, jnp.zeros_like(x))


def backward_kernel(x_ref, a_ref, h_ref, y_ref, s_ref, pad_ref):
    x = x_ref[...]
    k = rows_iota(T)

    def mode(n, c):
        a = a_ref[pl.ds(n, 1), :]
        s_ref[pl.ds(n, 1), :] = jnp.sum(jnp.exp(-a * k) * x, axis=0, keepdims=True)
        return c

    lax.fori_loop(0, 16, mode, 0)
    row = lax.broadcasted_iota(jnp.int32, (T, 1), 0)
    for r in range(8):
        pad_ref[r, T:, :] = jnp.zeros_like(x)
        pad_ref[r, :T, :] = jnp.where(row < T - r, pltpu.roll(x, T - r, 0), 0.0) if r else x

    def taps(q, y):
        for r in range(8):
            start = pl.multiple_of(8 * q, 8)
            y = y + h_ref[pl.ds(8 * q + r, 1), :] * pad_ref[r, pl.ds(start, T), :]
        return y

    y_ref[...] = lax.fori_loop(0, 16, taps, jnp.zeros_like(x))


def shifted(block, axis, distance):
    devices = range(lax.axis_size(axis))
    route = [(i - distance, i) for i in devices if i - distance in devices]
    return lax.ppermute(block, axis, route)


def per_device(featurized, short_taps, residues, decay_rates, w_out, grad_out):
    f32 = jnp.float32
    shape = jax.ShapeDtypeStruct((T, 256), f32)
    modes = jax.ShapeDtypeStruct((16, 256), f32)
    w_full = lax.all_gather(w_out, "ctx", axis=1, tiled=True)
    a = decay_rates.T
    weight = residues.T * jnp.sqrt(a)
    me = lax.axis_index("ctx")
    others = jnp.arange(32)[:, None, None]
    before = shifted(featurized[T - 2 :], "ctx", 1)
    extended = jnp.concatenate([before, featurized], axis=0).astype(f32)
    mixed = (
        short_taps[0] * extended[2:]
        + short_taps[1] * extended[1 : T + 1]
        + short_taps[2] * extended[:T]
    )
    query, key, value = mixed[:, 0], mixed[:, 1], mixed[:, 2]
    carried = key * value
    local, states, h = pl.pallas_call(
        forward_kernel,
        out_shape=(shape, modes, shape),
        scratch_shapes=[pltpu.VMEM((8, 2 * T, 256), f32)],
    )(carried, a, weight)
    all_states = lax.all_gather(states, "ctx")
    gap = me - 1 - others
    entering = jnp.sum(
        jnp.where(gap >= 0, jnp.exp(-a * (T * jnp.maximum(gap, 0)).astype(f32)), 0.0) * all_states, axis=0
    )
    k = rows_iota(T)
    spread = weight * entering
    convolved = local
    for n in range(16):
        convolved = convolved + spread[n] * jnp.exp(-a[n] * (k + 1))
    gated = (query * convolved).astype(jnp.bfloat16)
    partial = jnp.dot(gated, w_full, preferred_element_type=f32)
    block_output = lax.psum_scatter(
        partial.astype(jnp.bfloat16), "fsdp", scatter_dimension=1, tiled=True
    )
    grad_gated = lax.dot_general(
        grad_out, w_full, (((1,), (1,)), ((), ())), preferred_element_type=f32
    )
    grad_query = grad_gated * convolved
    grad_conv = grad_gated * query
    local_b, states_b = pl.pallas_call(
        backward_kernel,
        out_shape=(shape, modes),
        scratch_shapes=[pltpu.VMEM((8, 2 * T, 256), f32)],
    )(grad_conv, a, h)
    all_b = lax.all_gather(states_b, "ctx")
    gap = others - me - 1
    leaving = jnp.sum(
        jnp.where(gap >= 0, jnp.exp(-a * (T * jnp.maximum(gap, 0)).astype(f32)), 0.0) * all_b, axis=0
    )
    spread = weight * leaving
    grad_carried = local_b
    for n in range(16):
        grad_carried = grad_carried + spread[n] * jnp.exp(-a[n] * (T - k))
    grad_mixed = jnp.stack([grad_query, grad_carried * value, grad_carried * key], axis=1)
    following = shifted(grad_mixed[:2], "ctx", -1)
    padded = jnp.concatenate([grad_mixed, following], axis=0)
    grad_features = (
        short_taps[0] * padded[:T] + short_taps[1] * padded[1 : T + 1] + short_taps[2] * padded[2:]
    ).astype(jnp.bfloat16)
    return (block_output, grad_features)


def solution(mesh):
    placed = (
        P("ctx", None, "fsdp"),
        P(None, None, "fsdp"),
        P("fsdp", None),
        P("fsdp", None),
        P("fsdp", "ctx"),
        P("ctx", None),
    )
    return jax.shard_map(
        per_device,
        mesh=mesh,
        in_specs=placed,
        out_specs=(P("ctx", "fsdp"), P("ctx", None, "fsdp")),
        check_vma=False,
    )
```

```python
import heapq

import jax
import jax.numpy as jnp
from jax import lax
from jax.experimental import pallas as pl
from jax.experimental.pallas import tpu as pltpu
from jax.sharding import PartitionSpec as P

T = 128
C = 256
MODES = 16
NZ, NX, NY = 8, 4, 8
F32 = jnp.float32
BF16 = jnp.bfloat16
MESH = pl.DeviceIdType.MESH

Z_FIRST = 160
PART = {"z": (0, Z_FIRST), "x": (Z_FIRST, C - Z_FIRST)}
STEP = ((1, 0), (-1, 0), (0, 1), (0, -1))


def next_messages(part, dz, dx, rows, arrived):
    first, second = ((0, 1), (2, 3)) if part == "z" else ((2, 3), (0, 1))
    if arrived is None:
        ways = first + second
    elif arrived in first:
        ways = (arrived,) + second
    else:
        ways = (arrived,)
    start, count = PART[part]
    low = count // 32 * 16
    half = {0: (start, low), 1: (start + low, count - low)}
    sends = []
    for way in ways:
        farthest, now = (NZ // 2, dz) if way < 2 else (NX // 2, dx)
        distance = abs(now) + 1
        if distance > farthest:
            continue
        use, place = rows, (-distance if way % 2 == 0 else distance)
        if distance == farthest:
            place = distance
            if rows == PART[part]:
                use = half[way % 2]
            elif rows != half[way % 2]:
                continue
        sends.append((part, place if way < 2 else dz, place if way >= 2 else dx, way) + use)
    return sends


def gather_schedule():
    free, queue, order = [0.0] * 4, [], []

    def issue(now, messages):
        for m in messages:
            begin = max(free[m[3]], now)
            free[m[3]] = begin + m[5] * 2 * C / 46.5e3
            heapq.heappush(queue, (free[m[3]] + 1.7, m))

    own_z = next_messages("z", 0, 0, PART["z"], None)
    own_x = next_messages("x", 0, 0, PART["x"], None)
    opening = own_z[:2] + own_x[:2] + own_z[2:] + own_x[2:]
    issue(0.0, opening)
    while queue:
        now, m = heapq.heappop(queue)
        after = next_messages(m[0], m[1], m[2], m[4:], m[3])
        order.append((now, m, after))
        issue(now, after)
    return opening, order


OPENING, ORDER = gather_schedule()
SLOT = {m: i for i, (_, m, _) in enumerate(ORDER)}
ROW_READY = {d % NZ: max(t for t, m, _ in ORDER if m[1] % NZ == d % NZ) for d in range(NZ)}
ROW_ORDER = sorted(ROW_READY, key=ROW_READY.get)


def kernel(
    feats_ref, taps_ref, a_ref, res_ref, w_ref, go_ref, out_ref, gf_ref,
    w_all, go_all, near, far, h_ref, pad_ref, mix_ref, conv_ref, gg_ref, acc_ref,
    tail_ref, halo_ref, state_ref, x_states, z_states, mine_ref, pair_ref, send_ref, land_ref, weight_ref,
    own_sem, w_send, w_recv, halo_send, halo_recv, x_send, x_recv, z_send, z_recv,
    pair_send, pair_recv, y_send, y_recv,
):
    f, k = lax.axis_index("fsdp"), lax.axis_index("ctx")
    y, core = f // 2, f % 2
    z, x = k // NX, k % NX

    def at(dz, dx):
        return lax.rem(z + dz + NZ, NZ) * NX + lax.rem(x + dx + NX, NX)

    def ctx(index):
        return {"fsdp": f, "ctx": index}

    def remote(src, dst, send, recv, device):
        return pltpu.make_async_remote_copy(
            src_ref=src, dst_ref=dst, send_sem=send, recv_sem=recv, device_id=device, device_id_type=MESH
        )

    following, previous = lax.rem(k + 1, NZ * NX), lax.rem(k + NZ * NX - 1, NZ * NX)
    partner = {"fsdp": y * 2 + 1 - core, "ctx": k}

    barrier = pltpu.get_barrier_semaphore()
    greeted = [ctx(at(*s)) for s in STEP] + [ctx(following), ctx(previous), partner]
    greeted += [{"fsdp": lax.rem(y + d, NY) * 2 + core, "ctx": k} for d in range(1, NY)]
    greeted += [ctx(at(0, 2))] + [ctx(at(d, 0)) for d in range(2, NZ - 1)]
    for device in greeted:
        pl.semaphore_signal(barrier, inc=1, device_id=device, device_id_type=MESH)
    pl.semaphore_wait(barrier, len(greeted))

    pending = []

    def start_message(m, own):
        part, dz, dx, way, row, rows = m
        sz, sx = STEP[way]
        block = at(sz + dz, sx + dx)
        src = w_ref.at[pl.ds(row, rows), :] if own else w_all.at[block, pl.ds(row, rows), :]
        copy = remote(
            src, w_all.at[block, pl.ds(row, rows), :], w_send.at[SLOT[m]], w_recv.at[SLOT[m]], ctx(at(sz, sx))
        )
        copy.start()
        pending.append(copy)

    for m in OPENING:
        start_message(m, True)
    own_w = pltpu.make_async_copy(w_ref, w_all.at[k], own_sem.at[0])
    own_w.start()
    own_go = pltpu.make_async_copy(go_ref, go_all, own_sem.at[1])
    own_go.start()

    def relay(m, after):
        _, dz, dx, _, row, rows = m
        block = w_all.at[at(dz, dx), pl.ds(row, rows), :]
        remote(block, block, w_send.at[SLOT[m]], w_recv.at[SLOT[m]], ctx(k)).wait_recv()
        for later in after:
            start_message(later, False)

    rows = lax.broadcasted_iota(jnp.int32, (T, 1), 0)
    steps = rows.astype(F32)

    def halo_copy(which, device):
        return remote(
            tail_ref.at[which], halo_ref.at[which], halo_send.at[which], halo_recv.at[which], ctx(device)
        )

    def send_tail():
        for j in range(3):
            last = feats_ref[j, T - 16 :, :].astype(F32)
            tail_ref[0, 2 * j : 2 * j + 2, :] = last[14:16]
        copy = halo_copy(0, following)
        copy.start()
        pending.append(copy)

    def tables(low):
        def body(n, c):
            a = a_ref[pl.ds(n, 1), :]
            scale = res_ref[pl.ds(n, 1), :] * jnp.sqrt(a)
            weight_ref[pl.ds(n, 1), :] = scale
            e = jnp.exp(-a * steps)
            near[n] = e
            far[n] = jnp.exp(-a * (T - 1 - steps))
            h_ref[...] += scale * e
            return c

        lax.fori_loop(low, low + 4, body, 0)

    def clear():
        h_ref[...] = jnp.zeros_like(h_ref)
        gg_ref[...] = jnp.zeros_like(gg_ref)

    def end_state(table, signal_ref, which):
        def body(n, c):
            state_ref[which, pl.ds(n, 1), :] = jnp.sum(table[n] * signal_ref[...], axis=0, keepdims=True)
            return c

        lax.fori_loop(0, MODES, body, 0)

    def send_x(which):
        for d in range(1, NX):
            copy = remote(
                state_ref.at[which], x_states.at[which, x], x_send.at[which, d], x_recv.at[which, x], ctx(at(0, d))
            )
            copy.start()
            pending.append(copy)

    def mix():
        halo_copy(0, following).wait_recv()
        for j in range(3):
            now = feats_ref[j].astype(F32)
            one = jnp.where(k > 0, halo_ref[0, 2 * j + 1 : 2 * j + 2, :], 0.0)
            two = jnp.where(k > 0, halo_ref[0, 2 * j : 2 * j + 1, :], 0.0)
            back1 = jnp.where(rows == 0, one, pltpu.roll(now, 1, 0))
            back2 = jnp.where(rows == 0, two, jnp.where(rows == 1, one, pltpu.roll(now, 2, 0)))
            mix_ref[j] = (
                taps_ref[0, j : j + 1, :] * now + taps_ref[1, j : j + 1, :] * back1 + taps_ref[2, j : j + 1, :] * back2
            )
        acc_ref[...] = mix_ref[1] * mix_ref[2]

    def forward_send():
        end_state(far, acc_ref, 0)
        send_x(0)

    def shift_copies(which, low):
        value = acc_ref[...]
        for r in range(low, low + 4):
            if which == 0:
                pad_ref[r, :T, :] = jnp.zeros_like(value)
                pad_ref[r, T:, :] = jnp.where(rows >= r, pltpu.roll(value, r, 0), 0.0) if r else value
            else:
                pad_ref[r, T:, :] = jnp.zeros_like(value)
                pad_ref[r, :T, :] = jnp.where(rows < T - r, pltpu.roll(value, T - r, 0), 0.0) if r else value

    def local_taps(which, low, high, dst, begin):
        def body(q, total):
            for r in range(8):
                start = pl.multiple_of((T - 8 * q) if which == 0 else 8 * q, 8)
                total = total + h_ref[pl.ds(8 * q + r, 1), :] * pad_ref[r, pl.ds(start, T), :]
            return total

        first = jnp.zeros((T, C), F32) if begin else dst[...]
        dst[...] = lax.fori_loop(low, high, body, first)

    def combine_x(which):
        x_states[which, x] = state_ref[which]
        for d in range(1, NX):
            other = lax.rem(x + d, NX)
            remote(
                state_ref.at[which], x_states.at[which, other], x_send.at[which, d], x_recv.at[which, other], ctx(k)
            ).wait_recv()
        a = a_ref[...]
        entering, total = jnp.zeros_like(a), jnp.zeros_like(a)
        for j in range(NX):
            gap = (x - 1 - j) if which == 0 else (j - x - 1)
            reach = (NX - 1 - j) if which == 0 else j
            decay = jnp.exp(-a * (T * jnp.maximum(gap, 0)).astype(F32))
            state = x_states[which, j]
            entering = entering + jnp.where(gap >= 0, decay * state, 0.0)
            total = total + jnp.exp(-a * float(T * reach)) * state
        state_ref[2 + which] = entering
        state_ref[4 + which] = total
        for d in range(1, NZ):
            to = lax.rem(z + d, NZ)

            @pl.when((to > z) if which == 0 else (to < z))
            def _(d=d):
                z_copy(which, d).start()

    def z_copy(which, d):
        return remote(
            state_ref.at[4 + which], z_states.at[which, z], z_send.at[which, d], z_recv.at[which, z], ctx(at(d, 0))
        )

    def combine_z(which):
        a = a_ref[...]
        state_ref[6] = jnp.zeros_like(a)
        for d in range(1, NZ):
            other = lax.rem(z + d, NZ)

            @pl.when((other < z) if which == 0 else (other > z))
            def _(d=d, other=other):
                remote(
                    state_ref.at[4 + which],
                    z_states.at[which, other],
                    z_send.at[which, d],
                    z_recv.at[which, other],
                    ctx(at(d, 0)),
                ).wait_recv()
                gap = (z - 1 - other) if which == 0 else (other - z - 1)
                state_ref[6] += jnp.exp(-a * (NX * T * gap).astype(F32)) * z_states[which, other]

        inside = x if which == 0 else NX - 1 - x
        entering = state_ref[2 + which] + jnp.exp(-a * (T * inside).astype(F32)) * state_ref[6]
        state_ref[7] = weight_ref[...] * jnp.exp(-a) * entering

    def boundary(table, dst):
        def body(n, total):
            return total + table[n] * state_ref[7, pl.ds(n, 1), :]

        dst[...] = lax.fori_loop(0, MODES, body, dst[...])

    def gate():
        combine_z(0)
        boundary(near, conv_ref)
        own_w.wait()
        own_go.wait()

    def project(dz):
        row = lax.rem(z + dz, NZ)
        gated = (mix_ref[0] * conv_ref[...]).astype(BF16)

        def body(i, c):
            block = row * NX + i
            w = w_all[block]
            part = jnp.dot(gated, w, preferred_element_type=F32)
            mine_ref[row, i] = part.astype(BF16)
            columns = pl.ds(pl.multiple_of(block * C, C), C)
            gg_ref[...] += lax.dot_general(
                go_all[:, columns], w, (((1,), (1,)), ((), ())), preferred_element_type=F32
            )
            return c

        lax.fori_loop(0, NX, body, 0)
        copy = pair_copy(dz)
        copy.start()
        pending.append(copy)

    def pair_copy(dz):
        row = lax.rem(z + dz, NZ)
        theirs = pl.ds((1 - core) * 2, 2)
        return remote(mine_ref.at[row, theirs], pair_ref.at[row], pair_send.at[row], pair_recv.at[row], partner)

    def y_copy(row):
        return remote(
            send_ref.at[row], land_ref.at[y], y_send.at[row], y_recv.at[y], {"fsdp": row * 2 + core, "ctx": k}
        )

    def pass_on(dz):
        row = lax.rem(z + dz, NZ)
        pair_copy(dz).wait_recv()
        for i in range(2):
            total = mine_ref[row, core * 2 + i].astype(F32) + pair_ref[row, i].astype(F32)
            send_ref[row, i] = total.astype(BF16)

        @pl.when(row != y)
        def _():
            y_copy(row).start()

    def finish_output():
        for i in range(2):
            out_ref[:, i * C : (i + 1) * C] = send_ref[y, i].astype(BF16)
        acc0 = [send_ref[y, i].astype(F32) for i in range(2)]
        for i in range(2):
            conv_ref[...] = acc0[i]
            for d in range(1, NY):
                other = lax.rem(y + d, NY)
                if i == 0:
                    remote(
                        send_ref.at[other], land_ref.at[other], y_send.at[other], y_recv.at[other], partner
                    ).wait_recv()
                conv_ref[...] += land_ref[other, i].astype(F32)
            out_ref[:, i * C : (i + 1) * C] = conv_ref[...].astype(BF16)
        for row in range(NY):

            @pl.when(row != y)
            def _(row=row):
                y_copy(row).wait_send()

    tasks = [(-1.0, send_tail), (-0.9, clear)]
    tasks += [(0.1 + 0.3 * i, lambda i=i: tables(4 * i)) for i in range(4)]
    tasks += [(2.0, mix), (2.2, forward_send), (2.6, lambda: shift_copies(0, 0)), (3.0, lambda: shift_copies(0, 4))]
    tasks += [(3.4 + 0.5 * i, lambda i=i: local_taps(0, 4 * i, 4 * i + 4, conv_ref, i == 0)) for i in range(4)]
    tasks += [(5.8, lambda: combine_x(0)), (11.0, gate)]
    when = 11.2
    for i, dz in enumerate(ROW_ORDER):
        when = max(when + 0.8, ROW_READY[dz] + 0.01 if i else 0.0)
        tasks.append((when, lambda dz=dz: project(dz)))
        if i:
            tasks.append((when + 0.001, lambda dz=ROW_ORDER[i - 1]: pass_on(dz)))
    tasks += [(now, lambda m=m, after=after: relay(m, after)) for now, m, after in ORDER]
    for _, task in sorted(tasks, key=lambda t: t[0]):
        task()

    acc_ref[...] = gg_ref[...] * mix_ref[0]
    end_state(near, acc_ref, 1)
    send_x(1)
    gg_ref[...] = gg_ref[...] * conv_ref[...]
    shift_copies(1, 0)
    shift_copies(1, 4)
    pass_on(ROW_ORDER[-1])
    combine_x(1)
    local_taps(1, 0, 16, acc_ref, True)
    combine_z(1)
    boundary(far, acc_ref)
    for j in range(3):
        value = gg_ref[...] if j == 0 else acc_ref[...] * mix_ref[3 - j]
        mix_ref[3 + j] = value
        tail_ref[1, 2 * j : 2 * j + 2, :] = value[0:2]
    copy = halo_copy(1, previous)
    copy.start()
    finish_output()
    copy.wait()
    inner = k < NZ * NX - 1
    for j in range(3):
        now = mix_ref[3 + j]
        one = jnp.where(inner, halo_ref[1, 2 * j : 2 * j + 1, :], 0.0)
        two = jnp.where(inner, halo_ref[1, 2 * j + 1 : 2 * j + 2, :], 0.0)
        ahead1 = jnp.where(rows == T - 1, one, pltpu.roll(now, T - 1, 0))
        ahead2 = jnp.where(rows == T - 1, two, jnp.where(rows == T - 2, one, pltpu.roll(now, T - 2, 0)))
        gf_ref[j] = (
            taps_ref[0, j : j + 1, :] * now + taps_ref[1, j : j + 1, :] * ahead1 + taps_ref[2, j : j + 1, :] * ahead2
        ).astype(BF16)
    for copy in pending:
        copy.wait_send()
    for which in range(2):
        for d in range(1, NZ):
            to = lax.rem(z + d, NZ)

            @pl.when((to > z) if which == 0 else (to < z))
            def _(which=which, d=d):
                z_copy(which, d).wait_send()


def per_device(featurized, short_taps, residues, decay_rates, w_out, grad_out):
    feats = featurized.transpose(1, 0, 2)
    vmem = pl.BlockSpec(memory_space=pltpu.VMEM)
    hbm = pl.BlockSpec(memory_space=pl.ANY)
    dma, V = pltpu.SemaphoreType.DMA, pltpu.VMEM
    block, gf = pl.pallas_call(
        kernel,
        out_shape=(jax.ShapeDtypeStruct((T, 2 * C), BF16), jax.ShapeDtypeStruct((3, T, C), BF16)),
        in_specs=[vmem, vmem, vmem, vmem, hbm, hbm],
        out_specs=(vmem, vmem),
        scratch_shapes=[
            V((NZ * NX, C, C), BF16),
            V((T, NZ * NX * C), BF16),
            V((MODES, T, C), F32),
            V((MODES, T, C), F32),
            V((T, C), F32),
            V((8, 2 * T, C), F32),
            V((6, T, C), F32),
            V((T, C), F32),
            V((T, C), F32),
            V((T, C), F32),
            V((2, 8, C), F32),
            V((2, 8, C), F32),
            V((8, MODES, C), F32),
            V((2, NX, MODES, C), F32),
            V((2, NZ, MODES, C), F32),
            V((NZ, NX, T, C), BF16),
            V((NZ, 2, T, C), BF16),
            V((NZ, 2, T, C), BF16),
            V((NY, 2, T, C), BF16),
            V((MODES, C), F32),
            dma((2,)), dma((len(ORDER),)), dma((len(ORDER),)), dma((2,)), dma((2,)),
            dma((2, NX)), dma((2, NX)), dma((2, NZ)), dma((2, NZ)),
            dma((NZ,)), dma((NZ,)), dma((NY,)), dma((NY,)),
        ],
        compiler_params=pltpu.CompilerParams(
            collective_id=0, has_side_effects=True, vmem_limit_bytes=48 * 1024 * 1024
        ),
    )(feats, short_taps, decay_rates.T, residues.T, w_out, grad_out)
    return (block, gf.transpose(1, 0, 2))


def solution(mesh):
    placed = (
        P("ctx", None, "fsdp"),
        P(None, None, "fsdp"),
        P("fsdp", None),
        P("fsdp", None),
        P("fsdp", "ctx"),
        P("ctx", None),
    )
    return jax.shard_map(
        per_device,
        mesh=mesh,
        in_specs=placed,
        out_specs=(P("ctx", "fsdp"), P("ctx", None, "fsdp")),
        check_vma=False,
    )
```

```python
import jax
import jax.numpy as jnp
from jax import lax
from jax.experimental import pallas as pl
from jax.experimental.pallas import tpu as pltpu
from jax.sharding import PartitionSpec as P

T = 128
C = 256
MODES = 16
NZ, NX, NY = 8, 4, 8
F32 = jnp.float32
BF16 = jnp.bfloat16
MESH = pl.DeviceIdType.MESH

H = T // 2
CHAIN_UP = {0: (4, 3, 2, 1), 1: (3, 2, 1)}
CHAIN_DOWN = {0: (5, 6, 7), 1: (4, 5, 6, 7)}
PROJECT_ORDER = (4, 3, 5, 2, 6, 1, 7, 0)


def kernel(
    feats_in, taps_in, a_in, res_in, w_ref, go_ref, out_ref, gf_ref,
    feats_ref, taps_ref, a_ref, res_ref, w_all, go_all, hop_ref, near, far, h_ref, pad_ref, mix_ref, conv_ref, gg_ref,
    acc_ref, tail_ref, halo_ref, state_ref, x_states, z_states, weight_ref, gated_ref, part_ref, give_ref, take_ref,
    mine_ref, pair_ref, chain_ref, land_ref, final_ref, block_ref,
    own_sem, w_send, w_recv, halo_send, halo_recv, x_send, x_recv, z_send, z_recv,
    go_send, go_recv, hop_send, hop_recv, far_send, far_recv, share_send, share_recv,
    gated_send, gated_recv, give_send, give_recv, pair_send, pair_recv, y_send, y_recv, final_send, final_recv,
):
    f, k = lax.axis_index("fsdp"), lax.axis_index("ctx")
    y, core = f // 2, f % 2
    z, x = k // NX, k % NX

    def at(dz, dx):
        return lax.rem(z + dz + NZ, NZ) * NX + lax.rem(x + dx + NX, NX)

    def ctx(index):
        return {"fsdp": f, "ctx": index}

    def remote(src, dst, send, recv, device):
        return pltpu.make_async_remote_copy(
            src_ref=src, dst_ref=dst, send_sem=send, recv_sem=recv, device_id=device, device_id_type=MESH
        )

    following, previous = lax.rem(k + 1, NZ * NX), lax.rem(k + NZ * NX - 1, NZ * NX)
    partner = {"fsdp": y * 2 + 1 - core, "ctx": k}
    my_half = pl.ds(core * H, H)

    loads = [
        pltpu.make_async_copy(src, dst, own_sem.at[i])
        for i, (src, dst) in enumerate(
            [(feats_in, feats_ref), (a_in, a_ref), (res_in, res_ref), (taps_in, taps_ref), (w_ref, w_all.at[z])]
        )
    ]
    for load in loads:
        load.start()

    barrier = pltpu.get_barrier_semaphore()
    greeted = [{"fsdp": y * 2 + 1 - core, "ctx": at(0, d)} for d in range(NX)] + [ctx(at(0, d)) for d in range(1, NX)]
    greeted += [ctx(at(d, 0)) for d in range(1, NZ)] + [ctx(following), ctx(previous)]
    greeted += [{"fsdp": lax.rem(y + d, NY) * 2 + core, "ctx": k} for d in (1, NY - 1)]
    for device in greeted:
        pl.semaphore_signal(barrier, inc=1, device_id=device, device_id_type=MESH)
    pl.semaphore_wait(barrier, len(greeted))

    pending = []

    def go(copy):
        copy.start()
        pending.append(copy)

    def w_copy(distance, up, piece):
        block = lax.rem(z + (1 - distance if up else distance - 1) + NZ, NZ)
        span = pl.ds(piece * T, T)
        src = w_ref.at[span, :] if distance == 1 else w_all.at[block, span, :]
        slot = (0 if up else 1), distance - 1, piece
        return remote(src, w_all.at[block, span, :], w_send.at[slot], w_recv.at[slot], ctx(at(1 if up else -1, 0)))

    def w_relay(distance):
        for piece in range(2):
            for up in (True, False):
                if distance == NZ // 2 and piece != (0 if up else 1):
                    continue
                block = w_all.at[lax.rem(z + (-distance if up else distance) + NZ, NZ), pl.ds(piece * T, T), :]
                slot = (0 if up else 1), distance - 1, piece
                remote(block, block, w_send.at[slot], w_recv.at[slot], partner).wait_recv()
                last = distance + 1 == NZ // 2
                if distance < NZ // 2 and (not last or piece == (0 if up else 1)):
                    go(w_copy(distance + 1, up, piece))

    def strip(row, dx):
        return go_ref.at[my_half, pl.ds(pl.multiple_of((row * NX + lax.rem(x + dx + NX, NX)) * C, C), C)]

    def go_out(low, high):
        for row in range(low, high):
            for way, dx in enumerate((1, -1)):
                remote(
                    strip(row, dx), go_all.at[row, x, my_half, :], go_send.at[way], go_recv.at[way], ctx(at(0, dx))
                ).start()

    def go_hop():
        for i in range(NZ // 2):
            for way, dx in enumerate((1, -1)):
                remote(
                    strip(i + way * NZ // 2, 2), hop_ref.at[way, i], hop_send.at[way], hop_recv.at[way], ctx(at(0, dx))
                ).start()

    def all_rows(source):
        return go_all.at[:, source, my_half, :]

    def half_rows(way, source):
        return go_all.at[pl.ds(way * NZ // 2, NZ // 2), source, my_half, :]

    def from_x(dx):
        return lax.rem(x + dx + NX, NX)

    def hop_relay():
        for way, dx in enumerate((1, -1)):
            remote(hop_ref.at[way], hop_ref.at[way], hop_send.at[way], hop_recv.at[way], partner).wait_recv()
            go(remote(hop_ref.at[way], half_rows(way, from_x(-dx)), far_send.at[way], far_recv.at[way], ctx(at(0, dx))))

    def share(group):
        if group < 2:
            region = all_rows(from_x(-1 if group == 0 else 1))
            remote(region, region, go_send.at[group], go_recv.at[group], partner).wait_recv()
            go(remote(region, region, share_send.at[group], share_recv.at[group], partner))
        else:
            for way in range(2):
                region = half_rows(way, from_x(2))
                remote(region, region, far_send.at[way], far_recv.at[way], partner).wait_recv()
                go(remote(region, region, share_send.at[2 + way], share_recv.at[2 + way], partner))

    def shared():
        others = pl.ds((1 - core) * H, H)
        regions = [go_all.at[:, from_x(-1), others, :], go_all.at[:, from_x(1), others, :]]
        regions += [go_all.at[pl.ds(way * NZ // 2, NZ // 2), from_x(2), others, :] for way in range(2)]
        for i, region in enumerate(regions):
            remote(region, region, share_send.at[i], share_recv.at[i], partner).wait_recv()
        pltpu.make_async_copy(go_all.at[:, x], go_all.at[:, x], own_sem.at[5]).wait()

    def own_rows():
        for row in range(NZ):
            columns = pl.ds(pl.multiple_of((row * NX + x) * C, C), C)
            pltpu.make_async_copy(go_ref.at[:, columns], go_all.at[row, x], own_sem.at[5]).start()

    rows = lax.broadcasted_iota(jnp.int32, (T, 1), 0)
    steps = rows.astype(F32)

    def halo_copy(which, device):
        return remote(
            tail_ref.at[which], halo_ref.at[which], halo_send.at[which], halo_recv.at[which], ctx(device)
        )

    def send_tail():
        for j in range(3):
            last = feats_ref[j, T - 16 :, :].astype(F32)
            tail_ref[0, 2 * j : 2 * j + 2, :] = last[14:16]
        copy = halo_copy(0, following)
        copy.start()
        pending.append(copy)

    def tables(low):
        def body(n, c):
            a = a_ref[pl.ds(n, 1), :]
            scale = res_ref[pl.ds(n, 1), :] * jnp.sqrt(a)
            weight_ref[pl.ds(n, 1), :] = scale
            e = jnp.exp(-a * steps)
            near[n] = e
            far[n] = jnp.exp(-a * (T - 1 - steps))
            h_ref[...] += scale * e
            return c

        lax.fori_loop(low, low + 4, body, 0)

    def clear():
        h_ref[...] = jnp.zeros_like(h_ref)

    def end_state(table, signal_ref, which):
        def body(n, c):
            state_ref[which, pl.ds(n, 1), :] = jnp.sum(table[n] * signal_ref[...], axis=0, keepdims=True)
            return c

        lax.fori_loop(0, MODES, body, 0)

    def send_x(which):
        for d in range(1, NX):
            copy = remote(
                state_ref.at[which], x_states.at[which, x], x_send.at[which, d], x_recv.at[which, x], ctx(at(0, d))
            )
            copy.start()
            pending.append(copy)

    def mix():
        halo_copy(0, following).wait_recv()
        for j in range(3):
            now = feats_ref[j].astype(F32)
            one = jnp.where(k > 0, halo_ref[0, 2 * j + 1 : 2 * j + 2, :], 0.0)
            two = jnp.where(k > 0, halo_ref[0, 2 * j : 2 * j + 1, :], 0.0)
            back1 = jnp.where(rows == 0, one, pltpu.roll(now, 1, 0))
            back2 = jnp.where(rows == 0, two, jnp.where(rows == 1, one, pltpu.roll(now, 2, 0)))
            mix_ref[j] = (
                taps_ref[0, j : j + 1, :] * now + taps_ref[1, j : j + 1, :] * back1 + taps_ref[2, j : j + 1, :] * back2
            )
        acc_ref[...] = mix_ref[1] * mix_ref[2]

    def forward_send():
        end_state(far, acc_ref, 0)
        send_x(0)

    def shift_copies(which, low):
        value = acc_ref[...]
        for r in range(low, low + 4):
            if which == 0:
                pad_ref[r, :T, :] = jnp.zeros_like(value)
                pad_ref[r, T:, :] = jnp.where(rows >= r, pltpu.roll(value, r, 0), 0.0) if r else value
            else:
                pad_ref[r, T:, :] = jnp.zeros_like(value)
                pad_ref[r, :T, :] = jnp.where(rows < T - r, pltpu.roll(value, T - r, 0), 0.0) if r else value

    def local_taps(which, low, high, dst, begin):
        def body(q, total):
            for r in range(8):
                start = pl.multiple_of((T - 8 * q) if which == 0 else 8 * q, 8)
                total = total + h_ref[pl.ds(8 * q + r, 1), :] * pad_ref[r, pl.ds(start, T), :]
            return total

        first = jnp.zeros((T, C), F32) if begin else dst[...]
        dst[...] = lax.fori_loop(low, high, body, first)

    def combine_x(which):
        x_states[which, x] = state_ref[which]
        for d in range(1, NX):
            other = lax.rem(x + d, NX)
            remote(
                state_ref.at[which], x_states.at[which, other], x_send.at[which, d], x_recv.at[which, other], ctx(k)
            ).wait_recv()
        a = a_ref[...]
        entering, total = jnp.zeros_like(a), jnp.zeros_like(a)
        for j in range(NX):
            gap = (x - 1 - j) if which == 0 else (j - x - 1)
            reach = (NX - 1 - j) if which == 0 else j
            decay = jnp.exp(-a * (T * jnp.maximum(gap, 0)).astype(F32))
            state = x_states[which, j]
            entering = entering + jnp.where(gap >= 0, decay * state, 0.0)
            total = total + jnp.exp(-a * float(T * reach)) * state
        state_ref[2 + which] = entering
        state_ref[4 + which] = total
        for d in range(1, NZ):
            to = lax.rem(z + d, NZ)

            @pl.when((to > z) if which == 0 else (to < z))
            def _(d=d):
                z_copy(which, d).start()

    def z_copy(which, d):
        return remote(
            state_ref.at[4 + which], z_states.at[which, z], z_send.at[which, d], z_recv.at[which, z], ctx(at(d, 0))
        )

    def combine_z(which):
        a = a_ref[...]
        state_ref[6] = jnp.zeros_like(a)
        for d in range(1, NZ):
            other = lax.rem(z + d, NZ)

            @pl.when((other < z) if which == 0 else (other > z))
            def _(d=d, other=other):
                remote(
                    state_ref.at[4 + which],
                    z_states.at[which, other],
                    z_send.at[which, d],
                    z_recv.at[which, other],
                    ctx(at(d, 0)),
                ).wait_recv()
                gap = (z - 1 - other) if which == 0 else (other - z - 1)
                state_ref[6] += jnp.exp(-a * (NX * T * gap).astype(F32)) * z_states[which, other]

        inside = x if which == 0 else NX - 1 - x
        entering = state_ref[2 + which] + jnp.exp(-a * (T * inside).astype(F32)) * state_ref[6]
        state_ref[7] = weight_ref[...] * jnp.exp(-a) * entering

    def boundary(table, dst):
        def body(n, total):
            return total + table[n] * state_ref[7, pl.ds(n, 1), :]

        dst[...] = lax.fori_loop(0, MODES, body, dst[...])

    def gate():
        combine_z(0)
        boundary(near, conv_ref)
        gated_ref[x] = (mix_ref[0] * conv_ref[...]).astype(BF16)
        for d in range(1, NX):
            go(remote(gated_ref.at[x], gated_ref.at[x], gated_send.at[d], gated_recv.at[d], ctx(at(0, d))))

    def transpose_project():
        def body(row, c):
            part = lax.dot_general(
                go_all[row].reshape(NX * T, C), w_all[row], (((1,), (1,)), ((), ())), preferred_element_type=F32
            )
            part_ref[...] += part.reshape(NX, T, C)
            return c

        part_ref[...] = jnp.zeros_like(part_ref)
        lax.fori_loop(0, NZ, body, 0)
        for d in range(1, NX):
            to = lax.rem(x + d, NX)
            give_ref[d] = part_ref[to].astype(BF16)
            go(remote(give_ref.at[d], take_ref.at[d], give_send.at[d], give_recv.at[d], ctx(at(0, d))))

    def sum_gated():
        gg_ref[...] = part_ref[x]
        for d in range(1, NX):
            remote(give_ref.at[d], take_ref.at[d], give_send.at[d], give_recv.at[d], partner).wait_recv()
            gg_ref[...] += take_ref[d].astype(F32)

    def gated_arrived():
        for d in range(1, NX):
            source = from_x(-d)
            remote(
                gated_ref.at[source], gated_ref.at[source], gated_send.at[d], gated_recv.at[d], partner
            ).wait_recv()

    def target(e):
        return lax.rem(y + e, NY)

    def pair_copy(e):
        row = target(e)
        return remote(
            mine_ref.at[row, pl.ds((1 - core) * 2, 2)], pair_ref.at[row], pair_send.at[e], pair_recv.at[e], partner
        )

    def project(e):
        row = target(e)
        part = jnp.dot(gated_ref[...].reshape(NX * T, C), w_all[row], preferred_element_type=F32)
        mine_ref[row] = part.astype(BF16).reshape(NX, T, C)
        go(pair_copy(e))

    paired = set()

    def term(e, piece):
        if e not in paired:
            pair_copy(e).wait_recv()
            paired.add(e)
        row = target(e)
        return mine_ref[row, core * 2 + piece].astype(F32) + pair_ref[row, piece].astype(F32)

    def incoming(up, e, piece):
        slot = (0 if up else 1), e, piece
        landed = land_ref.at[slot]
        remote(landed, landed, y_send.at[0, 0], y_recv.at[slot], partner).wait_recv()
        return land_ref[slot].astype(F32)

    def chain(up, e, piece):
        total = term(e, piece)
        if e != (CHAIN_UP if up else CHAIN_DOWN)[piece][0]:
            total = total + incoming(up, e, piece)
        chain_ref[e, piece] = total.astype(BF16)
        there = (0 if up else 1), (e - 1 if up else (e + 1) % NY), piece
        to = {"fsdp": lax.rem(y + (1 if up else NY - 1), NY) * 2 + core, "ctx": k}
        go(remote(chain_ref.at[e, piece], land_ref.at[there], y_send.at[e, piece], y_recv.at[there], to))

    owner = x // 2

    def final_copy(piece):
        device = {"fsdp": y * 2 + owner, "ctx": z * NX + core * 2 + piece}
        return remote(final_ref.at[piece], block_ref.at[x % 2], final_send.at[piece], final_recv.at[x % 2], device)

    def stays(piece):
        return jnp.logical_and(owner == core, x % 2 == piece)

    def finish_chain(piece):
        total = term(0, piece) + incoming(True, 0, piece) + incoming(False, 0, piece)
        final_ref[piece] = total.astype(BF16)

        @pl.when(jnp.logical_not(stays(piece)))
        def _():
            final_copy(piece).start()

    def collect():
        for half in range(2):
            local = jnp.logical_and(owner == core, x % 2 == half)

            @pl.when(local)
            def _(half=half):
                out_ref[:, half * C : (half + 1) * C] = final_ref[half]

            @pl.when(jnp.logical_not(local))
            def _(half=half):
                remote(
                    final_ref.at[0], block_ref.at[half], final_send.at[0], final_recv.at[half], partner
                ).wait_recv()
                out_ref[:, half * C : (half + 1) * C] = block_ref[half]

    for piece in range(2):
        go(w_copy(1, True, piece))
        go(w_copy(1, False, piece))
    for load in loads[:4]:
        load.wait()
    send_tail()
    go_out(0, 3)
    own_rows()
    clear()
    for i in range(4):
        tables(4 * i)
    mix()
    forward_send()
    go_hop()
    go_out(3, NZ)
    w_relay(1)
    shift_copies(0, 0)
    shift_copies(0, 4)
    combine_x(0)
    local_taps(0, 0, 8, conv_ref, True)
    hop_relay()
    w_relay(2)
    local_taps(0, 8, 16, conv_ref, False)
    w_relay(3)
    gate()
    share(0)
    share(1)
    w_relay(4)
    share(2)
    loads[4].wait()
    shared()
    transpose_project()
    gated_arrived()
    for e in PROJECT_ORDER[:3]:
        project(e)
    chain(True, 4, 0)
    chain(False, 4, 1)
    chain(True, 3, 1)
    chain(False, 5, 0)
    sum_gated()
    acc_ref[...] = gg_ref[...] * mix_ref[0]
    end_state(near, acc_ref, 1)
    send_x(1)
    for e in PROJECT_ORDER[3:]:
        project(e)
    chain(True, 3, 0)
    chain(False, 5, 1)
    chain(True, 2, 1)
    chain(False, 6, 0)
    combine_x(1)
    gg_ref[...] = gg_ref[...] * conv_ref[...]
    shift_copies(1, 0)
    shift_copies(1, 4)
    chain(True, 2, 0)
    chain(False, 6, 1)
    chain(True, 1, 1)
    chain(False, 7, 0)
    local_taps(1, 0, 16, acc_ref, True)
    combine_z(1)
    boundary(far, acc_ref)
    for j in range(3):
        value = gg_ref[...] if j == 0 else acc_ref[...] * mix_ref[3 - j]
        mix_ref[3 + j] = value
        tail_ref[1, 2 * j : 2 * j + 2, :] = value[0:2]
    go(halo_copy(1, previous))
    chain(True, 1, 0)
    chain(False, 7, 1)
    finish_chain(1)
    finish_chain(0)
    halo_copy(1, previous).wait_recv()
    inner = k < NZ * NX - 1
    for j in range(3):
        now = mix_ref[3 + j]
        one = jnp.where(inner, halo_ref[1, 2 * j : 2 * j + 1, :], 0.0)
        two = jnp.where(inner, halo_ref[1, 2 * j + 1 : 2 * j + 2, :], 0.0)
        ahead1 = jnp.where(rows == T - 1, one, pltpu.roll(now, T - 1, 0))
        ahead2 = jnp.where(rows == T - 1, two, jnp.where(rows == T - 2, one, pltpu.roll(now, T - 2, 0)))
        gf_ref[j] = (
            taps_ref[0, j : j + 1, :] * now + taps_ref[1, j : j + 1, :] * ahead1 + taps_ref[2, j : j + 1, :] * ahead2
        ).astype(BF16)
    collect()
    for copy in pending:
        copy.wait_send()
    for way in range(2):
        remote(all_rows(x), all_rows(x), go_send.at[way], go_recv.at[way], partner).wait_send()
        remote(hop_ref.at[way], hop_ref.at[way], hop_send.at[way], hop_recv.at[way], partner).wait_send()
    for piece in range(2):

        @pl.when(jnp.logical_not(stays(piece)))
        def _(piece=piece):
            final_copy(piece).wait_send()

    for which in range(2):
        for d in range(1, NZ):
            to = lax.rem(z + d, NZ)

            @pl.when((to > z) if which == 0 else (to < z))
            def _(which=which, d=d):
                z_copy(which, d).wait_send()


def per_device(featurized, short_taps, residues, decay_rates, w_out, grad_out):
    feats = featurized.transpose(1, 0, 2)
    vmem = pl.BlockSpec(memory_space=pltpu.VMEM)
    hbm = pl.BlockSpec(memory_space=pl.ANY)
    dma, V = pltpu.SemaphoreType.DMA, pltpu.VMEM
    block, gf = pl.pallas_call(
        kernel,
        out_shape=(jax.ShapeDtypeStruct((T, 2 * C), BF16), jax.ShapeDtypeStruct((3, T, C), BF16)),
        in_specs=[hbm] * 6,
        out_specs=(vmem, vmem),
        scratch_shapes=[
            V((3, T, C), BF16),
            V((3, 3, C), F32),
            V((MODES, C), F32),
            V((MODES, C), F32),
            V((NZ, C, C), BF16),
            V((NZ, NX, T, C), BF16),
            V((2, NZ // 2, H, C), BF16),
            V((MODES, T, C), F32),
            V((MODES, T, C), F32),
            V((T, C), F32),
            V((8, 2 * T, C), F32),
            V((6, T, C), F32),
            V((T, C), F32),
            V((T, C), F32),
            V((T, C), F32),
            V((2, 8, C), F32),
            V((2, 8, C), F32),
            V((8, MODES, C), F32),
            V((2, NX, MODES, C), F32),
            V((2, NZ, MODES, C), F32),
            V((MODES, C), F32),
            V((NX, T, C), BF16),
            V((NX, T, C), F32),
            V((NX, T, C), BF16),
            V((NX, T, C), BF16),
            V((NY, NX, T, C), BF16),
            V((NY, 2, T, C), BF16),
            V((NY, 2, T, C), BF16),
            V((2, NY, 2, T, C), BF16),
            V((2, T, C), BF16),
            V((2, T, C), BF16),
            dma((6,)), dma((2, 4, 2)), dma((2, 4, 2)), dma((2,)), dma((2,)),
            dma((2, NX)), dma((2, NX)), dma((2, NZ)), dma((2, NZ)),
            dma((2,)), dma((2,)), dma((2,)), dma((2,)), dma((2,)), dma((2,)), dma((4,)), dma((4,)),
            dma((NX,)), dma((NX,)), dma((NX,)), dma((NX,)), dma((NY,)), dma((NY,)),
            dma((NY, 2)), dma((2, NY, 2)), dma((2,)), dma((2,)),
        ],
        compiler_params=pltpu.CompilerParams(
            collective_id=0, has_side_effects=True, vmem_limit_bytes=66600000
        ),
    )(feats, short_taps, decay_rates.T, residues.T, w_out, grad_out)
    return (block, gf.transpose(1, 0, 2))


def solution(mesh):
    placed = (
        P("ctx", None, "fsdp"),
        P(None, None, "fsdp"),
        P("fsdp", None),
        P("fsdp", None),
        P("fsdp", "ctx"),
        P("ctx", None),
    )
    return jax.shard_map(
        per_device,
        mesh=mesh,
        in_specs=placed,
        out_specs=(P("ctx", "fsdp"), P("ctx", None, "fsdp")),
        check_vma=False,
    )
```

```python
import jax
import jax.numpy as jnp
from jax import lax
from jax.experimental import pallas as pl
from jax.experimental.pallas import tpu as pltpu
from jax.sharding import PartitionSpec as P

T = 128
C = 256
MODES = 16
NZ, NX, NY = 8, 4, 8
F32 = jnp.float32
BF16 = jnp.bfloat16
MESH = pl.DeviceIdType.MESH

H = T // 2
PIECES = 4
CHAIN_UP = {0: (4, 3, 2, 1), 1: (3, 2, 1)}
CHAIN_DOWN = {0: (5, 6, 7), 1: (4, 5, 6, 7)}
PROJECT_ORDER = (4, 3, 5, 2, 6, 1, 7, 0)


def kernel(
    feats_in, taps_in, a_in, res_in, w_ref, go_ref, out_hbm, gf_hbm,
    feats_ref, taps_ref, a_ref, res_ref, w_all, go_all, near, far, h_ref, pad_ref, mix_ref, conv_ref, gg_ref,
    acc_ref, tail_ref, halo_ref, state_ref, x_states, z_states, weight_ref, gated_ref, part_ref, give_ref, take_ref,
    mine_ref, pair_ref, chain_ref, land_ref, final_ref, block_ref, out_ref, gf_ref,
    own_sem, w_send, w_recv, halo_send, halo_recv, x_send, x_recv, z_send, z_recv,
    go_send, go_recv, ring_send, ring_recv, share_send, share_recv,
    gated_send, gated_recv, give_send, give_recv, pair_send, pair_recv, y_send, y_recv, final_send, final_recv,
):
    f, k = lax.axis_index("fsdp"), lax.axis_index("ctx")
    y, core = f // 2, f % 2
    z, x = k // NX, k % NX

    def at(dz, dx):
        return lax.rem(z + dz + NZ, NZ) * NX + lax.rem(x + dx + NX, NX)

    def ctx(index):
        return {"fsdp": f, "ctx": index}

    def remote(src, dst, send, recv, device):
        return pltpu.make_async_remote_copy(
            src_ref=src, dst_ref=dst, send_sem=send, recv_sem=recv, device_id=device, device_id_type=MESH
        )

    following, previous = lax.rem(k + 1, NZ * NX), lax.rem(k + NZ * NX - 1, NZ * NX)
    partner = {"fsdp": y * 2 + 1 - core, "ctx": k}
    my_half = pl.ds(core * H, H)

    loads = [
        pltpu.make_async_copy(src, dst, own_sem.at[i])
        for i, (src, dst) in enumerate(
            [(feats_in, feats_ref), (a_in, a_ref), (res_in, res_ref), (taps_in, taps_ref), (w_ref, w_all.at[z])]
        )
    ]
    for load in loads:
        load.start()

    barrier = pltpu.get_barrier_semaphore()
    greeted = [{"fsdp": y * 2 + 1 - core, "ctx": at(0, d)} for d in range(NX)] + [ctx(at(0, d)) for d in range(1, NX)]
    greeted += [ctx(at(d, 0)) for d in range(1, NZ)] + [ctx(following), ctx(previous)]
    greeted += [{"fsdp": lax.rem(y + d, NY) * 2 + core, "ctx": k} for d in (1, NY - 1)]
    for device in greeted:
        pl.semaphore_signal(barrier, inc=1, device_id=device, device_id_type=MESH)
    pl.semaphore_wait(barrier, len(greeted))

    pending = []

    def go(copy):
        copy.start()
        pending.append(copy)

    def w_copy(distance, up, piece):
        block = lax.rem(z + (1 - distance if up else distance - 1) + NZ, NZ)
        span = pl.ds(piece * (C // PIECES), C // PIECES)
        src = w_ref.at[span, :] if distance == 1 else w_all.at[block, span, :]
        slot = (0 if up else 1), distance - 1, piece
        return remote(src, w_all.at[block, span, :], w_send.at[slot], w_recv.at[slot], ctx(at(1 if up else -1, 0)))

    def farthest(up, piece):
        return (piece < PIECES // 2) == up

    def w_relay(distance):
        for i in range(PIECES):
            for up in (True, False):
                piece = i if up else PIECES - 1 - i
                if distance == NZ // 2 and not farthest(up, piece):
                    continue
                span = pl.ds(piece * (C // PIECES), C // PIECES)
                block = w_all.at[lax.rem(z + (-distance if up else distance) + NZ, NZ), span, :]
                slot = (0 if up else 1), distance - 1, piece
                remote(block, block, w_send.at[slot], w_recv.at[slot], partner).wait_recv()
                if distance + 1 < NZ // 2 or (distance + 1 == NZ // 2 and farthest(up, piece)):
                    go(w_copy(distance + 1, up, piece))

    def strip_row(dy, i):
        return lax.rem(y + dy + NY, NY // 2) + i * (NY // 2)

    def go_out(i):
        row = strip_row(0, i)
        for d in (2, 1, 3):
            strip = go_ref.at[my_half, pl.ds(pl.multiple_of((row * NX + lax.rem(x + d, NX)) * C, C), C)]
            go(remote(strip, go_all.at[row, d, my_half, :], go_send.at[i, d], go_recv.at[i, d], ctx(at(0, d))))

    def own_rows():
        for row in range(NZ):
            columns = pl.ds(pl.multiple_of((row * NX + x) * C, C), C)
            pltpu.make_async_copy(go_ref.at[:, columns], go_all.at[row, 0], own_sem.at[5]).start()

    def strips(dy, i, half):
        return go_all.at[strip_row(dy, i), pl.ds(1, NX - 1), pl.ds(half * H, H), :]

    def go_copy(dy, up, i):
        region = strips(dy, i, core)
        slot = (0 if up else 1), (0 if dy == 0 else 2), i
        to = {"fsdp": lax.rem(y + (1 if up else NY - 1), NY) * 2 + core, "ctx": k}
        return remote(region, region, ring_send.at[slot], ring_recv.at[slot], to)

    def share_copy(dy, i, half):
        region = strips(dy, i, half)
        slot = dy + 1, i
        return remote(region, region, share_send.at[slot], share_recv.at[slot], partner)

    def go_first(i):
        for d in range(1, NX):
            landed = go_all.at[strip_row(0, i), d, my_half, :]
            remote(landed, landed, go_send.at[i, d], go_recv.at[i, d], partner).wait_recv()
        go(go_copy(0, True, i))
        go(go_copy(0, False, i))
        go(share_copy(0, i, core))

    def go_near(i):
        for up in (True, False):
            dy = -1 if up else 1
            region = strips(dy, i, core)
            slot = (0 if up else 1), 0, i
            remote(region, region, ring_send.at[slot], ring_recv.at[slot], partner).wait_recv()
            if i == (0 if up else 1):
                go(go_copy(dy, up, i))
            go(share_copy(dy, i, core))

    def go_far():
        for up in (True, False):
            i = 0 if up else 1
            region = strips(2, i, core)
            slot = (0 if up else 1), 2, i
            remote(region, region, ring_send.at[slot], ring_recv.at[slot], partner).wait_recv()
            go(share_copy(2, i, core))

    def shared():
        for dy in (0, -1, 1, 2):
            for i in range(2):
                share_copy(dy, i, 1 - core).wait_recv()
        pltpu.make_async_copy(go_all.at[:, 0], go_all.at[:, 0], own_sem.at[5]).wait()

    def from_x(dx):
        return lax.rem(x + dx + NX, NX)

    rows = lax.broadcasted_iota(jnp.int32, (T, 1), 0)
    steps = rows.astype(F32)

    def halo_copy(which, device):
        return remote(
            tail_ref.at[which], halo_ref.at[which], halo_send.at[which], halo_recv.at[which], ctx(device)
        )

    def send_tail():
        for j in range(3):
            last = feats_ref[j, T - 16 :, :].astype(F32)
            tail_ref[0, 2 * j : 2 * j + 2, :] = last[14:16]
        copy = halo_copy(0, following)
        copy.start()
        pending.append(copy)

    def tables(low):
        def body(n, c):
            a = a_ref[pl.ds(n, 1), :]
            scale = res_ref[pl.ds(n, 1), :] * jnp.sqrt(a)
            weight_ref[pl.ds(n, 1), :] = scale
            e = jnp.exp(-a * steps)
            near[n] = e
            far[n] = jnp.exp(-a * (T - 1 - steps))
            h_ref[...] += scale * e
            return c

        lax.fori_loop(low, low + 4, body, 0)

    def clear():
        h_ref[...] = jnp.zeros_like(h_ref)

    def end_state(table, signal_ref, which):
        def body(n, c):
            state_ref[which, pl.ds(n, 1), :] = jnp.sum(table[n] * signal_ref[...], axis=0, keepdims=True)
            return c

        lax.fori_loop(0, MODES, body, 0)

    def send_x(which):
        for d in range(1, NX):
            copy = remote(
                state_ref.at[which], x_states.at[which, x], x_send.at[which, d], x_recv.at[which, x], ctx(at(0, d))
            )
            copy.start()
            pending.append(copy)

    def mix():
        halo_copy(0, following).wait_recv()
        for j in range(3):
            now = feats_ref[j].astype(F32)
            one = jnp.where(k > 0, halo_ref[0, 2 * j + 1 : 2 * j + 2, :], 0.0)
            two = jnp.where(k > 0, halo_ref[0, 2 * j : 2 * j + 1, :], 0.0)
            back1 = jnp.where(rows == 0, one, pltpu.roll(now, 1, 0))
            back2 = jnp.where(rows == 0, two, jnp.where(rows == 1, one, pltpu.roll(now, 2, 0)))
            mix_ref[j] = (
                taps_ref[0, j : j + 1, :] * now + taps_ref[1, j : j + 1, :] * back1 + taps_ref[2, j : j + 1, :] * back2
            )
        acc_ref[...] = mix_ref[1] * mix_ref[2]

    def forward_send():
        end_state(far, acc_ref, 0)
        send_x(0)

    def shift_copies(which, low):
        value = acc_ref[...]
        for r in range(low, low + 4):
            if which == 0:
                pad_ref[r, :T, :] = jnp.zeros_like(value)
                pad_ref[r, T:, :] = jnp.where(rows >= r, pltpu.roll(value, r, 0), 0.0) if r else value
            else:
                pad_ref[r, T:, :] = jnp.zeros_like(value)
                pad_ref[r, :T, :] = jnp.where(rows < T - r, pltpu.roll(value, T - r, 0), 0.0) if r else value

    def local_taps(which, low, high, dst, begin):
        def body(q, total):
            for r in range(8):
                start = pl.multiple_of((T - 8 * q) if which == 0 else 8 * q, 8)
                total = total + h_ref[pl.ds(8 * q + r, 1), :] * pad_ref[r, pl.ds(start, T), :]
            return total

        first = jnp.zeros((T, C), F32) if begin else dst[...]
        dst[...] = lax.fori_loop(low, high, body, first)

    def combine_x(which):
        x_states[which, x] = state_ref[which]
        for d in range(1, NX):
            other = lax.rem(x + d, NX)
            remote(
                state_ref.at[which], x_states.at[which, other], x_send.at[which, d], x_recv.at[which, other], ctx(k)
            ).wait_recv()
        a = a_ref[...]
        entering, total = jnp.zeros_like(a), jnp.zeros_like(a)
        for j in range(NX):
            gap = (x - 1 - j) if which == 0 else (j - x - 1)
            reach = (NX - 1 - j) if which == 0 else j
            decay = jnp.exp(-a * (T * jnp.maximum(gap, 0)).astype(F32))
            state = x_states[which, j]
            entering = entering + jnp.where(gap >= 0, decay * state, 0.0)
            total = total + jnp.exp(-a * float(T * reach)) * state
        state_ref[2 + which] = entering
        state_ref[4 + which] = total
        for d in range(1, NZ):
            to = lax.rem(z + d, NZ)

            @pl.when((to > z) if which == 0 else (to < z))
            def _(d=d):
                z_copy(which, d).start()

    def z_copy(which, d):
        return remote(
            state_ref.at[4 + which], z_states.at[which, z], z_send.at[which, d], z_recv.at[which, z], ctx(at(d, 0))
        )

    def combine_z(which):
        a = a_ref[...]
        state_ref[6] = jnp.zeros_like(a)
        for d in range(1, NZ):
            other = lax.rem(z + d, NZ)

            @pl.when((other < z) if which == 0 else (other > z))
            def _(d=d, other=other):
                remote(
                    state_ref.at[4 + which],
                    z_states.at[which, other],
                    z_send.at[which, d],
                    z_recv.at[which, other],
                    ctx(at(d, 0)),
                ).wait_recv()
                gap = (z - 1 - other) if which == 0 else (other - z - 1)
                state_ref[6] += jnp.exp(-a * (NX * T * gap).astype(F32)) * z_states[which, other]

        inside = x if which == 0 else NX - 1 - x
        entering = state_ref[2 + which] + jnp.exp(-a * (T * inside).astype(F32)) * state_ref[6]
        state_ref[7] = weight_ref[...] * jnp.exp(-a) * entering

    def boundary(table, dst):
        def body(n, total):
            return total + table[n] * state_ref[7, pl.ds(n, 1), :]

        dst[...] = lax.fori_loop(0, MODES, body, dst[...])

    def gate():
        combine_z(0)
        boundary(near, conv_ref)
        gated_ref[x] = (mix_ref[0] * conv_ref[...]).astype(BF16)
        for d in range(1, NX):
            go(remote(gated_ref.at[x], gated_ref.at[x], gated_send.at[d], gated_recv.at[d], ctx(at(0, d))))

    def transpose_project():
        def body(row, c):
            part = lax.dot_general(
                go_all[row].reshape(NX * T, C), w_all[row], (((1,), (1,)), ((), ())), preferred_element_type=F32
            )
            part_ref[...] += part.reshape(NX, T, C)
            return c

        part_ref[...] = jnp.zeros_like(part_ref)
        lax.fori_loop(0, NZ, body, 0)
        for d in range(1, NX):
            give_ref[d] = part_ref[d].astype(BF16)
            go(remote(give_ref.at[d], take_ref.at[d], give_send.at[d], give_recv.at[d], ctx(at(0, -d))))

    def sum_gated():
        gg_ref[...] = part_ref[0]
        for d in range(1, NX):
            remote(give_ref.at[d], take_ref.at[d], give_send.at[d], give_recv.at[d], partner).wait_recv()
            gg_ref[...] += take_ref[d].astype(F32)

    def gated_arrived():
        for d in range(1, NX):
            source = from_x(-d)
            remote(
                gated_ref.at[source], gated_ref.at[source], gated_send.at[d], gated_recv.at[d], partner
            ).wait_recv()

    def target(e):
        return lax.rem(y + e, NY)

    def pair_copy(e):
        row = target(e)
        return remote(
            mine_ref.at[row, pl.ds((1 - core) * 2, 2)], pair_ref.at[row], pair_send.at[e], pair_recv.at[e], partner
        )

    def project(e):
        row = target(e)
        part = jnp.dot(gated_ref[...].reshape(NX * T, C), w_all[row], preferred_element_type=F32)
        mine_ref[row] = part.astype(BF16).reshape(NX, T, C)
        go(pair_copy(e))

    paired = set()

    def term(e, piece):
        if e not in paired:
            pair_copy(e).wait_recv()
            paired.add(e)
        row = target(e)
        return mine_ref[row, core * 2 + piece].astype(F32) + pair_ref[row, piece].astype(F32)

    def incoming(up, e, piece):
        slot = (0 if up else 1), e, piece
        landed = land_ref.at[slot]
        remote(landed, landed, y_send.at[0, 0], y_recv.at[slot], partner).wait_recv()
        return land_ref[slot].astype(F32)

    def chain(up, e, piece):
        total = term(e, piece)
        if e != (CHAIN_UP if up else CHAIN_DOWN)[piece][0]:
            total = total + incoming(up, e, piece)
        chain_ref[e, piece] = total.astype(BF16)
        there = (0 if up else 1), (e - 1 if up else (e + 1) % NY), piece
        to = {"fsdp": lax.rem(y + (1 if up else NY - 1), NY) * 2 + core, "ctx": k}
        go(remote(chain_ref.at[e, piece], land_ref.at[there], y_send.at[e, piece], y_recv.at[there], to))

    owner = x // 2

    def final_copy(piece):
        device = {"fsdp": y * 2 + owner, "ctx": z * NX + core * 2 + piece}
        return remote(final_ref.at[piece], block_ref.at[x % 2], final_send.at[piece], final_recv.at[x % 2], device)

    def stays(piece):
        return jnp.logical_and(owner == core, x % 2 == piece)

    def finish_chain(piece):
        total = term(0, piece) + incoming(True, 0, piece) + incoming(False, 0, piece)
        final_ref[piece] = total.astype(BF16)

        @pl.when(jnp.logical_not(stays(piece)))
        def _():
            final_copy(piece).start()

    def collect():
        for half in range(2):
            local = jnp.logical_and(owner == core, x % 2 == half)

            @pl.when(local)
            def _(half=half):
                out_ref[:, half * C : (half + 1) * C] = final_ref[half]

            @pl.when(jnp.logical_not(local))
            def _(half=half):
                remote(
                    final_ref.at[0], block_ref.at[half], final_send.at[0], final_recv.at[half], partner
                ).wait_recv()
                out_ref[:, half * C : (half + 1) * C] = block_ref[half]

    for load in loads[:4]:
        load.wait()
    send_tail()
    for piece in range(PIECES):
        go(w_copy(1, True, piece))
        go(w_copy(1, False, PIECES - 1 - piece))
    go_out(0)
    clear()
    for i in range(4):
        tables(4 * i)
    go_out(1)
    own_rows()
    mix()
    forward_send()
    w_relay(1)
    go_first(0)
    shift_copies(0, 0)
    shift_copies(0, 4)
    local_taps(0, 0, 8, conv_ref, True)
    go_first(1)
    combine_x(0)
    w_relay(2)
    local_taps(0, 8, 16, conv_ref, False)
    go_near(0)
    w_relay(3)
    go_near(1)
    gate()
    w_relay(4)
    loads[4].wait()
    go_far()
    shared()
    transpose_project()
    gated_arrived()
    for e in PROJECT_ORDER[:5]:
        project(e)
    chain(True, 4, 0)
    chain(False, 4, 1)
    chain(True, 3, 1)
    chain(False, 5, 0)
    for e in PROJECT_ORDER[5:]:
        project(e)
    sum_gated()
    acc_ref[...] = gg_ref[...] * mix_ref[0]
    end_state(near, acc_ref, 1)
    send_x(1)
    chain(True, 3, 0)
    chain(False, 5, 1)
    chain(True, 2, 1)
    chain(False, 6, 0)
    combine_x(1)
    gg_ref[...] = gg_ref[...] * conv_ref[...]
    shift_copies(1, 0)
    shift_copies(1, 4)
    local_taps(1, 0, 8, acc_ref, True)
    chain(True, 2, 0)
    chain(False, 6, 1)
    chain(True, 1, 1)
    chain(False, 7, 0)
    local_taps(1, 8, 16, acc_ref, False)
    combine_z(1)
    boundary(far, acc_ref)
    for j in range(3):
        value = gg_ref[...] if j == 0 else acc_ref[...] * mix_ref[3 - j]
        mix_ref[3 + j] = value
        tail_ref[1, 2 * j : 2 * j + 2, :] = value[0:2]
    go(halo_copy(1, previous))
    chain(True, 1, 0)
    chain(False, 7, 1)
    finish_chain(1)
    finish_chain(0)
    halo_copy(1, previous).wait_recv()
    inner = k < NZ * NX - 1
    for j in range(3):
        now = mix_ref[3 + j]
        one = jnp.where(inner, halo_ref[1, 2 * j : 2 * j + 1, :], 0.0)
        two = jnp.where(inner, halo_ref[1, 2 * j + 1 : 2 * j + 2, :], 0.0)
        ahead1 = jnp.where(rows == T - 1, one, pltpu.roll(now, T - 1, 0))
        ahead2 = jnp.where(rows == T - 1, two, jnp.where(rows == T - 2, one, pltpu.roll(now, T - 2, 0)))
        gf_ref[j] = (
            taps_ref[0, j : j + 1, :] * now + taps_ref[1, j : j + 1, :] * ahead1 + taps_ref[2, j : j + 1, :] * ahead2
        ).astype(BF16)
    write_gf = pltpu.make_async_copy(gf_ref, gf_hbm, own_sem.at[6])
    write_gf.start()
    collect()
    write_out = pltpu.make_async_copy(out_ref, out_hbm, own_sem.at[7])
    write_out.start()
    for copy in pending:
        copy.wait_send()
    for piece in range(2):

        @pl.when(jnp.logical_not(stays(piece)))
        def _(piece=piece):
            final_copy(piece).wait_send()

    for which in range(2):
        for d in range(1, NZ):
            to = lax.rem(z + d, NZ)

            @pl.when((to > z) if which == 0 else (to < z))
            def _(which=which, d=d):
                z_copy(which, d).wait_send()

    write_gf.wait()
    write_out.wait()


def per_device(featurized, short_taps, residues, decay_rates, w_out, grad_out):
    operands = (featurized.transpose(1, 0, 2), short_taps, decay_rates.T, residues.T, w_out, grad_out)
    hbm = pl.BlockSpec(memory_space=pl.ANY)
    dma, V = pltpu.SemaphoreType.DMA, pltpu.VMEM
    block, gf = pl.pallas_call(
        kernel,
        out_shape=(jax.ShapeDtypeStruct((T, 2 * C), BF16), jax.ShapeDtypeStruct((3, T, C), BF16)),
        in_specs=[hbm] * 6,
        out_specs=(hbm, hbm),
        scratch_shapes=[
            V((3, T, C), BF16),
            V((3, 3, C), F32),
            V((MODES, C), F32),
            V((MODES, C), F32),
            V((NZ, C, C), BF16),
            V((NZ, NX, T, C), BF16),
            V((MODES, T, C), F32),
            V((MODES, T, C), F32),
            V((T, C), F32),
            V((8, 2 * T, C), F32),
            V((6, T, C), F32),
            V((T, C), F32),
            V((T, C), F32),
            V((T, C), F32),
            V((2, 8, C), F32),
            V((2, 8, C), F32),
            V((8, MODES, C), F32),
            V((2, NX, MODES, C), F32),
            V((2, NZ, MODES, C), F32),
            V((MODES, C), F32),
            V((NX, T, C), BF16),
            V((NX, T, C), F32),
            V((NX, T, C), BF16),
            V((NX, T, C), BF16),
            V((NY, NX, T, C), BF16),
            V((NY, 2, T, C), BF16),
            V((NY, 2, T, C), BF16),
            V((2, NY, 2, T, C), BF16),
            V((2, T, C), BF16),
            V((2, T, C), BF16),
            V((T, 2 * C), BF16),
            V((3, T, C), BF16),
            dma((8,)), dma((2, 4, PIECES)), dma((2, 4, PIECES)), dma((2,)), dma((2,)),
            dma((2, NX)), dma((2, NX)), dma((2, NZ)), dma((2, NZ)),
            dma((2, NX)), dma((2, NX)), dma((2, 3, 2)), dma((2, 3, 2)), dma((4, 2)), dma((4, 2)),
            dma((NX,)), dma((NX,)), dma((NX,)), dma((NX,)), dma((NY,)), dma((NY,)),
            dma((NY, 2)), dma((2, NY, 2)), dma((2,)), dma((2,)),
        ],
        compiler_params=pltpu.CompilerParams(
            collective_id=0, has_side_effects=True, vmem_limit_bytes=48000000
        ),
    )(*(pltpu.with_memory_space_constraint(v, pltpu.HBM) for v in operands))
    return (block, gf.transpose(1, 0, 2))


def solution(mesh):
    placed = (
        P("ctx", None, "fsdp"),
        P(None, None, "fsdp"),
        P("fsdp", None),
        P("fsdp", None),
        P("fsdp", "ctx"),
        P("ctx", None),
    )
    return jax.shard_map(
        per_device,
        mesh=mesh,
        in_specs=placed,
        out_specs=(P("ctx", "fsdp"), P("ctx", None, "fsdp")),
        check_vma=False,
    )
```

```python
import jax
import jax.numpy as jnp
from jax import lax
from jax.experimental import pallas as pl
from jax.experimental.pallas import tpu as pltpu
from jax.sharding import PartitionSpec as P

T = 128
C = 256
MODES = 16
NZ, NX, NY = 8, 4, 8
F32 = jnp.float32
BF16 = jnp.bfloat16
MESH = pl.DeviceIdType.MESH

H = T // 2
PIECES = 4
CHAIN_UP = {0: (4, 3, 2, 1), 1: (4, 3, 2, 1), 2: (3, 2, 1), 3: (3, 2, 1)}
CHAIN_DOWN = {0: (5, 6, 7), 1: (5, 6, 7), 2: (4, 5, 6, 7), 3: (4, 5, 6, 7)}
PROJECT_ORDER = (4, 3, 5, 2, 6, 1, 7, 0)


def kernel(
    feats_in, taps_in, a_in, res_in, w_ref, go_ref, out_hbm, gf_hbm,
    feats_ref, taps_ref, a_ref, res_ref, w_all, go_all, near, far, h_ref, pad_ref, mix_ref, conv_ref, gg_ref,
    acc_ref, tail_ref, halo_ref, state_ref, x_states, z_states, weight_ref, gated_ref, part_ref, give_ref, take_ref,
    mine_ref, pair_ref, chain_ref, land_ref, final_ref, out_ref, gf_ref,
    own_sem, w_send, w_recv, halo_send, halo_recv, x_send, x_recv, z_send, z_recv,
    go_send, go_recv, ring_send, ring_recv, share_send, share_recv,
    gated_send, gated_recv, give_send, give_recv, pair_send, pair_recv, y_send, y_recv, final_recv,
):
    f, k = lax.axis_index("fsdp"), lax.axis_index("ctx")
    y, core = f // 2, f % 2
    z, x = k // NX, k % NX

    def at(dz, dx):
        return lax.rem(z + dz + NZ, NZ) * NX + lax.rem(x + dx + NX, NX)

    def ctx(index):
        return {"fsdp": f, "ctx": index}

    def remote(src, dst, send, recv, device):
        return pltpu.make_async_remote_copy(
            src_ref=src, dst_ref=dst, send_sem=send, recv_sem=recv, device_id=device, device_id_type=MESH
        )

    following, previous = lax.rem(k + 1, NZ * NX), lax.rem(k + NZ * NX - 1, NZ * NX)
    partner = {"fsdp": y * 2 + 1 - core, "ctx": k}
    my_half = pl.ds(core * H, H)

    loads = [
        pltpu.make_async_copy(src, dst, own_sem.at[i])
        for i, (src, dst) in enumerate(
            [(feats_in, feats_ref), (a_in, a_ref), (res_in, res_ref), (taps_in, taps_ref), (w_ref, w_all.at[z])]
        )
    ]
    for load in loads:
        load.start()

    barrier = pltpu.get_barrier_semaphore()
    greeted = [{"fsdp": y * 2 + 1 - core, "ctx": at(0, d)} for d in range(NX)] + [ctx(at(0, d)) for d in range(1, NX)]
    greeted += [ctx(at(d, 0)) for d in range(1, NZ)] + [ctx(following), ctx(previous)]
    greeted += [{"fsdp": lax.rem(y + d, NY) * 2 + core, "ctx": k} for d in (1, NY - 1)]
    greeted += [
        {"fsdp": lax.rem(y + d, NY) * 2 + x // 2, "ctx": z * NX + core * 2 + i} for d in (1, NY - 1) for i in range(2)
    ]
    for device in greeted:
        pl.semaphore_signal(barrier, inc=1, device_id=device, device_id_type=MESH)
    pl.semaphore_wait(barrier, len(greeted))

    pending = []

    def go(copy):
        copy.start()
        pending.append(copy)

    def w_copy(distance, up, piece):
        block = lax.rem(z + (1 - distance if up else distance - 1) + NZ, NZ)
        span = pl.ds(piece * (C // PIECES), C // PIECES)
        src = w_ref.at[span, :] if distance == 1 else w_all.at[block, span, :]
        slot = (0 if up else 1), distance - 1, piece
        return remote(src, w_all.at[block, span, :], w_send.at[slot], w_recv.at[slot], ctx(at(1 if up else -1, 0)))

    def farthest(up, piece):
        return (piece < PIECES // 2) == up

    def w_relay(distance):
        for i in range(PIECES):
            for up in (True, False):
                piece = i if up else PIECES - 1 - i
                if distance == NZ // 2 and not farthest(up, piece):
                    continue
                span = pl.ds(piece * (C // PIECES), C // PIECES)
                block = w_all.at[lax.rem(z + (-distance if up else distance) + NZ, NZ), span, :]
                slot = (0 if up else 1), distance - 1, piece
                remote(block, block, w_send.at[slot], w_recv.at[slot], partner).wait_recv()
                if distance + 1 < NZ // 2 or (distance + 1 == NZ // 2 and farthest(up, piece)):
                    go(w_copy(distance + 1, up, piece))

    def strip_row(dy, i):
        return lax.rem(y + dy + NY, NY // 2) + i * (NY // 2)

    def go_out(i):
        row = strip_row(0, i)
        for d in (2, 1, 3):
            strip = go_ref.at[my_half, pl.ds(pl.multiple_of((row * NX + lax.rem(x + d, NX)) * C, C), C)]
            go(remote(strip, go_all.at[row, d, my_half, :], go_send.at[i, d], go_recv.at[i, d], ctx(at(0, d))))

    def own_rows():
        for row in range(NZ):
            columns = pl.ds(pl.multiple_of((row * NX + x) * C, C), C)
            pltpu.make_async_copy(go_ref.at[:, columns], go_all.at[row, 0], own_sem.at[5]).start()

    def strips(dy, i, half):
        return go_all.at[strip_row(dy, i), pl.ds(1, NX - 1), pl.ds(half * H, H), :]

    def go_copy(dy, up, i):
        region = strips(dy, i, core)
        slot = (0 if up else 1), (0 if dy == 0 else 2), i
        to = {"fsdp": lax.rem(y + (1 if up else NY - 1), NY) * 2 + core, "ctx": k}
        return remote(region, region, ring_send.at[slot], ring_recv.at[slot], to)

    def share_copy(dy, i, half):
        region = strips(dy, i, half)
        slot = dy + 1, i
        return remote(region, region, share_send.at[slot], share_recv.at[slot], partner)

    def go_first(i):
        for d in range(1, NX):
            landed = go_all.at[strip_row(0, i), d, my_half, :]
            remote(landed, landed, go_send.at[i, d], go_recv.at[i, d], partner).wait_recv()
        go(go_copy(0, True, i))
        go(go_copy(0, False, i))
        go(share_copy(0, i, core))

    def go_near(i):
        for up in (True, False):
            dy = -1 if up else 1
            region = strips(dy, i, core)
            slot = (0 if up else 1), 0, i
            remote(region, region, ring_send.at[slot], ring_recv.at[slot], partner).wait_recv()
            if i == (0 if up else 1):
                go(go_copy(dy, up, i))
            go(share_copy(dy, i, core))

    def go_far():
        for up in (True, False):
            i = 0 if up else 1
            region = strips(2, i, core)
            slot = (0 if up else 1), 2, i
            remote(region, region, ring_send.at[slot], ring_recv.at[slot], partner).wait_recv()
            go(share_copy(2, i, core))

    def shared():
        for dy in (0, -1, 1, 2):
            for i in range(2):
                share_copy(dy, i, 1 - core).wait_recv()
        pltpu.make_async_copy(go_all.at[:, 0], go_all.at[:, 0], own_sem.at[5]).wait()

    def from_x(dx):
        return lax.rem(x + dx + NX, NX)

    rows = lax.broadcasted_iota(jnp.int32, (T, 1), 0)
    steps = rows.astype(F32)

    def halo_copy(which, device):
        return remote(
            tail_ref.at[which], halo_ref.at[which], halo_send.at[which], halo_recv.at[which], ctx(device)
        )

    def send_tail():
        for j in range(3):
            last = feats_ref[j, T - 16 :, :].astype(F32)
            tail_ref[0, 2 * j : 2 * j + 2, :] = last[14:16]
        copy = halo_copy(0, following)
        copy.start()
        pending.append(copy)

    def tables(low):
        def body(n, c):
            a = a_ref[pl.ds(n, 1), :]
            scale = res_ref[pl.ds(n, 1), :] * jnp.sqrt(a)
            weight_ref[pl.ds(n, 1), :] = scale
            e = jnp.exp(-a * steps)
            near[n] = e
            far[n] = jnp.exp(-a * (T - 1 - steps))
            h_ref[...] += scale * e
            return c

        lax.fori_loop(low, low + 4, body, 0)

    def clear():
        h_ref[...] = jnp.zeros_like(h_ref)

    def end_state(table, signal_ref, which):
        def body(n, c):
            state_ref[which, pl.ds(n, 1), :] = jnp.sum(table[n] * signal_ref[...], axis=0, keepdims=True)
            return c

        lax.fori_loop(0, MODES, body, 0)

    def send_x(which):
        for d in range(1, NX):
            copy = remote(
                state_ref.at[which], x_states.at[which, x], x_send.at[which, d], x_recv.at[which, x], ctx(at(0, d))
            )
            copy.start()
            pending.append(copy)

    def mix():
        halo_copy(0, following).wait_recv()
        for j in range(3):
            now = feats_ref[j].astype(F32)
            one = jnp.where(k > 0, halo_ref[0, 2 * j + 1 : 2 * j + 2, :], 0.0)
            two = jnp.where(k > 0, halo_ref[0, 2 * j : 2 * j + 1, :], 0.0)
            back1 = jnp.where(rows == 0, one, pltpu.roll(now, 1, 0))
            back2 = jnp.where(rows == 0, two, jnp.where(rows == 1, one, pltpu.roll(now, 2, 0)))
            mix_ref[j] = (
                taps_ref[0, j : j + 1, :] * now + taps_ref[1, j : j + 1, :] * back1 + taps_ref[2, j : j + 1, :] * back2
            )
        acc_ref[...] = mix_ref[1] * mix_ref[2]

    def forward_send():
        end_state(far, acc_ref, 0)
        send_x(0)

    def shift_copies(which, low):
        value = acc_ref[...]
        for r in range(low, low + 4):
            if which == 0:
                pad_ref[r, :T, :] = jnp.zeros_like(value)
                pad_ref[r, T:, :] = jnp.where(rows >= r, pltpu.roll(value, r, 0), 0.0) if r else value
            else:
                pad_ref[r, T:, :] = jnp.zeros_like(value)
                pad_ref[r, :T, :] = jnp.where(rows < T - r, pltpu.roll(value, T - r, 0), 0.0) if r else value

    def local_taps(which, low, high, dst, begin):
        def body(q, total):
            for r in range(8):
                start = pl.multiple_of((T - 8 * q) if which == 0 else 8 * q, 8)
                total = total + h_ref[pl.ds(8 * q + r, 1), :] * pad_ref[r, pl.ds(start, T), :]
            return total

        first = jnp.zeros((T, C), F32) if begin else dst[...]
        dst[...] = lax.fori_loop(low, high, body, first)

    def combine_x(which):
        x_states[which, x] = state_ref[which]
        for d in range(1, NX):
            other = lax.rem(x + d, NX)
            remote(
                state_ref.at[which], x_states.at[which, other], x_send.at[which, d], x_recv.at[which, other], ctx(k)
            ).wait_recv()
        a = a_ref[...]
        entering, total = jnp.zeros_like(a), jnp.zeros_like(a)
        for j in range(NX):
            gap = (x - 1 - j) if which == 0 else (j - x - 1)
            reach = (NX - 1 - j) if which == 0 else j
            decay = jnp.exp(-a * (T * jnp.maximum(gap, 0)).astype(F32))
            state = x_states[which, j]
            entering = entering + jnp.where(gap >= 0, decay * state, 0.0)
            total = total + jnp.exp(-a * float(T * reach)) * state
        state_ref[2 + which] = entering
        state_ref[4 + which] = total
        for d in range(1, NZ):
            to = lax.rem(z + d, NZ)

            @pl.when((to > z) if which == 0 else (to < z))
            def _(d=d):
                z_copy(which, d).start()

    def z_copy(which, d):
        return remote(
            state_ref.at[4 + which], z_states.at[which, z], z_send.at[which, d], z_recv.at[which, z], ctx(at(d, 0))
        )

    def combine_z(which):
        a = a_ref[...]
        state_ref[6] = jnp.zeros_like(a)
        for d in range(1, NZ):
            other = lax.rem(z + d, NZ)

            @pl.when((other < z) if which == 0 else (other > z))
            def _(d=d, other=other):
                remote(
                    state_ref.at[4 + which],
                    z_states.at[which, other],
                    z_send.at[which, d],
                    z_recv.at[which, other],
                    ctx(at(d, 0)),
                ).wait_recv()
                gap = (z - 1 - other) if which == 0 else (other - z - 1)
                state_ref[6] += jnp.exp(-a * (NX * T * gap).astype(F32)) * z_states[which, other]

        inside = x if which == 0 else NX - 1 - x
        entering = state_ref[2 + which] + jnp.exp(-a * (T * inside).astype(F32)) * state_ref[6]
        state_ref[7] = weight_ref[...] * jnp.exp(-a) * entering

    def boundary(table, dst):
        def body(n, total):
            return total + table[n] * state_ref[7, pl.ds(n, 1), :]

        dst[...] = lax.fori_loop(0, MODES, body, dst[...])

    def gate():
        combine_z(0)
        boundary(near, conv_ref)
        gated_ref[x] = (mix_ref[0] * conv_ref[...]).astype(BF16)
        for d in range(1, NX):
            go(remote(gated_ref.at[x], gated_ref.at[x], gated_send.at[d], gated_recv.at[d], ctx(at(0, d))))

    def transpose_project():
        def body(row, c):
            part = lax.dot_general(
                go_all[row].reshape(NX * T, C), w_all[row], (((1,), (1,)), ((), ())), preferred_element_type=F32
            )
            part_ref[...] += part.reshape(NX, T, C)
            return c

        part_ref[...] = jnp.zeros_like(part_ref)
        lax.fori_loop(0, NZ, body, 0)
        for d in range(1, NX):
            give_ref[d] = part_ref[d].astype(BF16)
            go(remote(give_ref.at[d], take_ref.at[d], give_send.at[d], give_recv.at[d], ctx(at(0, -d))))

    def sum_gated():
        gg_ref[...] = part_ref[0]
        for d in range(1, NX):
            remote(give_ref.at[d], take_ref.at[d], give_send.at[d], give_recv.at[d], partner).wait_recv()
            gg_ref[...] += take_ref[d].astype(F32)

    def gated_arrived():
        for d in range(1, NX):
            source = from_x(-d)
            remote(
                gated_ref.at[source], gated_ref.at[source], gated_send.at[d], gated_recv.at[d], partner
            ).wait_recv()

    def target(e):
        return lax.rem(y + e, NY)

    def pair_copy(e):
        row = target(e)
        return remote(
            mine_ref.at[row, pl.ds((1 - core) * 2, 2)], pair_ref.at[row], pair_send.at[e], pair_recv.at[e], partner
        )

    def project(e):
        row = target(e)
        part = jnp.dot(gated_ref[...].reshape(NX * T, C), w_all[row], preferred_element_type=F32)
        mine_ref[row] = part.astype(BF16).reshape(NX, T, C)
        go(pair_copy(e))

    paired = set()

    def rows_of(piece):
        return pl.ds(piece % 2 * H, H)

    def term(e, piece):
        if e not in paired:
            pair_copy(e).wait_recv()
            paired.add(e)
        row, span = target(e), rows_of(piece)
        mine = mine_ref[row, core * 2 + piece // 2, span, :]
        return mine.astype(F32) + pair_ref[row, piece // 2, span, :].astype(F32)

    owner = x // 2

    def owner_of(piece, dy):
        return {"fsdp": lax.rem(y + dy + NY, NY) * 2 + owner, "ctx": z * NX + core * 2 + piece // 2}

    def to_owner(piece, kind, e, dy):
        there = kind, x % 2, rows_of(piece), slice(None)
        return remote(
            chain_ref.at[e, piece],
            final_ref.at[there],
            y_send.at[e, piece],
            final_recv.at[kind, x % 2, piece % 2],
            owner_of(piece, dy),
        )

    def chain(up, e, piece):
        total = term(e, piece)
        if e != (CHAIN_UP if up else CHAIN_DOWN)[piece][0]:
            slot = (0 if up else 1), e, piece
            landed = land_ref.at[slot]
            remote(landed, landed, y_send.at[0, 0], y_recv.at[slot], partner).wait_recv()
            total = total + land_ref[slot].astype(F32)
        chain_ref[e, piece] = total.astype(BF16)
        if e == (1 if up else NY - 1):
            go(to_owner(piece, 1 if up else 2, e, 1 if up else -1))
            return
        there = (0 if up else 1), (e - 1 if up else e + 1), piece
        to = {"fsdp": lax.rem(y + (1 if up else NY - 1), NY) * 2 + core, "ctx": k}
        go(remote(chain_ref.at[e, piece], land_ref.at[there], y_send.at[e, piece], y_recv.at[there], to))

    def stage(n):
        for i in range(2):
            chain(True, 4 - n, i)
            chain(False, 4 + n, 2 + i)
        if n < 3:
            for i in range(2):
                chain(True, 3 - n, 2 + i)
                chain(False, 5 + n, i)

    def stays(piece):
        return jnp.logical_and(owner == core, x % 2 == piece // 2)

    def own_term():
        for piece in range(4):
            chain_ref[0, piece] = term(0, piece).astype(BF16)

            @pl.when(jnp.logical_not(stays(piece)))
            def _(piece=piece):
                to_owner(piece, 0, 0, 0).start()

    def collect():
        for half in range(2):
            local = jnp.logical_and(owner == core, x % 2 == half)
            for part in range(2):
                span, columns = rows_of(part), pl.ds(half * C, C)

                @pl.when(local)
                def _(half=half, part=part, span=span):
                    final_ref[0, half, span, :] = chain_ref[0, 2 * half + part]

                for kind in range(3):
                    landed = final_ref.at[kind, half, span, :]
                    arrived = remote(landed, landed, y_send.at[0, 0], final_recv.at[kind, half, part], partner)
                    if kind:
                        arrived.wait_recv()
                    else:
                        pl.when(jnp.logical_not(local))(arrived.wait_recv)
                total = final_ref[0, half, span, :].astype(F32) + final_ref[1, half, span, :].astype(F32)
                out_ref[span, columns] = (total + final_ref[2, half, span, :].astype(F32)).astype(BF16)

    for load in loads[:4]:
        load.wait()
    send_tail()
    for piece in range(PIECES):
        go(w_copy(1, True, piece))
        go(w_copy(1, False, PIECES - 1 - piece))
    go_out(0)
    clear()
    for i in range(4):
        tables(4 * i)
    go_out(1)
    own_rows()
    mix()
    forward_send()
    w_relay(1)
    go_first(0)
    shift_copies(0, 0)
    shift_copies(0, 4)
    local_taps(0, 0, 8, conv_ref, True)
    go_first(1)
    combine_x(0)
    w_relay(2)
    local_taps(0, 8, 16, conv_ref, False)
    go_near(0)
    w_relay(3)
    go_near(1)
    gate()
    w_relay(4)
    loads[4].wait()
    go_far()
    shared()
    transpose_project()
    gated_arrived()
    for e in PROJECT_ORDER[:5]:
        project(e)
    stage(0)
    for e in PROJECT_ORDER[5:]:
        project(e)
    sum_gated()
    acc_ref[...] = gg_ref[...] * mix_ref[0]
    end_state(near, acc_ref, 1)
    send_x(1)
    stage(1)
    own_term()
    combine_x(1)
    gg_ref[...] = gg_ref[...] * conv_ref[...]
    shift_copies(1, 0)
    shift_copies(1, 4)
    local_taps(1, 0, 8, acc_ref, True)
    stage(2)
    local_taps(1, 8, 16, acc_ref, False)
    combine_z(1)
    boundary(far, acc_ref)
    for j in range(3):
        value = gg_ref[...] if j == 0 else acc_ref[...] * mix_ref[3 - j]
        mix_ref[3 + j] = value
        tail_ref[1, 2 * j : 2 * j + 2, :] = value[0:2]
    go(halo_copy(1, previous))
    stage(3)
    halo_copy(1, previous).wait_recv()
    inner = k < NZ * NX - 1
    for j in range(3):
        now = mix_ref[3 + j]
        one = jnp.where(inner, halo_ref[1, 2 * j : 2 * j + 1, :], 0.0)
        two = jnp.where(inner, halo_ref[1, 2 * j + 1 : 2 * j + 2, :], 0.0)
        ahead1 = jnp.where(rows == T - 1, one, pltpu.roll(now, T - 1, 0))
        ahead2 = jnp.where(rows == T - 1, two, jnp.where(rows == T - 2, one, pltpu.roll(now, T - 2, 0)))
        gf_ref[j] = (
            taps_ref[0, j : j + 1, :] * now + taps_ref[1, j : j + 1, :] * ahead1 + taps_ref[2, j : j + 1, :] * ahead2
        ).astype(BF16)
    write_gf = pltpu.make_async_copy(gf_ref, gf_hbm, own_sem.at[6])
    write_gf.start()
    collect()
    write_out = pltpu.make_async_copy(out_ref, out_hbm, own_sem.at[7])
    write_out.start()
    for copy in pending:
        copy.wait_send()
    for piece in range(4):

        @pl.when(jnp.logical_not(stays(piece)))
        def _(piece=piece):
            to_owner(piece, 0, 0, 0).wait_send()

    for which in range(2):
        for d in range(1, NZ):
            to = lax.rem(z + d, NZ)

            @pl.when((to > z) if which == 0 else (to < z))
            def _(which=which, d=d):
                z_copy(which, d).wait_send()

    write_gf.wait()
    write_out.wait()


def per_device(featurized, short_taps, residues, decay_rates, w_out, grad_out):
    operands = (featurized.transpose(1, 0, 2), short_taps, decay_rates.T, residues.T, w_out, grad_out)
    hbm = pl.BlockSpec(memory_space=pl.ANY)
    dma, V = pltpu.SemaphoreType.DMA, pltpu.VMEM
    block, gf = pl.pallas_call(
        kernel,
        out_shape=(jax.ShapeDtypeStruct((T, 2 * C), BF16), jax.ShapeDtypeStruct((3, T, C), BF16)),
        in_specs=[hbm] * 6,
        out_specs=(hbm, hbm),
        scratch_shapes=[
            V((3, T, C), BF16),
            V((3, 3, C), F32),
            V((MODES, C), F32),
            V((MODES, C), F32),
            V((NZ, C, C), BF16),
            V((NZ, NX, T, C), BF16),
            V((MODES, T, C), F32),
            V((MODES, T, C), F32),
            V((T, C), F32),
            V((8, 2 * T, C), F32),
            V((6, T, C), F32),
            V((T, C), F32),
            V((T, C), F32),
            V((T, C), F32),
            V((2, 8, C), F32),
            V((2, 8, C), F32),
            V((8, MODES, C), F32),
            V((2, NX, MODES, C), F32),
            V((2, NZ, MODES, C), F32),
            V((MODES, C), F32),
            V((NX, T, C), BF16),
            V((NX, T, C), F32),
            V((NX, T, C), BF16),
            V((NX, T, C), BF16),
            V((NY, NX, T, C), BF16),
            V((NY, 2, T, C), BF16),
            V((NY, 4, H, C), BF16),
            V((2, NY, 4, H, C), BF16),
            V((3, 2, T, C), BF16),
            V((T, 2 * C), BF16),
            V((3, T, C), BF16),
            dma((8,)), dma((2, 4, PIECES)), dma((2, 4, PIECES)), dma((2,)), dma((2,)),
            dma((2, NX)), dma((2, NX)), dma((2, NZ)), dma((2, NZ)),
            dma((2, NX)), dma((2, NX)), dma((2, 3, 2)), dma((2, 3, 2)), dma((4, 2)), dma((4, 2)),
            dma((NX,)), dma((NX,)), dma((NX,)), dma((NX,)), dma((NY,)), dma((NY,)),
            dma((NY, 4)), dma((2, NY, 4)), dma((3, 2, 2)),
        ],
        compiler_params=pltpu.CompilerParams(
            collective_id=0, has_side_effects=True, vmem_limit_bytes=48000000
        ),
    )(*(pltpu.with_memory_space_constraint(v, pltpu.HBM) for v in operands))
    return (block, gf.transpose(1, 0, 2))


def solution(mesh):
    placed = (
        P("ctx", None, "fsdp"),
        P(None, None, "fsdp"),
        P("fsdp", None),
        P("fsdp", None),
        P("fsdp", "ctx"),
        P("ctx", None),
    )
    return jax.shard_map(
        per_device,
        mesh=mesh,
        in_specs=placed,
        out_specs=(P("ctx", "fsdp"), P("ctx", None, "fsdp")),
        check_vma=False,
    )
```

```python
import jax
import jax.numpy as jnp
from jax import lax
from jax.experimental import pallas as pl
from jax.experimental.pallas import tpu as pltpu
from jax.sharding import PartitionSpec as P

T = 128
C = 256
MODES = 16
NZ, NX, NY = 8, 4, 8
F32 = jnp.float32
BF16 = jnp.bfloat16
MESH = pl.DeviceIdType.MESH

H = T // 2
PIECES = 4
CHAIN_UP = {0: (4, 3, 2, 1), 1: (4, 3, 2, 1), 2: (3, 2, 1), 3: (3, 2, 1)}
CHAIN_DOWN = {0: (5, 6, 7), 1: (5, 6, 7), 2: (4, 5, 6, 7), 3: (4, 5, 6, 7)}
PROJECT_ORDER = (4, 3, 5, 2, 6, 1, 7, 0)


def kernel(
    feats_in, taps_in, a_in, res_in, w_ref, go_ref, out_hbm, gf_hbm,
    feats_ref, taps_ref, a_ref, res_ref, w_all, go_all, near, far, h_ref, pad_ref, mix_ref, conv_ref, gg_ref,
    acc_ref, tail_ref, halo_ref, state_ref, x_states, z_states, weight_ref, gated_ref, part_ref, give_ref, take_ref,
    mine_ref, pair_ref, chain_ref, land_ref, final_ref, out_ref, gf_ref,
    own_sem, w_send, w_recv, halo_send, halo_recv, x_send, x_recv, z_send, z_recv,
    go_send, go_recv, ring_send, ring_recv, share_send, share_recv,
    gated_send, gated_recv, give_send, give_recv, pair_send, pair_recv, y_send, own_send, y_recv, final_recv,
):
    f, k = lax.axis_index("fsdp"), lax.axis_index("ctx")
    y, core = f // 2, f % 2
    z, x = k // NX, k % NX

    def at(dz, dx):
        return lax.rem(z + dz + NZ, NZ) * NX + lax.rem(x + dx + NX, NX)

    def ctx(index):
        return {"fsdp": f, "ctx": index}

    def remote(src, dst, send, recv, device):
        return pltpu.make_async_remote_copy(
            src_ref=src, dst_ref=dst, send_sem=send, recv_sem=recv, device_id=device, device_id_type=MESH
        )

    following, previous = lax.rem(k + 1, NZ * NX), lax.rem(k + NZ * NX - 1, NZ * NX)
    partner = {"fsdp": y * 2 + 1 - core, "ctx": k}
    my_half = pl.ds(core * H, H)

    loads = [
        pltpu.make_async_copy(src, dst, own_sem.at[i])
        for i, (src, dst) in enumerate(
            [(feats_in, feats_ref), (a_in, a_ref), (res_in, res_ref), (taps_in, taps_ref), (w_ref, w_all.at[z])]
        )
    ]
    for load in loads:
        load.start()

    barrier = pltpu.get_barrier_semaphore()
    greeted = [{"fsdp": y * 2 + 1 - core, "ctx": at(0, d)} for d in range(NX)] + [ctx(at(0, d)) for d in range(1, NX)]
    greeted += [ctx(at(d, 0)) for d in range(1, NZ)] + [ctx(following), ctx(previous)]
    greeted += [{"fsdp": lax.rem(y + d, NY) * 2 + core, "ctx": k} for d in (1, NY - 1)]
    greeted += [
        {"fsdp": lax.rem(y + d, NY) * 2 + x // 2, "ctx": z * NX + core * 2 + i} for d in (1, NY - 1) for i in range(2)
    ]
    for device in greeted:
        pl.semaphore_signal(barrier, inc=1, device_id=device, device_id_type=MESH)
    pl.semaphore_wait(barrier, len(greeted))

    def go(copy):
        copy.start()

    def w_copy(distance, up, piece):
        block = lax.rem(z + (1 - distance if up else distance - 1) + NZ, NZ)
        span = pl.ds(piece * (C // PIECES), C // PIECES)
        src = w_ref.at[span, :] if distance == 1 else w_all.at[block, span, :]
        slot = (0 if up else 1), distance - 1, piece
        return remote(src, w_all.at[block, span, :], w_send.at[0], w_recv.at[slot], ctx(at(1 if up else -1, 0)))

    def farthest(up, piece):
        return (piece < PIECES // 2) == up

    def w_relay(distance):
        for i in range(PIECES):
            for up in (True, False):
                piece = i if up else PIECES - 1 - i
                if distance == NZ // 2 and not farthest(up, piece):
                    continue
                span = pl.ds(piece * (C // PIECES), C // PIECES)
                block = w_all.at[lax.rem(z + (-distance if up else distance) + NZ, NZ), span, :]
                slot = (0 if up else 1), distance - 1, piece
                remote(block, block, w_send.at[0], w_recv.at[slot], partner).wait_recv()
                if distance + 1 < NZ // 2 or (distance + 1 == NZ // 2 and farthest(up, piece)):
                    go(w_copy(distance + 1, up, piece))

    def strip_row(dy, i):
        return lax.rem(y + dy + NY, NY // 2) + i * (NY // 2)

    def go_out(i):
        row = strip_row(0, i)
        for d in (2, 1, 3):
            strip = go_ref.at[my_half, pl.ds(pl.multiple_of((row * NX + lax.rem(x + d, NX)) * C, C), C)]
            go(remote(strip, go_all.at[row, d, my_half, :], go_send.at[0], go_recv.at[i], ctx(at(0, d))))

    def own_rows():
        for row in range(NZ):
            columns = pl.ds(pl.multiple_of((row * NX + x) * C, C), C)
            pltpu.make_async_copy(go_ref.at[:, columns], go_all.at[row, 0], own_sem.at[5]).start()

    def strips(dy, i, half):
        return go_all.at[strip_row(dy, i), pl.ds(1, NX - 1), pl.ds(half * H, H), :]

    def go_copy(dy, up, i):
        region = strips(dy, i, core)
        slot = (0 if up else 1), (i if dy == 0 else 2)
        to = {"fsdp": lax.rem(y + (1 if up else NY - 1), NY) * 2 + core, "ctx": k}
        return remote(region, region, ring_send.at[0], ring_recv.at[slot], to)

    def share_copy(dy, i, half):
        region = strips(dy, i, half)
        return remote(region, region, share_send.at[0], share_recv.at[0], partner)

    def go_first(i):
        landed = strips(0, i, core)
        remote(landed, landed, go_send.at[0], go_recv.at[i], partner).wait_recv()
        go(go_copy(0, True, i))
        go(go_copy(0, False, i))
        go(share_copy(0, i, core))

    def go_near(i):
        for up in (True, False):
            dy = -1 if up else 1
            region = strips(dy, i, core)
            slot = (0 if up else 1), i
            remote(region, region, ring_send.at[0], ring_recv.at[slot], partner).wait_recv()
            if i == (0 if up else 1):
                go(go_copy(dy, up, i))
            go(share_copy(dy, i, core))

    def go_far():
        for up in (True, False):
            i = 0 if up else 1
            region = strips(2, i, core)
            slot = (0 if up else 1), 2
            remote(region, region, ring_send.at[0], ring_recv.at[slot], partner).wait_recv()
            go(share_copy(2, i, core))

    def shared():
        region = go_all.at[:, pl.ds(1, NX - 1), pl.ds((1 - core) * H, H), :]
        remote(region, region, share_send.at[0], share_recv.at[0], partner).wait_recv()
        pltpu.make_async_copy(go_all.at[:, 0], go_all.at[:, 0], own_sem.at[5]).wait()

    def from_x(dx):
        return lax.rem(x + dx + NX, NX)

    rows = lax.broadcasted_iota(jnp.int32, (T, 1), 0)
    steps = rows.astype(F32)

    def halo_copy(which, device):
        return remote(
            tail_ref.at[which], halo_ref.at[which], halo_send.at[0], halo_recv.at[which], ctx(device)
        )

    def send_tail():
        for j in range(3):
            last = feats_ref[j, T - 16 :, :].astype(F32)
            tail_ref[0, 2 * j : 2 * j + 2, :] = last[14:16]
        copy = halo_copy(0, following)
        copy.start()

    def tables(low):
        def body(n, c):
            a = a_ref[pl.ds(n, 1), :]
            scale = res_ref[pl.ds(n, 1), :] * jnp.sqrt(a)
            weight_ref[pl.ds(n, 1), :] = scale
            e = jnp.exp(-a * steps)
            near[n] = e
            far[n] = jnp.exp(-a * (T - 1 - steps))
            h_ref[...] += scale * e
            return c

        lax.fori_loop(low, low + 4, body, 0)

    def clear():
        h_ref[...] = jnp.zeros_like(h_ref)

    def end_state(table, signal_ref, which):
        def body(n, c):
            state_ref[which, pl.ds(n, 1), :] = jnp.sum(table[n] * signal_ref[...], axis=0, keepdims=True)
            return c

        lax.fori_loop(0, MODES, body, 0)

    def send_x(which):
        for d in range(1, NX):
            copy = remote(
                state_ref.at[which], x_states.at[which, x], x_send.at[which], x_recv.at[which, x], ctx(at(0, d))
            )
            copy.start()

    def mix():
        halo_copy(0, following).wait_recv()
        for j in range(3):
            now = feats_ref[j].astype(F32)
            one = jnp.where(k > 0, halo_ref[0, 2 * j + 1 : 2 * j + 2, :], 0.0)
            two = jnp.where(k > 0, halo_ref[0, 2 * j : 2 * j + 1, :], 0.0)
            back1 = jnp.where(rows == 0, one, pltpu.roll(now, 1, 0))
            back2 = jnp.where(rows == 0, two, jnp.where(rows == 1, one, pltpu.roll(now, 2, 0)))
            mix_ref[j] = (
                taps_ref[0, j : j + 1, :] * now + taps_ref[1, j : j + 1, :] * back1 + taps_ref[2, j : j + 1, :] * back2
            )
        acc_ref[...] = mix_ref[1] * mix_ref[2]

    def forward_send():
        end_state(far, acc_ref, 0)
        send_x(0)

    def shift_copies(which, low):
        value = acc_ref[...]
        for r in range(low, low + 4):
            if which == 0:
                pad_ref[r, :T, :] = jnp.zeros_like(value)
                pad_ref[r, T:, :] = jnp.where(rows >= r, pltpu.roll(value, r, 0), 0.0) if r else value
            else:
                pad_ref[r, T:, :] = jnp.zeros_like(value)
                pad_ref[r, :T, :] = jnp.where(rows < T - r, pltpu.roll(value, T - r, 0), 0.0) if r else value

    def local_taps(which, low, high, dst, begin):
        def body(q, total):
            for r in range(8):
                start = pl.multiple_of((T - 8 * q) if which == 0 else 8 * q, 8)
                total = total + h_ref[pl.ds(8 * q + r, 1), :] * pad_ref[r, pl.ds(start, T), :]
            return total

        first = jnp.zeros((T, C), F32) if begin else dst[...]
        dst[...] = lax.fori_loop(low, high, body, first)

    def combine_x(which):
        x_states[which, x] = state_ref[which]
        for d in range(1, NX):
            other = lax.rem(x + d, NX)
            remote(
                state_ref.at[which], x_states.at[which, other], x_send.at[which], x_recv.at[which, other], ctx(k)
            ).wait_recv()
        a = a_ref[...]
        entering, total = jnp.zeros_like(a), jnp.zeros_like(a)
        for j in range(NX):
            gap = (x - 1 - j) if which == 0 else (j - x - 1)
            reach = (NX - 1 - j) if which == 0 else j
            decay = jnp.exp(-a * (T * jnp.maximum(gap, 0)).astype(F32))
            state = x_states[which, j]
            entering = entering + jnp.where(gap >= 0, decay * state, 0.0)
            total = total + jnp.exp(-a * float(T * reach)) * state
        state_ref[2 + which] = entering
        state_ref[4 + which] = total
        for d in range(1, NZ):
            to = lax.rem(z + d, NZ)

            @pl.when((to > z) if which == 0 else (to < z))
            def _(d=d):
                z_copy(which, d).start()

    def z_copy(which, d):
        return remote(
            state_ref.at[4 + which], z_states.at[which, z], z_send.at[0], z_recv.at[z], ctx(at(d, 0))
        )

    def combine_z(which):
        a = a_ref[...]
        state_ref[6] = jnp.zeros_like(a)
        for d in range(1, NZ):
            other = lax.rem(z + d, NZ)

            @pl.when((other < z) if which == 0 else (other > z))
            def _(d=d, other=other):
                remote(
                    state_ref.at[4 + which],
                    z_states.at[which, other],
                    z_send.at[0],
                    z_recv.at[other],
                    ctx(at(d, 0)),
                ).wait_recv()
                gap = (z - 1 - other) if which == 0 else (other - z - 1)
                state_ref[6] += jnp.exp(-a * (NX * T * gap).astype(F32)) * z_states[which, other]

        inside = x if which == 0 else NX - 1 - x
        entering = state_ref[2 + which] + jnp.exp(-a * (T * inside).astype(F32)) * state_ref[6]
        state_ref[7] = weight_ref[...] * jnp.exp(-a) * entering

    def boundary(table, dst):
        def body(n, total):
            return total + table[n] * state_ref[7, pl.ds(n, 1), :]

        dst[...] = lax.fori_loop(0, MODES, body, dst[...])

    def gate():
        combine_z(0)
        boundary(near, conv_ref)
        gated_ref[x] = (mix_ref[0] * conv_ref[...]).astype(BF16)
        for d in range(1, NX):
            go(remote(gated_ref.at[x], gated_ref.at[x], gated_send.at[0], gated_recv.at[d], ctx(at(0, d))))

    def transpose_project():
        def body(row, c):
            part = lax.dot_general(
                go_all[row].reshape(NX * T, C), w_all[row], (((1,), (1,)), ((), ())), preferred_element_type=F32
            )
            part_ref[...] += part.reshape(NX, T, C)
            return c

        part_ref[...] = jnp.zeros_like(part_ref)
        lax.fori_loop(0, NZ, body, 0)
        for d in range(1, NX):
            give_ref[d] = part_ref[d].astype(BF16)
            go(remote(give_ref.at[d], take_ref.at[d], give_send.at[0], give_recv.at[0], ctx(at(0, -d))))

    def sum_gated():
        gg_ref[...] = part_ref[0]
        taken = take_ref.at[pl.ds(1, NX - 1)]
        remote(taken, taken, give_send.at[0], give_recv.at[0], partner).wait_recv()
        for d in range(1, NX):
            gg_ref[...] += take_ref[d].astype(F32)

    def gated_arrived():
        for d in range(1, NX):
            source = from_x(-d)
            remote(
                gated_ref.at[source], gated_ref.at[source], gated_send.at[0], gated_recv.at[d], partner
            ).wait_recv()

    def target(e):
        return lax.rem(y + e, NY)

    def pair_copy(e):
        row = target(e)
        return remote(
            mine_ref.at[row, pl.ds((1 - core) * 2, 2)], pair_ref.at[row], pair_send.at[0], pair_recv.at[e], partner
        )

    def project(e):
        row = target(e)
        part = jnp.dot(gated_ref[...].reshape(NX * T, C), w_all[row], preferred_element_type=F32)
        mine_ref[row] = part.astype(BF16).reshape(NX, T, C)
        go(pair_copy(e))

    paired = set()

    def rows_of(piece):
        return pl.ds(piece % 2 * H, H)

    def term(e, piece):
        if e not in paired:
            pair_copy(e).wait_recv()
            paired.add(e)
        row, span = target(e), rows_of(piece)
        mine = mine_ref[row, core * 2 + piece // 2, span, :]
        return mine.astype(F32) + pair_ref[row, piece // 2, span, :].astype(F32)

    owner = x // 2

    def owner_of(piece, dy):
        return {"fsdp": lax.rem(y + dy + NY, NY) * 2 + owner, "ctx": z * NX + core * 2 + piece // 2}

    def to_owner(piece, kind, e, dy):
        there = kind, x % 2, rows_of(piece), slice(None)
        return remote(
            chain_ref.at[e, piece],
            final_ref.at[there],
            y_send.at[0] if kind else own_send.at[piece],
            final_recv.at[kind, x % 2, piece % 2],
            owner_of(piece, dy),
        )

    def chain(up, e, piece):
        total = term(e, piece)
        if e != (CHAIN_UP if up else CHAIN_DOWN)[piece][0]:
            slot = (0 if up else 1), e, piece
            landed = land_ref.at[slot]
            remote(landed, landed, y_send.at[0], y_recv.at[slot[0], e - (1 if up else 5), piece], partner).wait_recv()
            total = total + land_ref[slot].astype(F32)
        chain_ref[e, piece] = total.astype(BF16)
        if e == (1 if up else NY - 1):
            go(to_owner(piece, 1 if up else 2, e, 1 if up else -1))
            return
        there = (0 if up else 1), (e - 1 if up else e + 1), piece
        to = {"fsdp": lax.rem(y + (1 if up else NY - 1), NY) * 2 + core, "ctx": k}
        go(remote(chain_ref.at[e, piece], land_ref.at[there], y_send.at[0], y_recv.at[there[0], there[1] - (1 if up else 5), piece], to))

    def stage(n):
        for i in range(2):
            chain(True, 4 - n, i)
            chain(False, 4 + n, 2 + i)
        if n < 3:
            for i in range(2):
                chain(True, 3 - n, 2 + i)
                chain(False, 5 + n, i)

    def stays(piece):
        return jnp.logical_and(owner == core, x % 2 == piece // 2)

    def own_term():
        for piece in range(4):
            chain_ref[0, piece] = term(0, piece).astype(BF16)

            @pl.when(jnp.logical_not(stays(piece)))
            def _(piece=piece):
                to_owner(piece, 0, 0, 0).start()

    def collect():
        for half in range(2):
            local = jnp.logical_and(owner == core, x % 2 == half)
            for part in range(2):
                span, columns = rows_of(part), pl.ds(half * C, C)

                @pl.when(local)
                def _(half=half, part=part, span=span):
                    final_ref[0, half, span, :] = chain_ref[0, 2 * half + part]

                for kind in range(3):
                    landed = final_ref.at[kind, half, span, :]
                    arrived = remote(landed, landed, y_send.at[0], final_recv.at[kind, half, part], partner)
                    if kind:
                        arrived.wait_recv()
                    else:
                        pl.when(jnp.logical_not(local))(arrived.wait_recv)
                total = final_ref[0, half, span, :].astype(F32) + final_ref[1, half, span, :].astype(F32)
                out_ref[span, columns] = (total + final_ref[2, half, span, :].astype(F32)).astype(BF16)

    for load in loads[:4]:
        load.wait()
    send_tail()
    for piece in range(PIECES):
        go(w_copy(1, True, piece))
        go(w_copy(1, False, PIECES - 1 - piece))
    go_out(0)
    clear()
    for i in range(4):
        tables(4 * i)
    go_out(1)
    own_rows()
    mix()
    forward_send()
    w_relay(1)
    go_first(0)
    shift_copies(0, 0)
    shift_copies(0, 4)
    local_taps(0, 0, 8, conv_ref, True)
    go_first(1)
    combine_x(0)
    w_relay(2)
    local_taps(0, 8, 16, conv_ref, False)
    go_near(0)
    w_relay(3)
    go_near(1)
    gate()
    w_relay(4)
    loads[4].wait()
    go_far()
    shared()
    transpose_project()
    gated_arrived()
    for e in PROJECT_ORDER[:5]:
        project(e)
    stage(0)
    for e in PROJECT_ORDER[5:]:
        project(e)
    sum_gated()
    acc_ref[...] = gg_ref[...] * mix_ref[0]
    end_state(near, acc_ref, 1)
    send_x(1)
    stage(1)
    own_term()
    combine_x(1)
    gg_ref[...] = gg_ref[...] * conv_ref[...]
    shift_copies(1, 0)
    shift_copies(1, 4)
    local_taps(1, 0, 8, acc_ref, True)
    stage(2)
    local_taps(1, 8, 16, acc_ref, False)
    combine_z(1)
    boundary(far, acc_ref)
    for j in range(3):
        value = gg_ref[...] if j == 0 else acc_ref[...] * mix_ref[3 - j]
        mix_ref[3 + j] = value
        tail_ref[1, 2 * j : 2 * j + 2, :] = value[0:2]
    go(halo_copy(1, previous))
    stage(3)
    halo_copy(1, previous).wait_recv()
    inner = k < NZ * NX - 1
    for j in range(3):
        now = mix_ref[3 + j]
        one = jnp.where(inner, halo_ref[1, 2 * j : 2 * j + 1, :], 0.0)
        two = jnp.where(inner, halo_ref[1, 2 * j + 1 : 2 * j + 2, :], 0.0)
        ahead1 = jnp.where(rows == T - 1, one, pltpu.roll(now, T - 1, 0))
        ahead2 = jnp.where(rows == T - 1, two, jnp.where(rows == T - 2, one, pltpu.roll(now, T - 2, 0)))
        gf_ref[j] = (
            taps_ref[0, j : j + 1, :] * now + taps_ref[1, j : j + 1, :] * ahead1 + taps_ref[2, j : j + 1, :] * ahead2
        ).astype(BF16)
    write_gf = pltpu.make_async_copy(gf_ref, gf_hbm, own_sem.at[6])
    write_gf.start()
    collect()
    write_out = pltpu.make_async_copy(out_ref, out_hbm, own_sem.at[7])
    write_out.start()
    rows_sent = go_all.at[pl.ds(0, 6), pl.ds(1, NX - 1), my_half, :]
    for sent, semaphore in [
        (w_all.at[pl.ds(0, NZ - 1)], w_send.at[0]),
        (go_all.at[pl.ds(0, 6), 1, my_half, :], go_send.at[0]),
        (rows_sent, ring_send.at[0]),
        (go_all.at[:, pl.ds(1, NX - 1), my_half, :], share_send.at[0]),
        (tail_ref, halo_send.at[0]),
        (x_states.at[0, pl.ds(0, NX - 1)], x_send.at[0]),
        (x_states.at[1, pl.ds(0, NX - 1)], x_send.at[1]),
        (z_states.at[0, pl.ds(0, NZ - 1)], z_send.at[0]),
        (gated_ref.at[pl.ds(0, NX - 1)], gated_send.at[0]),
        (give_ref.at[pl.ds(1, NX - 1)], give_send.at[0]),
        (pair_ref, pair_send.at[0]),
        (chain_ref.at[pl.ds(1, NY - 1)], y_send.at[0]),
    ]:
        remote(sent, sent, semaphore, own_sem.at[0], partner).wait_send()
    for piece in range(4):

        @pl.when(jnp.logical_not(stays(piece)))
        def _(piece=piece):
            to_owner(piece, 0, 0, 0).wait_send()

    write_gf.wait()
    write_out.wait()


def per_device(featurized, short_taps, residues, decay_rates, w_out, grad_out):
    operands = (featurized.transpose(1, 0, 2), short_taps, decay_rates.T, residues.T, w_out, grad_out)
    hbm = pl.BlockSpec(memory_space=pl.ANY)
    dma, V = pltpu.SemaphoreType.DMA, pltpu.VMEM
    block, gf = pl.pallas_call(
        kernel,
        out_shape=(jax.ShapeDtypeStruct((T, 2 * C), BF16), jax.ShapeDtypeStruct((3, T, C), BF16)),
        in_specs=[hbm] * 6,
        out_specs=(hbm, hbm),
        scratch_shapes=[
            V((3, T, C), BF16),
            V((3, 3, C), F32),
            V((MODES, C), F32),
            V((MODES, C), F32),
            V((NZ, C, C), BF16),
            V((NZ, NX, T, C), BF16),
            V((MODES, T, C), F32),
            V((MODES, T, C), F32),
            V((T, C), F32),
            V((8, 2 * T, C), F32),
            V((6, T, C), F32),
            V((T, C), F32),
            V((T, C), F32),
            V((T, C), F32),
            V((2, 8, C), F32),
            V((2, 8, C), F32),
            V((8, MODES, C), F32),
            V((2, NX, MODES, C), F32),
            V((2, NZ, MODES, C), F32),
            V((MODES, C), F32),
            V((NX, T, C), BF16),
            V((NX, T, C), F32),
            V((NX, T, C), BF16),
            V((NX, T, C), BF16),
            V((NY, NX, T, C), BF16),
            V((NY, 2, T, C), BF16),
            V((NY, 4, H, C), BF16),
            V((2, NY, 4, H, C), BF16),
            V((3, 2, T, C), BF16),
            V((T, 2 * C), BF16),
            V((3, T, C), BF16),
            dma((8,)), dma((1,)), dma((2, 4, PIECES)), dma((1,)), dma((2,)),
            dma((2,)), dma((2, NX)), dma((1,)), dma((NZ,)),
            dma((1,)), dma((2,)), dma((1,)), dma((2, 3)), dma((1,)), dma((1,)),
            dma((1,)), dma((NX,)), dma((1,)), dma((1,)), dma((1,)), dma((NY,)),
            dma((1,)), dma((4,)), dma((2, 3, 4)), dma((3, 2, 2)),
        ],
        compiler_params=pltpu.CompilerParams(
            collective_id=0, has_side_effects=True, vmem_limit_bytes=48000000
        ),
    )(*(pltpu.with_memory_space_constraint(v, pltpu.HBM) for v in operands))
    return (block, gf.transpose(1, 0, 2))


def solution(mesh):
    placed = (
        P("ctx", None, "fsdp"),
        P(None, None, "fsdp"),
        P("fsdp", None),
        P("fsdp", None),
        P("fsdp", "ctx"),
        P("ctx", None),
    )
    return jax.shard_map(
        per_device,
        mesh=mesh,
        in_specs=placed,
        out_specs=(P("ctx", "fsdp"), P("ctx", None, "fsdp")),
        check_vma=False,
    )
```

```python
import jax
import jax.numpy as jnp
from jax import lax
from jax.experimental import pallas as pl
from jax.experimental.pallas import tpu as pltpu
from jax.sharding import PartitionSpec as P

T = 128
C = 256
MODES = 16
NZ, NX, NY = 8, 4, 8
F32 = jnp.float32
BF16 = jnp.bfloat16
MESH = pl.DeviceIdType.MESH

H = T // 2
PIECES = 4
CHAIN_UP = {0: (4, 3, 2, 1), 1: (4, 3, 2, 1), 2: (3, 2, 1), 3: (3, 2, 1)}
CHAIN_DOWN = {0: (5, 6, 7), 1: (5, 6, 7), 2: (4, 5, 6, 7), 3: (4, 5, 6, 7)}
PROJECT_ORDER = (4, 3, 5, 2, 6, 1, 7, 0)


def kernel(
    feats_in, taps_in, a_in, res_in, w_ref, go_ref, out_ref, gf_ref,
    feats_ref, taps_ref, a_ref, res_ref, w_all, go_all, near, far, h_ref, pad_ref, mix_ref, conv_ref, gg_ref,
    acc_ref, tail_ref, halo_ref, state_ref, x_states, z_states, weight_ref, gated_ref, part_ref, give_ref, take_ref,
    mine_ref, pair_ref, chain_ref, land_ref, final_ref,
    own_sem, w_send, w_recv, halo_send, halo_recv, x_send, x_recv, z_send, z_recv,
    go_send, go_recv, ring_send, ring_recv, share_send, share_recv,
    gated_send, gated_recv, give_send, give_recv, pair_send, pair_recv, y_send, own_send, y_recv, final_recv,
):
    f, k = lax.axis_index("fsdp"), lax.axis_index("ctx")
    y, core = f // 2, f % 2
    z, x = k // NX, k % NX

    def at(dz, dx):
        return lax.rem(z + dz + NZ, NZ) * NX + lax.rem(x + dx + NX, NX)

    def ctx(index):
        return {"fsdp": f, "ctx": index}

    def remote(src, dst, send, recv, device):
        return pltpu.make_async_remote_copy(
            src_ref=src, dst_ref=dst, send_sem=send, recv_sem=recv, device_id=device, device_id_type=MESH
        )

    following, previous = lax.rem(k + 1, NZ * NX), lax.rem(k + NZ * NX - 1, NZ * NX)
    partner = {"fsdp": y * 2 + 1 - core, "ctx": k}
    my_half = pl.ds(core * H, H)

    loads = [
        pltpu.make_async_copy(src, dst, own_sem.at[i])
        for i, (src, dst) in enumerate(
            [(feats_in, feats_ref), (a_in, a_ref), (res_in, res_ref), (taps_in, taps_ref), (w_ref, w_all.at[z])]
        )
    ]
    for load in loads:
        load.start()

    barrier = pltpu.get_barrier_semaphore()
    greeted = [{"fsdp": y * 2 + 1 - core, "ctx": at(0, d)} for d in range(NX)] + [ctx(at(0, d)) for d in range(1, NX)]
    greeted += [ctx(at(d, 0)) for d in range(1, NZ)] + [ctx(following), ctx(previous)]
    greeted += [{"fsdp": lax.rem(y + d, NY) * 2 + core, "ctx": k} for d in (1, NY - 1)]
    greeted += [
        {"fsdp": lax.rem(y + d, NY) * 2 + x // 2, "ctx": z * NX + core * 2 + i} for d in (1, NY - 1) for i in range(2)
    ]
    for device in greeted:
        pl.semaphore_signal(barrier, inc=1, device_id=device, device_id_type=MESH)
    pl.semaphore_wait(barrier, len(greeted))

    def go(copy):
        copy.start()

    def w_copy(distance, up, piece):
        block = lax.rem(z + (1 - distance if up else distance - 1) + NZ, NZ)
        span = pl.ds(piece * (C // PIECES), C // PIECES)
        src = w_ref.at[span, :] if distance == 1 else w_all.at[block, span, :]
        slot = (0 if up else 1), distance - 1, piece
        return remote(src, w_all.at[block, span, :], w_send.at[0], w_recv.at[slot], ctx(at(1 if up else -1, 0)))

    def farthest(up, piece):
        return (piece < PIECES // 2) == up

    def w_relay(distance, pieces=range(PIECES)):
        for i in pieces:
            for up in (True, False):
                piece = i if up else PIECES - 1 - i
                if distance == NZ // 2 and not farthest(up, piece):
                    continue
                span = pl.ds(piece * (C // PIECES), C // PIECES)
                block = w_all.at[lax.rem(z + (-distance if up else distance) + NZ, NZ), span, :]
                slot = (0 if up else 1), distance - 1, piece
                remote(block, block, w_send.at[0], w_recv.at[slot], partner).wait_recv()
                if distance + 1 < NZ // 2 or (distance + 1 == NZ // 2 and farthest(up, piece)):
                    go(w_copy(distance + 1, up, piece))

    def strip_row(dy, i):
        return lax.rem(y + dy + NY, NY // 2) + i * (NY // 2)

    def go_out(i):
        row = strip_row(0, i)
        for d in (2, 1, 3):
            strip = go_ref.at[my_half, pl.ds(pl.multiple_of((row * NX + lax.rem(x + d, NX)) * C, C), C)]
            go(remote(strip, go_all.at[row, d, my_half, :], go_send.at[0], go_recv.at[i], ctx(at(0, d))))

    def own_rows():
        for row in range(NZ):
            columns = pl.ds(pl.multiple_of((row * NX + x) * C, C), C)
            pltpu.make_async_copy(go_ref.at[:, columns], go_all.at[row, 0], own_sem.at[5]).start()

    def strips(dy, i, half):
        return go_all.at[strip_row(dy, i), pl.ds(1, NX - 1), pl.ds(half * H, H), :]

    def go_copy(dy, up, i):
        region = strips(dy, i, core)
        slot = (0 if up else 1), (i if dy == 0 else 2)
        to = {"fsdp": lax.rem(y + (1 if up else NY - 1), NY) * 2 + core, "ctx": k}
        return remote(region, region, ring_send.at[0], ring_recv.at[slot], to)

    def share_copy(dy, i, half):
        region = strips(dy, i, half)
        return remote(region, region, share_send.at[0], share_recv.at[dy + 1, i], partner)

    def go_first(i):
        landed = strips(0, i, core)
        remote(landed, landed, go_send.at[0], go_recv.at[i], partner).wait_recv()
        go(go_copy(0, True, i))
        go(go_copy(0, False, i))
        go(share_copy(0, i, core))

    def go_near(i):
        for up in (True, False):
            dy = -1 if up else 1
            region = strips(dy, i, core)
            slot = (0 if up else 1), i
            remote(region, region, ring_send.at[0], ring_recv.at[slot], partner).wait_recv()
            if i == (0 if up else 1):
                go(go_copy(dy, up, i))
            go(share_copy(dy, i, core))

    def go_far():
        for up in (True, False):
            i = 0 if up else 1
            region = strips(2, i, core)
            slot = (0 if up else 1), 2
            remote(region, region, ring_send.at[0], ring_recv.at[slot], partner).wait_recv()
            go(share_copy(2, i, core))

    def from_x(dx):
        return lax.rem(x + dx + NX, NX)

    rows = lax.broadcasted_iota(jnp.int32, (T, 1), 0)
    steps = rows.astype(F32)

    def halo_copy(which, device):
        return remote(
            tail_ref.at[which], halo_ref.at[which], halo_send.at[0], halo_recv.at[which], ctx(device)
        )

    def send_tail():
        for j in range(3):
            last = feats_ref[j, T - 16 :, :].astype(F32)
            tail_ref[0, 2 * j : 2 * j + 2, :] = last[14:16]
        copy = halo_copy(0, following)
        copy.start()

    def tables(low):
        def body(n, c):
            a = a_ref[pl.ds(n, 1), :]
            scale = res_ref[pl.ds(n, 1), :] * jnp.sqrt(a)
            weight_ref[pl.ds(n, 1), :] = scale
            e = jnp.exp(-a * steps)
            near[n] = e
            far[n] = jnp.exp(-a * (T - 1 - steps))
            h_ref[...] += scale * e
            return c

        lax.fori_loop(low, low + 4, body, 0)

    def clear():
        h_ref[...] = jnp.zeros_like(h_ref)

    def end_state(table, signal_ref, which):
        def body(n, c):
            state_ref[which, pl.ds(n, 1), :] = jnp.sum(table[n] * signal_ref[...], axis=0, keepdims=True)
            return c

        lax.fori_loop(0, MODES, body, 0)

    def send_x(which):
        for d in range(1, NX):
            copy = remote(
                state_ref.at[which], x_states.at[which, x], x_send.at[which], x_recv.at[which, x], ctx(at(0, d))
            )
            copy.start()

    def mix():
        halo_copy(0, following).wait_recv()
        for j in range(3):
            now = feats_ref[j].astype(F32)
            one = jnp.where(k > 0, halo_ref[0, 2 * j + 1 : 2 * j + 2, :], 0.0)
            two = jnp.where(k > 0, halo_ref[0, 2 * j : 2 * j + 1, :], 0.0)
            back1 = jnp.where(rows == 0, one, pltpu.roll(now, 1, 0))
            back2 = jnp.where(rows == 0, two, jnp.where(rows == 1, one, pltpu.roll(now, 2, 0)))
            mix_ref[j] = (
                taps_ref[0, j : j + 1, :] * now + taps_ref[1, j : j + 1, :] * back1 + taps_ref[2, j : j + 1, :] * back2
            )
        acc_ref[...] = mix_ref[1] * mix_ref[2]

    def forward_send():
        end_state(far, acc_ref, 0)
        send_x(0)

    def shift_copies(which, low):
        value = acc_ref[...]
        for r in range(low, low + 4):
            if which == 0:
                pad_ref[r, :T, :] = jnp.zeros_like(value)
                pad_ref[r, T:, :] = jnp.where(rows >= r, pltpu.roll(value, r, 0), 0.0) if r else value
            else:
                pad_ref[r, T:, :] = jnp.zeros_like(value)
                pad_ref[r, :T, :] = jnp.where(rows < T - r, pltpu.roll(value, T - r, 0), 0.0) if r else value

    def local_taps(which, low, high, dst, begin):
        def body(q, total):
            for r in range(8):
                start = pl.multiple_of((T - 8 * q) if which == 0 else 8 * q, 8)
                total = total + h_ref[pl.ds(8 * q + r, 1), :] * pad_ref[r, pl.ds(start, T), :]
            return total

        first = jnp.zeros((T, C), F32) if begin else dst[...]
        dst[...] = lax.fori_loop(low, high, body, first)

    def combine_x(which):
        x_states[which, x] = state_ref[which]
        for d in range(1, NX):
            other = lax.rem(x + d, NX)
            remote(
                state_ref.at[which], x_states.at[which, other], x_send.at[which], x_recv.at[which, other], ctx(k)
            ).wait_recv()
        a = a_ref[...]
        entering, total = jnp.zeros_like(a), jnp.zeros_like(a)
        for j in range(NX):
            gap = (x - 1 - j) if which == 0 else (j - x - 1)
            reach = (NX - 1 - j) if which == 0 else j
            decay = jnp.exp(-a * (T * jnp.maximum(gap, 0)).astype(F32))
            state = x_states[which, j]
            entering = entering + jnp.where(gap >= 0, decay * state, 0.0)
            total = total + jnp.exp(-a * float(T * reach)) * state
        state_ref[2 + which] = entering
        state_ref[4 + which] = total
        for d in range(1, NZ):
            to = lax.rem(z + d, NZ)

            @pl.when((to > z) if which == 0 else (to < z))
            def _(d=d):
                z_copy(which, d).start()

    def z_copy(which, d):
        return remote(
            state_ref.at[4 + which], z_states.at[which, z], z_send.at[0], z_recv.at[z], ctx(at(d, 0))
        )

    def combine_z(which):
        a = a_ref[...]
        state_ref[6] = jnp.zeros_like(a)
        for d in range(1, NZ):
            other = lax.rem(z + d, NZ)

            @pl.when((other < z) if which == 0 else (other > z))
            def _(d=d, other=other):
                remote(
                    state_ref.at[4 + which],
                    z_states.at[which, other],
                    z_send.at[0],
                    z_recv.at[other],
                    ctx(at(d, 0)),
                ).wait_recv()
                gap = (z - 1 - other) if which == 0 else (other - z - 1)
                state_ref[6] += jnp.exp(-a * (NX * T * gap).astype(F32)) * z_states[which, other]

        inside = x if which == 0 else NX - 1 - x
        entering = state_ref[2 + which] + jnp.exp(-a * (T * inside).astype(F32)) * state_ref[6]
        state_ref[7] = weight_ref[...] * jnp.exp(-a) * entering

    def boundary(table, dst):
        def body(n, total):
            return total + table[n] * state_ref[7, pl.ds(n, 1), :]

        dst[...] = lax.fori_loop(0, MODES, body, dst[...])

    def gate():
        combine_z(0)
        boundary(near, conv_ref)
        gated_ref[x] = (mix_ref[0] * conv_ref[...]).astype(BF16)
        for d in range(1, NX):
            go(remote(gated_ref.at[x], gated_ref.at[x], gated_send.at[0], gated_recv.at[d], ctx(at(0, d))))

    def transpose_project(dy):
        for i in range(2):
            share_copy(dy, i, 1 - core).wait_recv()

        def body(i, c):
            row = strip_row(dy, i)
            part = lax.dot_general(
                go_all[row].reshape(NX * T, C), w_all[row], (((1,), (1,)), ((), ())), preferred_element_type=F32
            )
            part_ref[...] += part.reshape(NX, T, C)
            return c

        lax.fori_loop(0, 2, body, 0)

    def give():
        for d in range(1, NX):
            give_ref[d] = part_ref[d].astype(BF16)
            go(remote(give_ref.at[d], take_ref.at[d], give_send.at[0], give_recv.at[0], ctx(at(0, -d))))

    def sum_gated():
        gg_ref[...] = part_ref[0]
        taken = take_ref.at[pl.ds(1, NX - 1)]
        remote(taken, taken, give_send.at[0], give_recv.at[0], partner).wait_recv()
        for d in range(1, NX):
            gg_ref[...] += take_ref[d].astype(F32)

    def gated_arrived():
        for d in range(1, NX):
            source = from_x(-d)
            remote(
                gated_ref.at[source], gated_ref.at[source], gated_send.at[0], gated_recv.at[d], partner
            ).wait_recv()

    def target(e):
        return lax.rem(y + e, NY)

    def pair_copy(e):
        row = target(e)
        return remote(
            mine_ref.at[row, pl.ds((1 - core) * 2, 2)], pair_ref.at[row], pair_send.at[0], pair_recv.at[e], partner
        )

    def project(e):
        row = target(e)
        part = jnp.dot(gated_ref[...].reshape(NX * T, C), w_all[row], preferred_element_type=F32)
        mine_ref[row] = part.astype(BF16).reshape(NX, T, C)
        go(pair_copy(e))

    paired = set()

    def rows_of(piece):
        return pl.ds(piece % 2 * H, H)

    def term(e, piece):
        if e not in paired:
            pair_copy(e).wait_recv()
            paired.add(e)
        row, span = target(e), rows_of(piece)
        mine = mine_ref[row, core * 2 + piece // 2, span, :]
        return mine.astype(F32) + pair_ref[row, piece // 2, span, :].astype(F32)

    owner = x // 2

    def owner_of(piece, dy):
        return {"fsdp": lax.rem(y + dy + NY, NY) * 2 + owner, "ctx": z * NX + core * 2 + piece // 2}

    def to_owner(piece, kind, e, dy):
        there = kind, x % 2, rows_of(piece), slice(None)
        return remote(
            chain_ref.at[e, piece],
            final_ref.at[there],
            y_send.at[0] if kind else own_send.at[piece],
            final_recv.at[kind, x % 2, piece % 2],
            owner_of(piece, dy),
        )

    def chain(up, e, piece):
        total = term(e, piece)
        if e != (CHAIN_UP if up else CHAIN_DOWN)[piece][0]:
            slot = (0 if up else 1), e, piece
            landed = land_ref.at[slot]
            remote(landed, landed, y_send.at[0], y_recv.at[slot[0], e - (1 if up else 5), piece], partner).wait_recv()
            total = total + land_ref[slot].astype(F32)
        chain_ref[e, piece] = total.astype(BF16)
        if e == (1 if up else NY - 1):
            go(to_owner(piece, 1 if up else 2, e, 1 if up else -1))
            return
        there = (0 if up else 1), (e - 1 if up else e + 1), piece
        to = {"fsdp": lax.rem(y + (1 if up else NY - 1), NY) * 2 + core, "ctx": k}
        go(remote(chain_ref.at[e, piece], land_ref.at[there], y_send.at[0], y_recv.at[there[0], there[1] - (1 if up else 5), piece], to))

    def stage(n):
        for i in range(2):
            chain(True, 4 - n, i)
            chain(False, 4 + n, 2 + i)
        if n < 3:
            for i in range(2):
                chain(True, 3 - n, 2 + i)
                chain(False, 5 + n, i)

    def stays(piece):
        return jnp.logical_and(owner == core, x % 2 == piece // 2)

    def own_term():
        for piece in range(4):
            chain_ref[0, piece] = term(0, piece).astype(BF16)

            @pl.when(jnp.logical_not(stays(piece)))
            def _(piece=piece):
                to_owner(piece, 0, 0, 0).start()

    def collect():
        for half in range(2):
            local = jnp.logical_and(owner == core, x % 2 == half)
            for part in range(2):
                span, columns = rows_of(part), pl.ds(half * C, C)

                @pl.when(local)
                def _(half=half, part=part, span=span):
                    final_ref[0, half, span, :] = chain_ref[0, 2 * half + part]

                for kind in range(3):
                    landed = final_ref.at[kind, half, span, :]
                    arrived = remote(landed, landed, y_send.at[0], final_recv.at[kind, half, part], partner)
                    if kind:
                        arrived.wait_recv()
                    else:
                        pl.when(jnp.logical_not(local))(arrived.wait_recv)
                total = final_ref[0, half, span, :].astype(F32) + final_ref[1, half, span, :].astype(F32)
                out_ref[span, columns] = (total + final_ref[2, half, span, :].astype(F32)).astype(BF16)

    for load in loads[:4]:
        load.wait()
    send_tail()
    for piece in range(PIECES):
        go(w_copy(1, True, piece))
        go(w_copy(1, False, PIECES - 1 - piece))
    go_out(0)
    clear()
    for i in range(4):
        tables(4 * i)
    go_out(1)
    own_rows()
    mix()
    forward_send()
    w_relay(1)
    go_first(0)
    shift_copies(0, 0)
    shift_copies(0, 4)
    local_taps(0, 0, 8, conv_ref, True)
    go_first(1)
    combine_x(0)
    w_relay(2)
    local_taps(0, 8, 16, conv_ref, False)
    go_near(0)
    w_relay(3, range(PIECES // 2))
    go_near(1)
    w_relay(3, range(PIECES // 2, PIECES))
    gate()
    w_relay(4)
    loads[4].wait()
    pltpu.make_async_copy(go_all.at[:, 0], go_all.at[:, 0], own_sem.at[5]).wait()
    part_ref[...] = jnp.zeros_like(part_ref)
    for dy in (0, -1, 1):
        transpose_project(dy)
    go_far()
    transpose_project(2)
    give()
    gated_arrived()
    for e in PROJECT_ORDER[:5]:
        project(e)
    stage(0)
    for e in PROJECT_ORDER[5:]:
        project(e)
    sum_gated()
    acc_ref[...] = gg_ref[...] * mix_ref[0]
    end_state(near, acc_ref, 1)
    send_x(1)
    stage(1)
    own_term()
    combine_x(1)
    gg_ref[...] = gg_ref[...] * conv_ref[...]
    shift_copies(1, 0)
    shift_copies(1, 4)
    local_taps(1, 0, 8, acc_ref, True)
    stage(2)
    local_taps(1, 8, 16, acc_ref, False)
    combine_z(1)
    boundary(far, acc_ref)
    for j in range(3):
        value = gg_ref[...] if j == 0 else acc_ref[...] * mix_ref[3 - j]
        mix_ref[3 + j] = value
        tail_ref[1, 2 * j : 2 * j + 2, :] = value[0:2]
    go(halo_copy(1, previous))
    stage(3)
    halo_copy(1, previous).wait_recv()
    inner = k < NZ * NX - 1
    for j in range(3):
        now = mix_ref[3 + j]
        one = jnp.where(inner, halo_ref[1, 2 * j : 2 * j + 1, :], 0.0)
        two = jnp.where(inner, halo_ref[1, 2 * j + 1 : 2 * j + 2, :], 0.0)
        ahead1 = jnp.where(rows == T - 1, one, pltpu.roll(now, T - 1, 0))
        ahead2 = jnp.where(rows == T - 1, two, jnp.where(rows == T - 2, one, pltpu.roll(now, T - 2, 0)))
        gf_ref[j] = (
            taps_ref[0, j : j + 1, :] * now + taps_ref[1, j : j + 1, :] * ahead1 + taps_ref[2, j : j + 1, :] * ahead2
        ).astype(BF16)
    collect()
    rows_sent = go_all.at[pl.ds(0, 6), pl.ds(1, NX - 1), my_half, :]
    for sent, semaphore in [
        (w_all.at[pl.ds(0, NZ - 1)], w_send.at[0]),
        (go_all.at[pl.ds(0, 6), 1, my_half, :], go_send.at[0]),
        (rows_sent, ring_send.at[0]),
        (go_all.at[:, pl.ds(1, NX - 1), my_half, :], share_send.at[0]),
        (tail_ref, halo_send.at[0]),
        (x_states.at[0, pl.ds(0, NX - 1)], x_send.at[0]),
        (x_states.at[1, pl.ds(0, NX - 1)], x_send.at[1]),
        (z_states.at[0, pl.ds(0, NZ - 1)], z_send.at[0]),
        (gated_ref.at[pl.ds(0, NX - 1)], gated_send.at[0]),
        (give_ref.at[pl.ds(1, NX - 1)], give_send.at[0]),
        (pair_ref, pair_send.at[0]),
        (chain_ref.at[pl.ds(1, NY - 1)], y_send.at[0]),
    ]:
        remote(sent, sent, semaphore, own_sem.at[0], partner).wait_send()
    for piece in range(4):

        @pl.when(jnp.logical_not(stays(piece)))
        def _(piece=piece):
            to_owner(piece, 0, 0, 0).wait_send()


def per_device(featurized, short_taps, residues, decay_rates, w_out, grad_out):
    operands = (featurized.transpose(1, 0, 2), short_taps, decay_rates.T, residues.T, w_out, grad_out)
    hbm = pl.BlockSpec(memory_space=pl.ANY)
    dma, V = pltpu.SemaphoreType.DMA, pltpu.VMEM
    block, gf = pl.pallas_call(
        kernel,
        out_shape=(jax.ShapeDtypeStruct((T, 2 * C), BF16), jax.ShapeDtypeStruct((3, T, C), BF16)),
        in_specs=[hbm] * 6,
        out_specs=(pl.BlockSpec(memory_space=pltpu.VMEM),) * 2,
        scratch_shapes=[
            V((3, T, C), BF16),
            V((3, 3, C), F32),
            V((MODES, C), F32),
            V((MODES, C), F32),
            V((NZ, C, C), BF16),
            V((NZ, NX, T, C), BF16),
            V((MODES, T, C), F32),
            V((MODES, T, C), F32),
            V((T, C), F32),
            V((8, 2 * T, C), F32),
            V((6, T, C), F32),
            V((T, C), F32),
            V((T, C), F32),
            V((T, C), F32),
            V((2, 8, C), F32),
            V((2, 8, C), F32),
            V((8, MODES, C), F32),
            V((2, NX, MODES, C), F32),
            V((2, NZ, MODES, C), F32),
            V((MODES, C), F32),
            V((NX, T, C), BF16),
            V((NX, T, C), F32),
            V((NX, T, C), BF16),
            V((NX, T, C), BF16),
            V((NY, NX, T, C), BF16),
            V((NY, 2, T, C), BF16),
            V((NY, 4, H, C), BF16),
            V((2, NY, 4, H, C), BF16),
            V((3, 2, T, C), BF16),
            dma((6,)), dma((1,)), dma((2, 4, PIECES)), dma((1,)), dma((2,)),
            dma((2,)), dma((2, NX)), dma((1,)), dma((NZ,)),
            dma((1,)), dma((2,)), dma((1,)), dma((2, 3)), dma((1,)), dma((4, 2)),
            dma((1,)), dma((NX,)), dma((1,)), dma((1,)), dma((1,)), dma((NY,)),
            dma((1,)), dma((4,)), dma((2, 3, 4)), dma((3, 2, 2)),
        ],
        compiler_params=pltpu.CompilerParams(
            collective_id=0, has_side_effects=True, vmem_limit_bytes=48000000
        ),
    )(*(pltpu.with_memory_space_constraint(v, pltpu.HBM) for v in operands))
    return (block, gf.transpose(1, 0, 2))


def solution(mesh):
    placed = (
        P("ctx", None, "fsdp"),
        P(None, None, "fsdp"),
        P("fsdp", None),
        P("fsdp", None),
        P("fsdp", "ctx"),
        P("ctx", None),
    )
    return jax.shard_map(
        per_device,
        mesh=mesh,
        in_specs=placed,
        out_specs=(P("ctx", "fsdp"), P("ctx", None, "fsdp")),
        check_vma=False,
    )
```

```python
import jax
import jax.numpy as jnp
from jax import lax
from jax.experimental import pallas as pl
from jax.experimental.pallas import tpu as pltpu
from jax.sharding import PartitionSpec as P

T = 128
C = 256
MODES = 16
NZ, NX, NY = 8, 4, 8
F32 = jnp.float32
BF16 = jnp.bfloat16
MESH = pl.DeviceIdType.MESH

H = T // 2
PIECES = 4
CHAIN_UP = {0: (4, 3, 2, 1), 1: (4, 3, 2, 1), 2: (3, 2, 1), 3: (3, 2, 1)}
CHAIN_DOWN = {0: (5, 6, 7), 1: (5, 6, 7), 2: (4, 5, 6, 7), 3: (4, 5, 6, 7)}
PROJECT_ORDER = (4, 3, 5, 2, 6, 1, 7, 0)


def kernel(
    feats_in, taps_in, a_in, res_in, w_ref, go_ref, out_ref, gf_ref,
    feats_ref, taps_ref, a_ref, res_ref, w_all, go_all, near, far, h_ref, pad_ref, mix_ref, conv_ref, gg_ref,
    acc_ref, tail_ref, halo_ref, state_ref, x_states, z_states, weight_ref, gated_ref, part_ref, give_ref, take_ref,
    mine_ref, pair_ref, chain_ref, land_ref, final_ref,
    own_sem, w_send, w_recv, halo_send, halo_recv, x_send, x_recv, z_send, z_recv,
    go_send, go_recv, ring_send, ring_recv, share_send, share_recv,
    gated_send, gated_recv, give_send, give_recv, pair_send, pair_recv, y_send, own_send, y_recv, final_recv,
):
    f, k = lax.axis_index("fsdp"), lax.axis_index("ctx")
    y, core = f // 2, f % 2
    z, x = k // NX, k % NX

    def at(dz, dx):
        return lax.rem(z + dz + NZ, NZ) * NX + lax.rem(x + dx + NX, NX)

    def ctx(index):
        return {"fsdp": f, "ctx": index}

    def remote(src, dst, send, recv, device):
        return pltpu.make_async_remote_copy(
            src_ref=src, dst_ref=dst, send_sem=send, recv_sem=recv, device_id=device, device_id_type=MESH
        )

    following, previous = lax.rem(k + 1, NZ * NX), lax.rem(k + NZ * NX - 1, NZ * NX)
    partner = {"fsdp": y * 2 + 1 - core, "ctx": k}
    my_half = pl.ds(core * H, H)

    loads = [
        pltpu.make_async_copy(src, dst, own_sem.at[i])
        for i, (src, dst) in enumerate(
            [(feats_in, feats_ref), (a_in, a_ref), (res_in, res_ref), (taps_in, taps_ref), (w_ref, w_all.at[z])]
        )
    ]
    for load in loads:
        load.start()

    barrier = pltpu.get_barrier_semaphore()
    greeted = [{"fsdp": y * 2 + 1 - core, "ctx": at(0, d)} for d in range(NX)] + [ctx(at(0, d)) for d in range(1, NX)]
    greeted += [ctx(at(d, 0)) for d in range(1, NZ)] + [ctx(following), ctx(previous)]
    greeted += [{"fsdp": lax.rem(y + d, NY) * 2 + core, "ctx": k} for d in (1, NY - 1)]
    greeted += [
        {"fsdp": lax.rem(y + d, NY) * 2 + x // 2, "ctx": z * NX + core * 2 + i} for d in (1, NY - 1) for i in range(2)
    ]
    for device in greeted:
        pl.semaphore_signal(barrier, inc=1, device_id=device, device_id_type=MESH)
    pl.semaphore_wait(barrier, len(greeted))

    def go(copy):
        copy.start()

    def w_copy(distance, up, piece):
        block = lax.rem(z + (1 - distance if up else distance - 1) + NZ, NZ)
        span = pl.ds(piece * (C // PIECES), C // PIECES)
        src = w_ref.at[span, :] if distance == 1 else w_all.at[block, span, :]
        slot = (0 if up else 1), distance - 1, piece
        return remote(src, w_all.at[block, span, :], w_send.at[0], w_recv.at[slot], ctx(at(1 if up else -1, 0)))

    def farthest(up, piece):
        return (piece < PIECES // 2) == up

    def w_relay(distance, pieces=range(PIECES)):
        for i in pieces:
            for up in (True, False):
                piece = i if up else PIECES - 1 - i
                if distance == NZ // 2 and not farthest(up, piece):
                    continue
                span = pl.ds(piece * (C // PIECES), C // PIECES)
                block = w_all.at[lax.rem(z + (-distance if up else distance) + NZ, NZ), span, :]
                slot = (0 if up else 1), distance - 1, piece
                remote(block, block, w_send.at[0], w_recv.at[slot], partner).wait_recv()
                if distance + 1 < NZ // 2 or (distance + 1 == NZ // 2 and farthest(up, piece)):
                    go(w_copy(distance + 1, up, piece))

    def strip_row(dy, i):
        return lax.rem(y + dy + NY, NY // 2) + i * (NY // 2)

    def go_out(i):
        row = strip_row(0, i)
        for d in (2, 1, 3):
            strip = go_ref.at[my_half, pl.ds(pl.multiple_of((row * NX + lax.rem(x + d, NX)) * C, C), C)]
            go(remote(strip, go_all.at[row, d, my_half, :], go_send.at[0], go_recv.at[i], ctx(at(0, d))))

    def own_rows():
        for row in range(NZ):
            columns = pl.ds(pl.multiple_of((row * NX + x) * C, C), C)
            pltpu.make_async_copy(go_ref.at[:, columns], go_all.at[row, 0], own_sem.at[5]).start()

    def strips(dy, i, half):
        return go_all.at[strip_row(dy, i), pl.ds(1, NX - 1), pl.ds(half * H, H), :]

    def go_copy(dy, up, i):
        region = strips(dy, i, core)
        slot = (0 if up else 1), (i if dy == 0 else 2)
        to = {"fsdp": lax.rem(y + (1 if up else NY - 1), NY) * 2 + core, "ctx": k}
        return remote(region, region, ring_send.at[0], ring_recv.at[slot], to)

    def share_copy(dy, i, half):
        region = strips(dy, i, half)
        return remote(region, region, share_send.at[0], share_recv.at[dy + 1, i], partner)

    def go_first(i):
        landed = strips(0, i, core)
        remote(landed, landed, go_send.at[0], go_recv.at[i], partner).wait_recv()
        go(go_copy(0, True, i))
        go(go_copy(0, False, i))
        go(share_copy(0, i, core))

    def go_near(i):
        for up in (True, False):
            dy = -1 if up else 1
            region = strips(dy, i, core)
            slot = (0 if up else 1), i
            remote(region, region, ring_send.at[0], ring_recv.at[slot], partner).wait_recv()
            if i == (0 if up else 1):
                go(go_copy(dy, up, i))
            go(share_copy(dy, i, core))

    def go_far():
        for up in (True, False):
            i = 0 if up else 1
            region = strips(2, i, core)
            slot = (0 if up else 1), 2
            remote(region, region, ring_send.at[0], ring_recv.at[slot], partner).wait_recv()
            go(share_copy(2, i, core))

    def from_x(dx):
        return lax.rem(x + dx + NX, NX)

    rows = lax.broadcasted_iota(jnp.int32, (T, 1), 0)
    steps = rows.astype(F32)

    def halo_copy(which, device):
        return remote(
            tail_ref.at[which], halo_ref.at[which], halo_send.at[0], halo_recv.at[which], ctx(device)
        )

    def send_tail():
        for j in range(3):
            last = feats_ref[j, T - 16 :, :].astype(F32)
            tail_ref[0, 2 * j : 2 * j + 2, :] = last[14:16]
        copy = halo_copy(0, following)
        copy.start()

    def tables(low):
        def body(n, c):
            a = a_ref[pl.ds(n, 1), :]
            scale = res_ref[pl.ds(n, 1), :] * jnp.sqrt(a)
            weight_ref[pl.ds(n, 1), :] = scale
            e = jnp.exp(-a * steps)
            near[n] = e
            far[n] = jnp.exp(-a * (T - 1 - steps))
            h_ref[...] += scale * e
            return c

        lax.fori_loop(low, low + 4, body, 0)

    def clear():
        h_ref[...] = jnp.zeros_like(h_ref)

    def end_state(table, signal_ref, which):
        def body(n, c):
            state_ref[which, pl.ds(n, 1), :] = jnp.sum(table[n] * signal_ref[...], axis=0, keepdims=True)
            return c

        lax.fori_loop(0, MODES, body, 0)

    def send_x(which):
        for d in (2, 1, 3):
            copy = remote(
                state_ref.at[which], x_states.at[which, x], x_send.at[which], x_recv.at[which, x], ctx(at(0, d))
            )
            copy.start()

    def mix():
        halo_copy(0, following).wait_recv()
        for j in range(3):
            now = feats_ref[j].astype(F32)
            one = jnp.where(k > 0, halo_ref[0, 2 * j + 1 : 2 * j + 2, :], 0.0)
            two = jnp.where(k > 0, halo_ref[0, 2 * j : 2 * j + 1, :], 0.0)
            back1 = jnp.where(rows == 0, one, pltpu.roll(now, 1, 0))
            back2 = jnp.where(rows == 0, two, jnp.where(rows == 1, one, pltpu.roll(now, 2, 0)))
            mix_ref[j] = (
                taps_ref[0, j : j + 1, :] * now + taps_ref[1, j : j + 1, :] * back1 + taps_ref[2, j : j + 1, :] * back2
            )
        acc_ref[...] = mix_ref[1] * mix_ref[2]

    def forward_send():
        end_state(far, acc_ref, 0)
        send_x(0)

    def shift_copies(which, low):
        value = acc_ref[...]
        for r in range(low, low + 4):
            if which == 0:
                pad_ref[r, :T, :] = jnp.zeros_like(value)
                pad_ref[r, T:, :] = jnp.where(rows >= r, pltpu.roll(value, r, 0), 0.0) if r else value
            else:
                pad_ref[r, T:, :] = jnp.zeros_like(value)
                pad_ref[r, :T, :] = jnp.where(rows < T - r, pltpu.roll(value, T - r, 0), 0.0) if r else value

    def local_taps(which, low, high, dst, begin):
        def body(q, total):
            for r in range(8):
                start = pl.multiple_of((T - 8 * q) if which == 0 else 8 * q, 8)
                total = total + h_ref[pl.ds(8 * q + r, 1), :] * pad_ref[r, pl.ds(start, T), :]
            return total

        first = jnp.zeros((T, C), F32) if begin else dst[...]
        dst[...] = lax.fori_loop(low, high, body, first)

    def combine_x(which):
        x_states[which, x] = state_ref[which]
        for d in range(1, NX):
            other = lax.rem(x + d, NX)
            remote(
                state_ref.at[which], x_states.at[which, other], x_send.at[which], x_recv.at[which, other], ctx(k)
            ).wait_recv()
        a = a_ref[...]
        entering, total = jnp.zeros_like(a), jnp.zeros_like(a)
        for j in range(NX):
            gap = (x - 1 - j) if which == 0 else (j - x - 1)
            reach = (NX - 1 - j) if which == 0 else j
            decay = jnp.exp(-a * (T * jnp.maximum(gap, 0)).astype(F32))
            state = x_states[which, j]
            entering = entering + jnp.where(gap >= 0, decay * state, 0.0)
            total = total + jnp.exp(-a * float(T * reach)) * state
        state_ref[2 + which] = entering
        state_ref[4 + which] = total
        for d in range(1, NZ):
            to = lax.rem(z + d, NZ)

            @pl.when((to > z) if which == 0 else (to < z))
            def _(d=d):
                z_copy(which, d).start()

    def z_copy(which, d):
        return remote(
            state_ref.at[4 + which], z_states.at[which, z], z_send.at[0], z_recv.at[z], ctx(at(d, 0))
        )

    def combine_z(which):
        a = a_ref[...]
        state_ref[6] = jnp.zeros_like(a)
        for d in range(1, NZ):
            other = lax.rem(z + d, NZ)

            @pl.when((other < z) if which == 0 else (other > z))
            def _(d=d, other=other):
                remote(
                    state_ref.at[4 + which],
                    z_states.at[which, other],
                    z_send.at[0],
                    z_recv.at[other],
                    ctx(at(d, 0)),
                ).wait_recv()
                gap = (z - 1 - other) if which == 0 else (other - z - 1)
                state_ref[6] += jnp.exp(-a * (NX * T * gap).astype(F32)) * z_states[which, other]

        inside = x if which == 0 else NX - 1 - x
        entering = state_ref[2 + which] + jnp.exp(-a * (T * inside).astype(F32)) * state_ref[6]
        state_ref[7] = weight_ref[...] * jnp.exp(-a) * entering

    def boundary(table, dst):
        def body(n, total):
            return total + table[n] * state_ref[7, pl.ds(n, 1), :]

        dst[...] = lax.fori_loop(0, MODES, body, dst[...])

    def gate():
        combine_z(0)
        boundary(near, conv_ref)
        gated_ref[x] = (mix_ref[0] * conv_ref[...]).astype(BF16)
        for d in (2, 1, 3):
            go(remote(gated_ref.at[x], gated_ref.at[x], gated_send.at[0], gated_recv.at[d], ctx(at(0, d))))

    def transpose_project(dy):
        for i in range(2):
            share_copy(dy, i, 1 - core).wait_recv()

        def body(i, c):
            row = strip_row(dy, i)
            part = lax.dot_general(
                go_all[row].reshape(NX * T, C), w_all[row], (((1,), (1,)), ((), ())), preferred_element_type=F32
            )
            part_ref[...] += part.reshape(NX, T, C)
            return c

        lax.fori_loop(0, 2, body, 0)

    def give():
        for d in (2, 1, 3):
            give_ref[d] = part_ref[d].astype(BF16)
            go(remote(give_ref.at[d], take_ref.at[d], give_send.at[0], give_recv.at[0], ctx(at(0, -d))))

    def sum_gated():
        gg_ref[...] = part_ref[0]
        taken = take_ref.at[pl.ds(1, NX - 1)]
        remote(taken, taken, give_send.at[0], give_recv.at[0], partner).wait_recv()
        for d in range(1, NX):
            gg_ref[...] += take_ref[d].astype(F32)

    def gated_arrived():
        for d in range(1, NX):
            source = from_x(-d)
            remote(
                gated_ref.at[source], gated_ref.at[source], gated_send.at[0], gated_recv.at[d], partner
            ).wait_recv()

    def target(e):
        return lax.rem(y + e, NY)

    def pair_copy(e):
        row = target(e)
        return remote(
            mine_ref.at[row, pl.ds((1 - core) * 2, 2)], pair_ref.at[row], pair_send.at[0], pair_recv.at[e], partner
        )

    def project(e):
        row = target(e)
        part = jnp.dot(gated_ref[...].reshape(NX * T, C), w_all[row], preferred_element_type=F32)
        mine_ref[row] = part.astype(BF16).reshape(NX, T, C)
        go(pair_copy(e))

    paired = set()

    def rows_of(piece):
        return pl.ds(piece % 2 * H, H)

    def term(e, piece):
        if e not in paired:
            pair_copy(e).wait_recv()
            paired.add(e)
        row, span = target(e), rows_of(piece)
        mine = mine_ref[row, core * 2 + piece // 2, span, :]
        return mine.astype(F32) + pair_ref[row, piece // 2, span, :].astype(F32)

    owner = x // 2

    def owner_of(piece, dy):
        return {"fsdp": lax.rem(y + dy + NY, NY) * 2 + owner, "ctx": z * NX + core * 2 + piece // 2}

    def to_owner(piece, kind, e, dy):
        there = kind, x % 2, rows_of(piece), slice(None)
        return remote(
            chain_ref.at[e, piece],
            final_ref.at[there],
            y_send.at[0] if kind else own_send.at[piece],
            final_recv.at[kind, x % 2, piece % 2],
            owner_of(piece, dy),
        )

    def chain(up, e, piece):
        total = term(e, piece)
        if e != (CHAIN_UP if up else CHAIN_DOWN)[piece][0]:
            slot = (0 if up else 1), e, piece
            landed = land_ref.at[slot]
            remote(landed, landed, y_send.at[0], y_recv.at[slot[0], e - (1 if up else 5), piece], partner).wait_recv()
            total = total + land_ref[slot].astype(F32)
        chain_ref[e, piece] = total.astype(BF16)
        if e == (1 if up else NY - 1):
            go(to_owner(piece, 1 if up else 2, e, 1 if up else -1))
            return
        there = (0 if up else 1), (e - 1 if up else e + 1), piece
        to = {"fsdp": lax.rem(y + (1 if up else NY - 1), NY) * 2 + core, "ctx": k}
        go(remote(chain_ref.at[e, piece], land_ref.at[there], y_send.at[0], y_recv.at[there[0], there[1] - (1 if up else 5), piece], to))

    def stage(n):
        for i in range(2):
            chain(True, 4 - n, i)
            chain(False, 4 + n, 2 + i)
        if n < 3:
            for i in range(2):
                chain(True, 3 - n, 2 + i)
                chain(False, 5 + n, i)

    def stays(piece):
        return jnp.logical_and(owner == core, x % 2 == piece // 2)

    def own_term():
        for piece in range(4):
            chain_ref[0, piece] = term(0, piece).astype(BF16)

            @pl.when(jnp.logical_not(stays(piece)))
            def _(piece=piece):
                to_owner(piece, 0, 0, 0).start()

    def collect():
        for half in range(2):
            local = jnp.logical_and(owner == core, x % 2 == half)
            for part in range(2):
                span, columns = rows_of(part), pl.ds(half * C, C)

                @pl.when(local)
                def _(half=half, part=part, span=span):
                    final_ref[0, half, span, :] = chain_ref[0, 2 * half + part]

                for kind in range(3):
                    landed = final_ref.at[kind, half, span, :]
                    arrived = remote(landed, landed, y_send.at[0], final_recv.at[kind, half, part], partner)
                    if kind:
                        arrived.wait_recv()
                    else:
                        pl.when(jnp.logical_not(local))(arrived.wait_recv)
                total = final_ref[0, half, span, :].astype(F32) + final_ref[1, half, span, :].astype(F32)
                out_ref[span, columns] = (total + final_ref[2, half, span, :].astype(F32)).astype(BF16)

    for load in loads[:4]:
        load.wait()
    send_tail()
    for piece in range(PIECES):
        go(w_copy(1, True, piece))
        go(w_copy(1, False, PIECES - 1 - piece))
    go_out(0)
    clear()
    for i in range(4):
        tables(4 * i)
    go_out(1)
    own_rows()
    mix()
    forward_send()
    w_relay(1)
    go_first(0)
    shift_copies(0, 0)
    shift_copies(0, 4)
    local_taps(0, 0, 8, conv_ref, True)
    go_first(1)
    combine_x(0)
    w_relay(2)
    local_taps(0, 8, 16, conv_ref, False)
    go_near(0)
    w_relay(3, range(PIECES // 2))
    go_near(1)
    w_relay(3, range(PIECES // 2, PIECES))
    gate()
    w_relay(4)
    loads[4].wait()
    pltpu.make_async_copy(go_all.at[:, 0], go_all.at[:, 0], own_sem.at[5]).wait()
    part_ref[...] = jnp.zeros_like(part_ref)
    for dy in (0, -1, 1):
        transpose_project(dy)
    go_far()
    transpose_project(2)
    give()
    gated_arrived()
    for e in PROJECT_ORDER[:5]:
        project(e)
    stage(0)
    for e in PROJECT_ORDER[5:]:
        project(e)
    sum_gated()
    acc_ref[...] = gg_ref[...] * mix_ref[0]
    end_state(near, acc_ref, 1)
    send_x(1)
    stage(1)
    own_term()
    combine_x(1)
    gg_ref[...] = gg_ref[...] * conv_ref[...]
    shift_copies(1, 0)
    shift_copies(1, 4)
    local_taps(1, 0, 8, acc_ref, True)
    stage(2)
    local_taps(1, 8, 16, acc_ref, False)
    combine_z(1)
    boundary(far, acc_ref)
    for j in range(3):
        value = gg_ref[...] if j == 0 else acc_ref[...] * mix_ref[3 - j]
        mix_ref[3 + j] = value
        tail_ref[1, 2 * j : 2 * j + 2, :] = value[0:2]
    go(halo_copy(1, previous))
    stage(3)
    halo_copy(1, previous).wait_recv()
    inner = k < NZ * NX - 1
    for j in range(3):
        now = mix_ref[3 + j]
        one = jnp.where(inner, halo_ref[1, 2 * j : 2 * j + 1, :], 0.0)
        two = jnp.where(inner, halo_ref[1, 2 * j + 1 : 2 * j + 2, :], 0.0)
        ahead1 = jnp.where(rows == T - 1, one, pltpu.roll(now, T - 1, 0))
        ahead2 = jnp.where(rows == T - 1, two, jnp.where(rows == T - 2, one, pltpu.roll(now, T - 2, 0)))
        gf_ref[j] = (
            taps_ref[0, j : j + 1, :] * now + taps_ref[1, j : j + 1, :] * ahead1 + taps_ref[2, j : j + 1, :] * ahead2
        ).astype(BF16)
    collect()
    rows_sent = go_all.at[pl.ds(0, 6), pl.ds(1, NX - 1), my_half, :]
    for sent, semaphore in [
        (w_all.at[pl.ds(0, NZ - 1)], w_send.at[0]),
        (go_all.at[pl.ds(0, 6), 1, my_half, :], go_send.at[0]),
        (rows_sent, ring_send.at[0]),
        (go_all.at[:, pl.ds(1, NX - 1), my_half, :], share_send.at[0]),
        (tail_ref, halo_send.at[0]),
        (x_states.at[0, pl.ds(0, NX - 1)], x_send.at[0]),
        (x_states.at[1, pl.ds(0, NX - 1)], x_send.at[1]),
        (z_states.at[0, pl.ds(0, NZ - 1)], z_send.at[0]),
        (gated_ref.at[pl.ds(0, NX - 1)], gated_send.at[0]),
        (give_ref.at[pl.ds(1, NX - 1)], give_send.at[0]),
        (pair_ref, pair_send.at[0]),
        (chain_ref.at[pl.ds(1, NY - 1)], y_send.at[0]),
    ]:
        remote(sent, sent, semaphore, own_sem.at[0], partner).wait_send()
    for piece in range(4):

        @pl.when(jnp.logical_not(stays(piece)))
        def _(piece=piece):
            to_owner(piece, 0, 0, 0).wait_send()


def per_device(featurized, short_taps, residues, decay_rates, w_out, grad_out):
    operands = (featurized.transpose(1, 0, 2), short_taps, decay_rates.T, residues.T, w_out, grad_out)
    hbm = pl.BlockSpec(memory_space=pl.ANY)
    dma, V = pltpu.SemaphoreType.DMA, pltpu.VMEM
    block, gf = pl.pallas_call(
        kernel,
        out_shape=(jax.ShapeDtypeStruct((T, 2 * C), BF16), jax.ShapeDtypeStruct((3, T, C), BF16)),
        in_specs=[hbm] * 6,
        out_specs=(pl.BlockSpec(memory_space=pltpu.VMEM),) * 2,
        scratch_shapes=[
            V((3, T, C), BF16),
            V((3, 3, C), F32),
            V((MODES, C), F32),
            V((MODES, C), F32),
            V((NZ, C, C), BF16),
            V((NZ, NX, T, C), BF16),
            V((MODES, T, C), F32),
            V((MODES, T, C), F32),
            V((T, C), F32),
            V((8, 2 * T, C), F32),
            V((6, T, C), F32),
            V((T, C), F32),
            V((T, C), F32),
            V((T, C), F32),
            V((2, 8, C), F32),
            V((2, 8, C), F32),
            V((8, MODES, C), F32),
            V((2, NX, MODES, C), F32),
            V((2, NZ, MODES, C), F32),
            V((MODES, C), F32),
            V((NX, T, C), BF16),
            V((NX, T, C), F32),
            V((NX, T, C), BF16),
            V((NX, T, C), BF16),
            V((NY, NX, T, C), BF16),
            V((NY, 2, T, C), BF16),
            V((NY, 4, H, C), BF16),
            V((2, NY, 4, H, C), BF16),
            V((3, 2, T, C), BF16),
            dma((6,)), dma((1,)), dma((2, 4, PIECES)), dma((1,)), dma((2,)),
            dma((2,)), dma((2, NX)), dma((1,)), dma((NZ,)),
            dma((1,)), dma((2,)), dma((1,)), dma((2, 3)), dma((1,)), dma((4, 2)),
            dma((1,)), dma((NX,)), dma((1,)), dma((1,)), dma((1,)), dma((NY,)),
            dma((1,)), dma((4,)), dma((2, 3, 4)), dma((3, 2, 2)),
        ],
        compiler_params=pltpu.CompilerParams(
            collective_id=0, has_side_effects=True, vmem_limit_bytes=48000000
        ),
    )(*(pltpu.with_memory_space_constraint(v, pltpu.HBM) for v in operands))
    return (block, gf.transpose(1, 0, 2))


def solution(mesh):
    placed = (
        P("ctx", None, "fsdp"),
        P(None, None, "fsdp"),
        P("fsdp", None),
        P("fsdp", None),
        P("fsdp", "ctx"),
        P("ctx", None),
    )
    return jax.shard_map(
        per_device,
        mesh=mesh,
        in_specs=placed,
        out_specs=(P("ctx", "fsdp"), P("ctx", None, "fsdp")),
        check_vma=False,
    )
```

```python
import jax
import jax.numpy as jnp
from jax import lax
from jax.experimental import pallas as pl
from jax.experimental.pallas import tpu as pltpu
from jax.sharding import PartitionSpec as P

T = 128
C = 256
MODES = 16
NZ, NX, NY = 8, 4, 8
F32 = jnp.float32
BF16 = jnp.bfloat16
MESH = pl.DeviceIdType.MESH

H = T // 2
PIECES = 4
CHAIN_UP = {0: (4, 3, 2, 1), 1: (4, 3, 2, 1), 2: (3, 2, 1), 3: (3, 2, 1)}
CHAIN_DOWN = {0: (5, 6, 7), 1: (5, 6, 7), 2: (4, 5, 6, 7), 3: (4, 5, 6, 7)}
PROJECT_ORDER = (4, 3, 5, 2, 6, 1, 7, 0)


def kernel(
    feats_in, taps_in, a_in, res_in, w_ref, go_ref, out_ref, gf_ref,
    feats_ref, taps_ref, a_ref, res_ref, w_all, go_all, near, far, h_ref, pad_ref, mix_ref, conv_ref, gg_ref,
    acc_ref, tail_ref, halo_ref, state_ref, x_states, z_states, weight_ref, gated_ref, part_ref, give_ref, take_ref,
    mine_ref, pair_ref, chain_ref, land_ref, final_ref,
    own_sem, w_send, w_recv, halo_send, halo_recv, x_send, x_recv, z_send, z_recv,
    go_send, go_recv, ring_send, ring_recv, share_send, share_recv,
    gated_send, gated_recv, give_send, give_recv, pair_send, pair_recv, y_send, own_send, y_recv, final_recv,
):
    f, k = lax.axis_index("fsdp"), lax.axis_index("ctx")
    y, core = f // 2, f % 2
    z, x = k // NX, k % NX

    def at(dz, dx):
        return lax.rem(z + dz + NZ, NZ) * NX + lax.rem(x + dx + NX, NX)

    def ctx(index):
        return {"fsdp": f, "ctx": index}

    def remote(src, dst, send, recv, device):
        return pltpu.make_async_remote_copy(
            src_ref=src, dst_ref=dst, send_sem=send, recv_sem=recv, device_id=device, device_id_type=MESH
        )

    following, previous = lax.rem(k + 1, NZ * NX), lax.rem(k + NZ * NX - 1, NZ * NX)
    partner = {"fsdp": y * 2 + 1 - core, "ctx": k}
    my_half = pl.ds(core * H, H)

    loads = [
        pltpu.make_async_copy(src, dst, own_sem.at[i])
        for i, (src, dst) in enumerate(
            [(feats_in, feats_ref), (a_in, a_ref), (res_in, res_ref), (taps_in, taps_ref), (w_ref, w_all.at[z])]
        )
    ]
    for load in loads:
        load.start()

    barrier = pltpu.get_barrier_semaphore()
    greeted = [{"fsdp": y * 2 + 1 - core, "ctx": at(0, d)} for d in range(NX)] + [ctx(at(0, d)) for d in range(1, NX)]
    greeted += [ctx(at(d, 0)) for d in range(1, NZ)] + [ctx(following), ctx(previous)]
    greeted += [{"fsdp": lax.rem(y + d, NY) * 2 + core, "ctx": k} for d in (1, NY - 1)]
    greeted += [
        {"fsdp": lax.rem(y + d, NY) * 2 + x // 2, "ctx": z * NX + core * 2 + i} for d in (1, NY - 1) for i in range(2)
    ]
    for device in greeted:
        pl.semaphore_signal(barrier, inc=1, device_id=device, device_id_type=MESH)
    pl.semaphore_wait(barrier, len(greeted))

    def go(copy):
        copy.start()

    def w_copy(distance, up, piece):
        block = lax.rem(z + (1 - distance if up else distance - 1) + NZ, NZ)
        span = pl.ds(piece * (C // PIECES), C // PIECES)
        src = w_ref.at[span, :] if distance == 1 else w_all.at[block, span, :]
        slot = (0 if up else 1), distance - 1, piece
        return remote(src, w_all.at[block, span, :], w_send.at[0], w_recv.at[slot], ctx(at(1 if up else -1, 0)))

    def farthest(up, piece):
        return (piece < PIECES // 2) == up

    def w_relay(distance, pieces=range(PIECES)):
        for i in pieces:
            for up in (True, False):
                piece = i if up else PIECES - 1 - i
                if distance == NZ // 2 and not farthest(up, piece):
                    continue
                span = pl.ds(piece * (C // PIECES), C // PIECES)
                block = w_all.at[lax.rem(z + (-distance if up else distance) + NZ, NZ), span, :]
                slot = (0 if up else 1), distance - 1, piece
                remote(block, block, w_send.at[0], w_recv.at[slot], partner).wait_recv()
                if distance + 1 < NZ // 2 or (distance + 1 == NZ // 2 and farthest(up, piece)):
                    go(w_copy(distance + 1, up, piece))

    def strip_row(dy, i):
        return lax.rem(y + dy + NY, NY // 2) + i * (NY // 2)

    def go_out(i):
        row = strip_row(0, i)
        for d in (2, 1, 3):
            strip = go_ref.at[my_half, pl.ds(pl.multiple_of((row * NX + lax.rem(x + d, NX)) * C, C), C)]
            go(remote(strip, go_all.at[row, d, my_half, :], go_send.at[0], go_recv.at[i], ctx(at(0, d))))

    def own_rows():
        for row in range(NZ):
            columns = pl.ds(pl.multiple_of((row * NX + x) * C, C), C)
            pltpu.make_async_copy(go_ref.at[:, columns], go_all.at[row, 0], own_sem.at[5]).start()

    def strips(dy, i, half):
        return go_all.at[strip_row(dy, i), pl.ds(1, NX - 1), pl.ds(half * H, H), :]

    def go_copy(dy, up, i):
        region = strips(dy, i, core)
        slot = (0 if up else 1), (i if dy == 0 else 2)
        to = {"fsdp": lax.rem(y + (1 if up else NY - 1), NY) * 2 + core, "ctx": k}
        return remote(region, region, ring_send.at[0], ring_recv.at[slot], to)

    def share_copy(dy, i, half):
        region = strips(dy, i, half)
        return remote(region, region, share_send.at[0], share_recv.at[dy + 1, i], partner)

    def go_first(i):
        landed = strips(0, i, core)
        remote(landed, landed, go_send.at[0], go_recv.at[i], partner).wait_recv()
        go(go_copy(0, True, i))
        go(go_copy(0, False, i))
        go(share_copy(0, i, core))

    def go_near(i):
        for up in (True, False):
            dy = -1 if up else 1
            region = strips(dy, i, core)
            slot = (0 if up else 1), i
            remote(region, region, ring_send.at[0], ring_recv.at[slot], partner).wait_recv()
            if i == (0 if up else 1):
                go(go_copy(dy, up, i))
            go(share_copy(dy, i, core))

    def go_far():
        for up in (True, False):
            i = 0 if up else 1
            region = strips(2, i, core)
            slot = (0 if up else 1), 2
            remote(region, region, ring_send.at[0], ring_recv.at[slot], partner).wait_recv()
            go(share_copy(2, i, core))

    def from_x(dx):
        return lax.rem(x + dx + NX, NX)

    rows = lax.broadcasted_iota(jnp.int32, (T, 1), 0)
    steps = rows.astype(F32)

    def halo_copy(which, device):
        return remote(
            tail_ref.at[which], halo_ref.at[which], halo_send.at[0], halo_recv.at[which], ctx(device)
        )

    def send_tail():
        for j in range(3):
            last = feats_ref[j, T - 16 :, :].astype(F32)
            tail_ref[0, 2 * j : 2 * j + 2, :] = last[14:16]
        copy = halo_copy(0, following)
        copy.start()

    def tables(low):
        def body(n, c):
            a = a_ref[pl.ds(n, 1), :]
            scale = res_ref[pl.ds(n, 1), :] * jnp.sqrt(a)
            weight_ref[pl.ds(n, 1), :] = scale
            e = jnp.exp(-a * steps)
            near[n] = e
            far[n] = jnp.exp(-a * (T - 1 - steps))
            h_ref[...] += scale * e
            return c

        lax.fori_loop(low, low + 4, body, 0)

    def clear():
        h_ref[...] = jnp.zeros_like(h_ref)

    def end_state(table, signal_ref, which):
        def body(n, c):
            state_ref[which, pl.ds(n, 1), :] = jnp.sum(table[n] * signal_ref[...], axis=0, keepdims=True)
            return c

        lax.fori_loop(0, MODES, body, 0)

    def send_x(which):
        for d in range(1, NX):
            copy = remote(
                state_ref.at[which], x_states.at[which, x], x_send.at[which], x_recv.at[which, x], ctx(at(0, d))
            )
            copy.start()

    def mix():
        halo_copy(0, following).wait_recv()
        for j in range(3):
            now = feats_ref[j].astype(F32)
            one = jnp.where(k > 0, halo_ref[0, 2 * j + 1 : 2 * j + 2, :], 0.0)
            two = jnp.where(k > 0, halo_ref[0, 2 * j : 2 * j + 1, :], 0.0)
            back1 = jnp.where(rows == 0, one, pltpu.roll(now, 1, 0))
            back2 = jnp.where(rows == 0, two, jnp.where(rows == 1, one, pltpu.roll(now, 2, 0)))
            mix_ref[j] = (
                taps_ref[0, j : j + 1, :] * now + taps_ref[1, j : j + 1, :] * back1 + taps_ref[2, j : j + 1, :] * back2
            )
        acc_ref[...] = mix_ref[1] * mix_ref[2]

    def forward_send():
        end_state(far, acc_ref, 0)
        send_x(0)

    def shift_copies(which, low):
        value = acc_ref[...]
        for r in range(low, low + 4):
            if which == 0:
                pad_ref[r, :T, :] = jnp.zeros_like(value)
                pad_ref[r, T:, :] = jnp.where(rows >= r, pltpu.roll(value, r, 0), 0.0) if r else value
            else:
                pad_ref[r, T:, :] = jnp.zeros_like(value)
                pad_ref[r, :T, :] = jnp.where(rows < T - r, pltpu.roll(value, T - r, 0), 0.0) if r else value

    def local_taps(which, low, high, dst, begin):
        def body(q, total):
            for r in range(8):
                start = pl.multiple_of((T - 8 * q) if which == 0 else 8 * q, 8)
                total = total + h_ref[pl.ds(8 * q + r, 1), :] * pad_ref[r, pl.ds(start, T), :]
            return total

        first = jnp.zeros((T, C), F32) if begin else dst[...]
        dst[...] = lax.fori_loop(low, high, body, first)

    def combine_x(which):
        x_states[which, x] = state_ref[which]
        for d in range(1, NX):
            other = lax.rem(x + d, NX)
            remote(
                state_ref.at[which], x_states.at[which, other], x_send.at[which], x_recv.at[which, other], ctx(k)
            ).wait_recv()
        a = a_ref[...]
        entering, total = jnp.zeros_like(a), jnp.zeros_like(a)
        for j in range(NX):
            gap = (x - 1 - j) if which == 0 else (j - x - 1)
            reach = (NX - 1 - j) if which == 0 else j
            decay = jnp.exp(-a * (T * jnp.maximum(gap, 0)).astype(F32))
            state = x_states[which, j]
            entering = entering + jnp.where(gap >= 0, decay * state, 0.0)
            total = total + jnp.exp(-a * float(T * reach)) * state
        state_ref[2 + which] = entering
        state_ref[4 + which] = total
        for d in range(1, NZ):
            to = lax.rem(z + d, NZ)

            @pl.when((to > z) if which == 0 else (to < z))
            def _(d=d):
                z_copy(which, d).start()

    def z_copy(which, d):
        return remote(
            state_ref.at[4 + which], z_states.at[which, z], z_send.at[0], z_recv.at[z], ctx(at(d, 0))
        )

    def combine_z(which):
        a = a_ref[...]
        state_ref[6] = jnp.zeros_like(a)
        for d in range(1, NZ):
            other = lax.rem(z + d, NZ)

            @pl.when((other < z) if which == 0 else (other > z))
            def _(d=d, other=other):
                remote(
                    state_ref.at[4 + which],
                    z_states.at[which, other],
                    z_send.at[0],
                    z_recv.at[other],
                    ctx(at(d, 0)),
                ).wait_recv()
                gap = (z - 1 - other) if which == 0 else (other - z - 1)
                state_ref[6] += jnp.exp(-a * (NX * T * gap).astype(F32)) * z_states[which, other]

        inside = x if which == 0 else NX - 1 - x
        entering = state_ref[2 + which] + jnp.exp(-a * (T * inside).astype(F32)) * state_ref[6]
        state_ref[7] = weight_ref[...] * jnp.exp(-a) * entering

    def boundary(table, dst):
        def body(n, total):
            return total + table[n] * state_ref[7, pl.ds(n, 1), :]

        dst[...] = lax.fori_loop(0, MODES, body, dst[...])

    def gate():
        combine_z(0)
        boundary(near, conv_ref)
        gated_ref[x] = (mix_ref[0] * conv_ref[...]).astype(BF16)
        for d in range(1, NX):
            go(remote(gated_ref.at[x], gated_ref.at[x], gated_send.at[0], gated_recv.at[d], ctx(at(0, d))))

    def transpose_project(dy):
        for i in range(2):
            share_copy(dy, i, 1 - core).wait_recv()

        def body(i, c):
            row = strip_row(dy, i)
            part = lax.dot_general(
                go_all[row].reshape(NX * T, C), w_all[row], (((1,), (1,)), ((), ())), preferred_element_type=F32
            )
            part_ref[...] += part.reshape(NX, T, C)
            return c

        lax.fori_loop(0, 2, body, 0)

    def give():
        for d in range(1, NX):
            give_ref[d] = part_ref[d].astype(BF16)
            go(remote(give_ref.at[d], take_ref.at[d], give_send.at[0], give_recv.at[0], ctx(at(0, -d))))

    def sum_gated():
        gg_ref[...] = part_ref[0]
        taken = take_ref.at[pl.ds(1, NX - 1)]
        remote(taken, taken, give_send.at[0], give_recv.at[0], partner).wait_recv()
        for d in range(1, NX):
            gg_ref[...] += take_ref[d].astype(F32)

    def gated_arrived():
        for d in range(1, NX):
            source = from_x(-d)
            remote(
                gated_ref.at[source], gated_ref.at[source], gated_send.at[0], gated_recv.at[d], partner
            ).wait_recv()

    def target(e):
        return lax.rem(y + e, NY)

    def pair_copy(e):
        row = target(e)
        return remote(
            mine_ref.at[row, pl.ds((1 - core) * 2, 2)], pair_ref.at[row], pair_send.at[0], pair_recv.at[e], partner
        )

    def project(e):
        row = target(e)
        part = jnp.dot(gated_ref[...].reshape(NX * T, C), w_all[row], preferred_element_type=F32)
        mine_ref[row] = part.astype(BF16).reshape(NX, T, C)
        go(pair_copy(e))

    paired = set()

    def rows_of(piece):
        return pl.ds(piece % 2 * H, H)

    def term(e, piece):
        if e not in paired:
            pair_copy(e).wait_recv()
            paired.add(e)
        row, span = target(e), rows_of(piece)
        mine = mine_ref[row, core * 2 + piece // 2, span, :]
        return mine.astype(F32) + pair_ref[row, piece // 2, span, :].astype(F32)

    owner = x // 2

    def owner_of(piece, dy):
        return {"fsdp": lax.rem(y + dy + NY, NY) * 2 + owner, "ctx": z * NX + core * 2 + piece // 2}

    def to_owner(piece, kind, e, dy):
        there = kind, x % 2, rows_of(piece), slice(None)
        return remote(
            chain_ref.at[e, piece],
            final_ref.at[there],
            y_send.at[0] if kind else own_send.at[piece],
            final_recv.at[kind, x % 2, piece % 2],
            owner_of(piece, dy),
        )

    def chain(up, e, piece):
        total = term(e, piece)
        if e != (CHAIN_UP if up else CHAIN_DOWN)[piece][0]:
            slot = (0 if up else 1), e, piece
            landed = land_ref.at[slot]
            remote(landed, landed, y_send.at[0], y_recv.at[slot[0], e - (1 if up else 5), piece], partner).wait_recv()
            total = total + land_ref[slot].astype(F32)
        chain_ref[e, piece] = total.astype(BF16)
        if e == (1 if up else NY - 1):
            go(to_owner(piece, 1 if up else 2, e, 1 if up else -1))
            return
        there = (0 if up else 1), (e - 1 if up else e + 1), piece
        to = {"fsdp": lax.rem(y + (1 if up else NY - 1), NY) * 2 + core, "ctx": k}
        go(remote(chain_ref.at[e, piece], land_ref.at[there], y_send.at[0], y_recv.at[there[0], there[1] - (1 if up else 5), piece], to))

    def stage(n):
        for i in range(2):
            chain(True, 4 - n, i)
            chain(False, 4 + n, 2 + i)
        if n < 3:
            for i in range(2):
                chain(True, 3 - n, 2 + i)
                chain(False, 5 + n, i)

    def stays(piece):
        return jnp.logical_and(owner == core, x % 2 == piece // 2)

    def own_term():
        for piece in range(4):
            chain_ref[0, piece] = term(0, piece).astype(BF16)

            @pl.when(jnp.logical_not(stays(piece)))
            def _(piece=piece):
                to_owner(piece, 0, 0, 0).start()

    def collect():
        for half in range(2):
            local = jnp.logical_and(owner == core, x % 2 == half)
            for part in range(2):
                span, columns = rows_of(part), pl.ds(half * C, C)

                @pl.when(local)
                def _(half=half, part=part, span=span):
                    final_ref[0, half, span, :] = chain_ref[0, 2 * half + part]

                for kind in range(3):
                    landed = final_ref.at[kind, half, span, :]
                    arrived = remote(landed, landed, y_send.at[0], final_recv.at[kind, half, part], partner)
                    if kind:
                        arrived.wait_recv()
                    else:
                        pl.when(jnp.logical_not(local))(arrived.wait_recv)
                total = final_ref[0, half, span, :].astype(F32) + final_ref[1, half, span, :].astype(F32)
                out_ref[span, columns] = (total + final_ref[2, half, span, :].astype(F32)).astype(BF16)

    for load in loads[:4]:
        load.wait()
    send_tail()
    for piece in range(PIECES):
        go(w_copy(1, True, piece))
        go(w_copy(1, False, PIECES - 1 - piece))
    go_out(0)
    clear()
    for i in range(4):
        tables(4 * i)
    go_out(1)
    own_rows()
    mix()
    forward_send()
    w_relay(1)
    go_first(0)
    shift_copies(0, 0)
    shift_copies(0, 4)
    local_taps(0, 0, 8, conv_ref, True)
    go_first(1)
    combine_x(0)
    w_relay(2)
    local_taps(0, 8, 16, conv_ref, False)
    go_near(0)
    w_relay(3, range(PIECES // 2))
    go_near(1)
    w_relay(3, range(PIECES // 2, PIECES))
    gate()
    w_relay(4)
    loads[4].wait()
    pltpu.make_async_copy(go_all.at[:, 0], go_all.at[:, 0], own_sem.at[5]).wait()
    part_ref[...] = jnp.zeros_like(part_ref)
    for dy in (0, -1, 1):
        transpose_project(dy)
    go_far()
    transpose_project(2)
    give()
    gated_arrived()
    for e in PROJECT_ORDER[:5]:
        project(e)
    stage(0)
    for e in PROJECT_ORDER[5:]:
        project(e)
    sum_gated()
    acc_ref[...] = gg_ref[...] * mix_ref[0]
    end_state(near, acc_ref, 1)
    send_x(1)
    gg_ref[...] = gg_ref[...] * conv_ref[...]
    shift_copies(1, 0)
    shift_copies(1, 4)
    local_taps(1, 0, 8, acc_ref, True)
    stage(1)
    own_term()
    combine_x(1)
    stage(2)
    local_taps(1, 8, 16, acc_ref, False)
    combine_z(1)
    boundary(far, acc_ref)
    for j in range(3):
        value = gg_ref[...] if j == 0 else acc_ref[...] * mix_ref[3 - j]
        mix_ref[3 + j] = value
        tail_ref[1, 2 * j : 2 * j + 2, :] = value[0:2]
    go(halo_copy(1, previous))
    stage(3)
    halo_copy(1, previous).wait_recv()
    inner = k < NZ * NX - 1
    for j in range(3):
        now = mix_ref[3 + j]
        one = jnp.where(inner, halo_ref[1, 2 * j : 2 * j + 1, :], 0.0)
        two = jnp.where(inner, halo_ref[1, 2 * j + 1 : 2 * j + 2, :], 0.0)
        ahead1 = jnp.where(rows == T - 1, one, pltpu.roll(now, T - 1, 0))
        ahead2 = jnp.where(rows == T - 1, two, jnp.where(rows == T - 2, one, pltpu.roll(now, T - 2, 0)))
        gf_ref[j] = (
            taps_ref[0, j : j + 1, :] * now + taps_ref[1, j : j + 1, :] * ahead1 + taps_ref[2, j : j + 1, :] * ahead2
        ).astype(BF16)
    collect()
    rows_sent = go_all.at[pl.ds(0, 6), pl.ds(1, NX - 1), my_half, :]
    for sent, semaphore in [
        (w_all.at[pl.ds(0, NZ - 1)], w_send.at[0]),
        (go_all.at[pl.ds(0, 6), 1, my_half, :], go_send.at[0]),
        (rows_sent, ring_send.at[0]),
        (go_all.at[:, pl.ds(1, NX - 1), my_half, :], share_send.at[0]),
        (tail_ref, halo_send.at[0]),
        (x_states.at[0, pl.ds(0, NX - 1)], x_send.at[0]),
        (x_states.at[1, pl.ds(0, NX - 1)], x_send.at[1]),
        (z_states.at[0, pl.ds(0, NZ - 1)], z_send.at[0]),
        (gated_ref.at[pl.ds(0, NX - 1)], gated_send.at[0]),
        (give_ref.at[pl.ds(1, NX - 1)], give_send.at[0]),
        (pair_ref, pair_send.at[0]),
        (chain_ref.at[pl.ds(1, NY - 1)], y_send.at[0]),
    ]:
        remote(sent, sent, semaphore, own_sem.at[0], partner).wait_send()
    for piece in range(4):

        @pl.when(jnp.logical_not(stays(piece)))
        def _(piece=piece):
            to_owner(piece, 0, 0, 0).wait_send()


def per_device(featurized, short_taps, residues, decay_rates, w_out, grad_out):
    operands = (featurized.transpose(1, 0, 2), short_taps, decay_rates.T, residues.T, w_out, grad_out)
    hbm = pl.BlockSpec(memory_space=pl.ANY)
    dma, V = pltpu.SemaphoreType.DMA, pltpu.VMEM
    block, gf = pl.pallas_call(
        kernel,
        out_shape=(jax.ShapeDtypeStruct((T, 2 * C), BF16), jax.ShapeDtypeStruct((3, T, C), BF16)),
        in_specs=[hbm] * 6,
        out_specs=(pl.BlockSpec(memory_space=pltpu.VMEM),) * 2,
        scratch_shapes=[
            V((3, T, C), BF16),
            V((3, 3, C), F32),
            V((MODES, C), F32),
            V((MODES, C), F32),
            V((NZ, C, C), BF16),
            V((NZ, NX, T, C), BF16),
            V((MODES, T, C), F32),
            V((MODES, T, C), F32),
            V((T, C), F32),
            V((8, 2 * T, C), F32),
            V((6, T, C), F32),
            V((T, C), F32),
            V((T, C), F32),
            V((T, C), F32),
            V((2, 8, C), F32),
            V((2, 8, C), F32),
            V((8, MODES, C), F32),
            V((2, NX, MODES, C), F32),
            V((2, NZ, MODES, C), F32),
            V((MODES, C), F32),
            V((NX, T, C), BF16),
            V((NX, T, C), F32),
            V((NX, T, C), BF16),
            V((NX, T, C), BF16),
            V((NY, NX, T, C), BF16),
            V((NY, 2, T, C), BF16),
            V((NY, 4, H, C), BF16),
            V((2, NY, 4, H, C), BF16),
            V((3, 2, T, C), BF16),
            dma((6,)), dma((1,)), dma((2, 4, PIECES)), dma((1,)), dma((2,)),
            dma((2,)), dma((2, NX)), dma((1,)), dma((NZ,)),
            dma((1,)), dma((2,)), dma((1,)), dma((2, 3)), dma((1,)), dma((4, 2)),
            dma((1,)), dma((NX,)), dma((1,)), dma((1,)), dma((1,)), dma((NY,)),
            dma((1,)), dma((4,)), dma((2, 3, 4)), dma((3, 2, 2)),
        ],
        compiler_params=pltpu.CompilerParams(
            collective_id=0, has_side_effects=True, vmem_limit_bytes=48000000
        ),
    )(*(pltpu.with_memory_space_constraint(v, pltpu.HBM) for v in operands))
    return (block, gf.transpose(1, 0, 2))


def solution(mesh):
    placed = (
        P("ctx", None, "fsdp"),
        P(None, None, "fsdp"),
        P("fsdp", None),
        P("fsdp", None),
        P("fsdp", "ctx"),
        P("ctx", None),
    )
    return jax.shard_map(
        per_device,
        mesh=mesh,
        in_specs=placed,
        out_specs=(P("ctx", "fsdp"), P("ctx", None, "fsdp")),
        check_vma=False,
    )
```
